32 devices in a mesh: band: 4 (over y, core), shard: 8 (over z, x).
Axes of the slice: x: 2, y: 2, z: 4, core: 2. Of those that a mesh axis runs over, the one named last changes fastest.
Arguments:
- block_input: bfloat16 [8, 56, 14, 512], P('shard', 'band'), may hold values from -6 to 6
- output_grad: bfloat16 [8, 56, 14, 512], P('shard', 'band'), may hold values from -6 to 6
- region_ids: int32 [56, 14], P('band'), may hold values from 0 to 8, as said below
- relative_index: int32 [49, 49], replicated, may hold values from 0 to 168
- attention_weight: float32 [512, 2048], P('shard'), may hold values from -0.375 to 0.375
- expand_weight: float32 [512, 2048], P('shard'), may hold values from -0.25 to 0.25
- reduce_weight: float32 [2048, 512], P('shard'), may hold values from -0.125 to 0.125
- vectors: float32 [12, 512], P(None, 'shard'), may hold values from -0.5 to 0.5
- bias_table: float32 [169, 16], replicated, may hold values from -0.6 to 250
- attention_mean: float32 [512, 2048], P('shard'), may hold values from -0.3 to 0.3
- attention_square: float32 [512, 2048], P('shard'), may hold values from 0.0001 to 0.001
- expand_mean: float32 [512, 2048], P('shard'), may hold values from -0.3 to 0.3
- expand_square: float32 [512, 2048], P('shard'), may hold values from 0.0001 to 0.001
- reduce_mean: float32 [2048, 512], P('shard'), may hold values from -0.3 to 0.3
- reduce_square: float32 [2048, 512], P('shard'), may hold values from 0.0001 to 0.001
- vectors_mean: float32 [12, 512], P(None, 'shard'), may hold values from -0.3 to 0.3
- vectors_square: float32 [12, 512], P(None, 'shard'), may hold values from 0.0001 to 0.001
- table_mean: float32 [169, 16], replicated, may hold values from -0.3 to 0.3
- table_square: float32 [169, 16], replicated, may hold values from 0.0001 to 0.001
Outputs:
- block_output: float32 [8, 56, 14, 512], P('shard', 'band')
- input_grad: float32 [8, 56, 14, 512], P('shard', 'band')
- attention_grad: float32 [512, 2048], P('shard')
- expand_grad: float32 [512, 2048], P('shard')
- reduce_grad: float32 [2048, 512], P('shard')
- vectors_grad: float32 [12, 512], P(None, 'shard')
- table_grad: float32 [169, 16], replicated
- new_attention: float32 [512, 2048], P('shard')
- new_expand: float32 [512, 2048], P('shard')
- new_reduce: float32 [2048, 512], P('shard')
- new_vectors: float32 [12, 512], P(None, 'shard')
- new_table: float32 [169, 16], replicated
- new_attention_mean: float32 [512, 2048], P('shard')
- new_attention_square: float32 [512, 2048], P('shard')
- new_expand_mean: float32 [512, 2048], P('shard')
- new_expand_square: float32 [512, 2048], P('shard')
- new_reduce_mean: float32 [2048, 512], P('shard')
- new_reduce_square: float32 [2048, 512], P('shard')
- new_vectors_mean: float32 [12, 512], P(None, 'shard')
- new_vectors_square: float32 [12, 512], P(None, 'shard')
- new_table_mean: float32 [169, 16], replicated
- new_table_square: float32 [169, 16], replicated
The draws below stay inside these ranges and needn't reach their ends.
Inputs may be any that keep to these rules, and one draw needn't show every extreme that they name: region_ids[r, c] = 3 * a(r) + b(c), where a(r) is 0 for r < 49, 1 from there up to a cut inside the last 7 rows, 2 from the cut on; b(c) likewise over the 14 columns with a cut of its own; each cut leaves 1 to 6 tokens in region 2.
All inputs are finite; a program needn't handle non-finite values.
Results may differ from the reference program's by a relative error of at most 0.023.
Values may be sent and summed in bfloat16 or wider, within the bound.
A program may use at most 128 MiB of HBM per device.

```python
import math
import jax
import jax.numpy as jnp
from jax import lax

C = 512
HEADS = 16
FFN = 2048
WIN = 7
SHIFT = 3
STEP = 5
H = 56
W = 14
IMAGES = 8
WTOK = 49
TABLE = 169


def draw_region_ids(key, part):
    row_key = jax.random.fold_in(key, 11)
    col_key = jax.random.fold_in(key, 13)
    row_cut = jax.random.randint(row_key, (), 1, WIN)
    col_cut = jax.random.randint(col_key, (), 1, WIN)
    rows = jnp.arange(H, dtype=jnp.int32)
    cols = jnp.arange(W, dtype=jnp.int32)
    row_region = (rows >= H - WIN).astype(jnp.int32) + (rows >= H - row_cut).astype(jnp.int32)
    col_region = (cols >= W - WIN).astype(jnp.int32) + (cols >= W - col_cut).astype(jnp.int32)
    return 3 * row_region[:, None] + col_region[None, :]


def draw_bias_table(key, part):
    base_key = jax.random.fold_in(key, 0)
    table_draw = jnp.clip(0.15 * jax.random.normal(base_key, (TABLE, HEADS), jnp.float32), -0.6, 0.6)
    return table_draw


def with_ends(values, own_key, smallest, high):
    extent = values.shape
    place = [jax.random.randint(jax.random.fold_in(own_key, axis), (), 0, extent[axis]) for axis in range(len(extent))]
    values = values.at[tuple(place)].set(smallest)
    longest = extent.index(max(extent))
    place[longest] = (place[longest] + 1) % extent[longest]
    return values.at[tuple(place)].set(high)


def with_spikes(array, rng, source, target, blocks, factor):
    owner, partner = [(jnp.arange(array.shape[dim]) // (array.shape[dim] // blocks)).reshape([-1 if axis == dim else 1 for axis in range(array.ndim)]) for dim in (source, target)]
    chosen = jax.random.permutation(rng, blocks)[partner]
    strong = (owner == chosen) | (owner == (partner + blocks // 2) % blocks)
    return jnp.where(strong, factor * array, array)


def level_of(stream_key, extent, pieces, low, high):
    def one(position, blocks):
        draws = jax.random.uniform(jax.random.fold_in(jax.random.fold_in(stream_key, 6), position), (blocks,), jnp.float32, low / len(pieces), high / len(pieces))
        return jnp.repeat(jnp.exp(draws), extent[position] // blocks).reshape((-1,) + (1,) * (len(extent) - position - 1))

    level = one(*pieces[0])
    for cut in pieces[1:]:
        level = level * one(*cut)
    return level


def bell_draw(stream_key, extent, deviation, most, cuts=(), held_as=jnp.bfloat16):
    result = jax.random.normal(stream_key, extent, jnp.float32) * deviation
    if len(cuts) > 0:
        result = level_of(stream_key, extent, cuts, -0.22, 0.18) * result
    return jnp.clip(result, min=-most, max=most).astype(held_as)


def heavy_noise(stream_key, dims, spread, bound, pieces, heavy, kind=jnp.bfloat16):
    array = spread * jax.random.normal(stream_key, dims, jnp.float32)
    if pieces:
        array = array * level_of(stream_key, dims, pieces, -0.22, 0.18)
    return jnp.clip(with_spikes(array, jax.random.fold_in(stream_key, 3), *heavy), -bound, bound).astype(kind)


def setup_inputs(seed: int = 0) -> dict:
    streams_of = jax.random.split(jax.random.key(seed), 20)
    return {
        "block_input": bell_draw(streams_of[0], (IMAGES, H, W, C), 1.0, 6.0, ((0, 8), (1, 4))),
        "output_grad": heavy_noise(streams_of[1], (IMAGES, H, W, C), 1.0, 6.0, ((0, 8), (1, 4)), (0, 3, 8, 2.0)),
        "region_ids": draw_region_ids(jax.random.fold_in(streams_of[19], 71), 0),
        "relative_index": with_ends(jax.random.randint(streams_of[3], (WTOK, WTOK), 0, TABLE), jax.random.fold_in(streams_of[3], 1), 0, TABLE - 1).astype(jnp.int32),
        "attention_weight": bell_draw(streams_of[4], (C, 4 * C), (C // 2) ** -0.5, 0.375, ((0, 8),), jnp.float32),
        "expand_weight": bell_draw(streams_of[5], (C, FFN), C ** -0.5, 0.25, ((0, 8),), jnp.float32),
        "reduce_weight": bell_draw(streams_of[6], (FFN, C), FFN ** -0.5, 0.125, ((0, 8),), jnp.float32),
        "vectors": bell_draw(streams_of[7], (12, C), 0.1, 0.5, ((1, 8),), jnp.float32),
        "bias_table": draw_bias_table(jax.random.fold_in(streams_of[19], 71), 0),
        "attention_mean": bell_draw(streams_of[9], (C, 4 * C), 0.05, 0.3, ((0, 8),), jnp.float32),
        "attention_square": jnp.clip(jnp.exp(math.log(0.001) - 2.3025852 * jax.random.uniform(streams_of[10], (C, 4 * C), jnp.float32) ** level_of(streams_of[10], (C, 4 * C), ((0, 8),), -0.2, 0.2)), 0.0001, 0.001),
        "expand_mean": bell_draw(streams_of[11], (C, FFN), 0.05, 0.3, ((0, 8),), jnp.float32),
        "expand_square": jnp.clip(jnp.exp(math.log(0.001) - 2.3025852 * jax.random.uniform(streams_of[12], (C, FFN), jnp.float32) ** level_of(streams_of[12], (C, FFN), ((0, 8),), -0.2, 0.2)), 0.0001, 0.001),
        "reduce_mean": bell_draw(streams_of[13], (FFN, C), 0.05, 0.3, ((0, 8),), jnp.float32),
        "reduce_square": jnp.clip(jnp.exp(math.log(0.001) - 2.3025852 * jax.random.uniform(streams_of[14], (FFN, C), jnp.float32) ** level_of(streams_of[14], (FFN, C), ((0, 8),), -0.2, 0.2)), 0.0001, 0.001),
        "vectors_mean": bell_draw(streams_of[15], (12, C), 0.05, 0.3, ((1, 8),), jnp.float32),
        "vectors_square": jnp.clip(jnp.exp(math.log(0.001) - 2.3025852 * jax.random.uniform(streams_of[16], (12, C), jnp.float32) ** level_of(streams_of[16], (12, C), ((1, 8),), -0.2, 0.2)), 0.0001, 0.001),
        "table_mean": bell_draw(streams_of[17], (TABLE, HEADS), 0.05, 0.3, (), jnp.float32),
        "table_square": jnp.clip(jnp.exp(jax.random.uniform(streams_of[18], (TABLE, HEADS), jnp.float32, math.log(0.0001), math.log(0.001))), 0.0001, 0.001),
    }


NORM_EPS = 1e-05
LEARN_RATE = 0.02
BETA_ONE = 0.9
BETA_TWO = 0.999
ADAM_EPS = 1e-08
WEIGHT_DECAY = 0.05
MASK_VALUE = -1000000000.0

def to_windows(frame):
    image_count, rows_total, cols_total = (frame.shape[0], frame.shape[1], frame.shape[2])
    trailing = frame.shape[3:]
    blocks = frame.reshape((image_count, rows_total // WIN, WIN, cols_total // WIN, WIN) + trailing)
    blocks = jnp.moveaxis(blocks, 3, 2)
    return blocks.reshape((image_count * (rows_total // WIN) * (cols_total // WIN), WIN * WIN) + trailing)

def from_windows(blocks, image_count, rows_total, cols_total):
    trailing = blocks.shape[2:]
    frame = blocks.reshape((image_count, rows_total // WIN, cols_total // WIN, WIN, WIN) + trailing)
    frame = jnp.moveaxis(frame, 3, 2)
    return frame.reshape((image_count, rows_total, cols_total) + trailing)

def layer_normalize(values):
    center = lax.optimization_barrier(jnp.mean(values, axis=-1, keepdims=True))
    centered = values - center
    variance = lax.optimization_barrier(jnp.mean(centered * centered, axis=-1, keepdims=True))
    inverse_deviation = lax.rsqrt(variance + NORM_EPS)
    return (centered * inverse_deviation, inverse_deviation)

def normalize_backward(gradient_standardized, standardized_input, inverse_deviation):
    return inverse_deviation * (gradient_standardized - lax.optimization_barrier(jnp.mean(gradient_standardized, axis=-1, keepdims=True)) - standardized_input * lax.optimization_barrier(jnp.mean(gradient_standardized * standardized_input, axis=-1, keepdims=True)))

def gelu_parts(hidden_pre):
    normal_cdf = 0.5 * (1.0 + lax.erf(hidden_pre * (1.0 / math.sqrt(2.0))))
    density = jnp.exp(-0.5 * hidden_pre * hidden_pre) * (1.0 / math.sqrt(2.0 * math.pi))
    return (hidden_pre * normal_cdf, normal_cdf + hidden_pre * density)

def window_scores(per_head_queries, per_head_keys, same_region, pos_bias):
    raw = jnp.einsum('wihd,wjhd->whij', per_head_queries.astype(jnp.float32), per_head_keys.astype(jnp.float32))
    return jnp.where(same_region[:, None], raw + pos_bias[None], MASK_VALUE)

def forward(windows_in, same_region, matrices, row_vectors_list, pos_bias):
    attention, expand, shrink = matrices
    window_count, window_size, features = windows_in.shape
    head_count = pos_bias.shape[0]
    head_width = features // head_count
    score_scale = 1.0 / math.sqrt(head_width)
    incoming_tokens = windows_in.reshape(window_count * window_size, features).astype(jnp.float32)
    first_standardized, first_inverse_deviation = layer_normalize(incoming_tokens)
    first_normalized = (first_standardized * (1.0 + row_vectors_list[0]) + row_vectors_list[1]).astype(jnp.bfloat16)
    projected = jnp.dot(first_normalized, attention[:, :3 * features], preferred_element_type=jnp.float32)
    head_shape = (window_count, window_size, head_count, head_width)
    per_head_queries = ((projected[:, :features] + row_vectors_list[2]) * score_scale).astype(jnp.bfloat16).reshape(head_shape)
    per_head_keys = projected[:, features:2 * features].astype(jnp.bfloat16).reshape(head_shape)
    per_head_values = (projected[:, 2 * features:] + row_vectors_list[3]).astype(jnp.bfloat16).reshape(head_shape)
    scores = window_scores(per_head_queries, per_head_keys, same_region, pos_bias)
    row_peak = lax.optimization_barrier(jnp.max(scores, axis=-1, keepdims=True))
    powers = jnp.exp(scores - row_peak)
    totals = lax.optimization_barrier(jnp.sum(powers, axis=-1, keepdims=True))
    logarithm_total = row_peak + jnp.log(totals)
    prob_b = (powers / totals).astype(jnp.bfloat16)
    attended = jnp.einsum('whij,wjhd->wihd', prob_b.astype(jnp.float32), per_head_values.astype(jnp.float32))
    attended_bfloat = attended.reshape(window_count * window_size, features).astype(jnp.bfloat16)
    residual_stream = incoming_tokens + jnp.dot(attended_bfloat, attention[:, 3 * features:], preferred_element_type=jnp.float32) + row_vectors_list[4]
    second_standardized, second_inverse_deviation = layer_normalize(residual_stream)
    second_normalized = (second_standardized * (1.0 + row_vectors_list[5]) + row_vectors_list[6]).astype(jnp.bfloat16)
    hidden_pre = jnp.dot(second_normalized, expand, preferred_element_type=jnp.float32) + row_vectors_list[8:].reshape(-1)
    activated, gaussian_unit_slope = gelu_parts(hidden_pre)
    activated_bfloat = activated.astype(jnp.bfloat16)
    output = residual_stream + jnp.dot(activated_bfloat, shrink, preferred_element_type=jnp.float32) + row_vectors_list[7]
    stored_tensors = (first_standardized, first_inverse_deviation, first_normalized, per_head_queries, per_head_keys, per_head_values, logarithm_total, attended_bfloat, second_standardized, second_inverse_deviation, second_normalized, gaussian_unit_slope, activated_bfloat)
    return (output, stored_tensors)

def backward(stored_tensors, grad_windows, same_region, matrices, row_vectors_list, pos_bias):
    first_standardized, first_inverse_deviation, first_normalized, per_head_queries, per_head_keys, per_head_values, logarithm_total, attended_bfloat, second_standardized, second_inverse_deviation, second_normalized, gaussian_unit_slope, activated_bfloat = stored_tensors
    attention, expand, shrink = matrices
    window_count, window_size, head_count, head_width = per_head_queries.shape
    features = head_count * head_width
    score_scale = 1.0 / math.sqrt(head_width)
    rows_shape = (window_count * window_size, features)
    grad_rows = grad_windows.reshape(rows_shape)
    gradient_single_float = grad_rows.astype(jnp.float32)
    grad_obias = lax.optimization_barrier(jnp.sum(gradient_single_float, axis=0))
    grad_shrink = jnp.dot(activated_bfloat.T, grad_rows, preferred_element_type=jnp.float32)
    grad_act = jnp.dot(grad_rows, shrink.T, preferred_element_type=jnp.float32)
    grad_pre = grad_act * gaussian_unit_slope
    grad_pre_b = grad_pre.astype(jnp.bfloat16)
    grad_ebias = lax.optimization_barrier(jnp.sum(grad_pre, axis=0))
    grad_expand = jnp.dot(second_normalized.T, grad_pre_b, preferred_element_type=jnp.float32)
    gradient_second_normalized = jnp.dot(grad_pre_b, expand.T, preferred_element_type=jnp.float32)
    gradient_second_gain = lax.optimization_barrier(jnp.sum(gradient_second_normalized * second_standardized, axis=0))
    grad_beta_two = lax.optimization_barrier(jnp.sum(gradient_second_normalized, axis=0))
    gradient_residual_stream = gradient_single_float + normalize_backward(gradient_second_normalized * (1.0 + row_vectors_list[5]), second_standardized, second_inverse_deviation)
    grad_resid_b = gradient_residual_stream.astype(jnp.bfloat16)
    grad_pbias = lax.optimization_barrier(jnp.sum(gradient_residual_stream, axis=0))
    grad_outproj = jnp.dot(attended_bfloat.T, grad_resid_b, preferred_element_type=jnp.float32)
    head_shape = (window_count, window_size, head_count, head_width)
    grad_attended = jnp.dot(grad_resid_b, attention[:, 3 * features:].T, preferred_element_type=jnp.float32).astype(jnp.bfloat16).reshape(head_shape)
    scores = window_scores(per_head_queries, per_head_keys, same_region, pos_bias)
    prob_full = jnp.exp(scores - logarithm_total)
    prob_b = prob_full.astype(jnp.bfloat16)
    grad_probs = jnp.einsum('wihd,wjhd->whij', grad_attended.astype(jnp.float32), per_head_values.astype(jnp.float32))
    grad_value = jnp.einsum('whij,wihd->wjhd', prob_b.astype(jnp.float32), grad_attended.astype(jnp.float32))
    inner_sum = lax.optimization_barrier(jnp.sum(prob_full * grad_probs, axis=-1, keepdims=True))
    grad_scores = prob_full * (grad_probs - inner_sum)
    grad_posbias = lax.optimization_barrier(jnp.sum(grad_scores, axis=0))
    grad_scores_b = grad_scores.astype(jnp.bfloat16).astype(jnp.float32)
    grad_query = jnp.einsum('whij,wjhd->wihd', grad_scores_b, per_head_keys.astype(jnp.float32)) * score_scale
    grad_key = jnp.einsum('whij,wihd->wjhd', grad_scores_b, per_head_queries.astype(jnp.float32))
    grad_query = grad_query.reshape(rows_shape)
    grad_value = grad_value.reshape(rows_shape)
    grad_qkv = jnp.concatenate([grad_query, grad_key.reshape(rows_shape), grad_value], axis=1)
    grad_qkv_b = grad_qkv.astype(jnp.bfloat16)
    grad_inproj = jnp.dot(first_normalized.T, grad_qkv_b, preferred_element_type=jnp.float32)
    gradient_first_normalized = jnp.dot(grad_qkv_b, attention[:, :3 * features].T, preferred_element_type=jnp.float32)
    gradient_first_gain = lax.optimization_barrier(jnp.sum(gradient_first_normalized * first_standardized, axis=0))
    grad_beta_one = lax.optimization_barrier(jnp.sum(gradient_first_normalized, axis=0))
    gradient_token_rows = gradient_residual_stream + normalize_backward(gradient_first_normalized * (1.0 + row_vectors_list[0]), first_standardized, first_inverse_deviation)
    grad_attention = jnp.concatenate([grad_inproj, grad_outproj], axis=1)
    grad_vectors = jnp.concatenate([jnp.stack([gradient_first_gain, grad_beta_one, lax.optimization_barrier(jnp.sum(grad_query, axis=0)), lax.optimization_barrier(jnp.sum(grad_value, axis=0)), grad_pbias, gradient_second_gain, grad_beta_two, grad_obias]), grad_ebias.reshape(4, features)], axis=0)
    return (gradient_token_rows, (grad_attention, grad_expand, grad_shrink, grad_vectors, grad_posbias))

def adamw(weight, grad, first, second, decay):
    first_new = BETA_ONE * first + (1.0 - BETA_ONE) * grad
    second_new = BETA_TWO * second + (1.0 - BETA_TWO) * grad * grad
    corr_one = 1.0 - BETA_ONE ** STEP
    corr_two = 1.0 - BETA_TWO ** STEP
    step_dir = first_new / corr_one / (jnp.sqrt(second_new / corr_two) + ADAM_EPS)
    return (weight - LEARN_RATE * (step_dir + decay * weight), first_new, second_new)

def reference(block_input, output_grad, region_ids, relative_index, attention_weight, expand_weight, reduce_weight, vectors, bias_table, attention_mean, attention_square, expand_mean, expand_square, reduce_mean, reduce_square, vectors_mean, vectors_square, table_mean, table_square):
    matrices = (attention_weight.astype(jnp.bfloat16), expand_weight.astype(jnp.bfloat16), reduce_weight.astype(jnp.bfloat16))
    row_vectors_list = lax.optimization_barrier(vectors.astype(jnp.bfloat16)).astype(jnp.float32)
    pos_bias = jnp.transpose(bias_table[relative_index], (2, 0, 1))
    region_windows = to_windows(region_ids[None])
    same_region = region_windows[:, :, None] == region_windows[:, None, :]
    window_size = WIN * WIN

    def shift_in(image):
        return to_windows(jnp.roll(image, (-SHIFT, -SHIFT), axis=(0, 1))[None])

    def shift_out(rows_flat):
        frame = from_windows(rows_flat.reshape(-1, window_size, C), 1, H, W)[0]
        return jnp.roll(frame, (SHIFT, SHIFT), axis=(0, 1))

    def per_image(running, inputs_pair):
        image, grad_image = inputs_pair
        output, stored_tensors = forward(shift_in(image), same_region, matrices, row_vectors_list, pos_bias)
        gradient_token_rows, gradients = backward(stored_tensors, shift_in(grad_image), same_region, matrices, row_vectors_list, pos_bias)
        running = tuple((total + term for total, term in zip(running, gradients)))
        return (running, (shift_out(output), shift_out(gradient_token_rows)))
    start = (jnp.zeros((C, 4 * C), jnp.float32), jnp.zeros((C, FFN), jnp.float32), jnp.zeros((FFN, C), jnp.float32), jnp.zeros((12, C), jnp.float32), jnp.zeros((HEADS, window_size, window_size), jnp.float32))
    sums, (block_output, input_grad) = lax.scan(per_image, start, (block_input, output_grad))
    inv_root = 1.0 / math.sqrt(IMAGES * H * W)
    attention_grad = sums[0] * inv_root
    expand_grad = sums[1] * inv_root
    reduce_grad = sums[2] * inv_root
    vectors_grad = sums[3] * inv_root
    table_grad = jax.ops.segment_sum(sums[4].reshape(HEADS, window_size * window_size).T, relative_index.reshape(-1).astype(jnp.int32), num_segments=TABLE) * inv_root
    new_attention, new_attention_mean, new_attention_square = adamw(attention_weight, attention_grad, attention_mean, attention_square, WEIGHT_DECAY)
    new_expand, new_expand_mean, new_expand_square = adamw(expand_weight, expand_grad, expand_mean, expand_square, WEIGHT_DECAY)
    new_reduce, new_reduce_mean, new_reduce_square = adamw(reduce_weight, reduce_grad, reduce_mean, reduce_square, WEIGHT_DECAY)
    new_vectors, new_vectors_mean, new_vectors_square = adamw(vectors, vectors_grad, vectors_mean, vectors_square, 0.0)
    new_table, new_table_mean, new_table_square = adamw(bias_table, table_grad, table_mean, table_square, 0.0)
    return (block_output, input_grad, attention_grad, expand_grad, reduce_grad, vectors_grad, table_grad, new_attention, new_expand, new_reduce, new_vectors, new_table, new_attention_mean, new_attention_square, new_expand_mean, new_expand_square, new_reduce_mean, new_reduce_square, new_vectors_mean, new_vectors_square, new_table_mean, new_table_square)
```

```python
import functools
import math

import jax
import jax.numpy as jnp
from jax import lax
from jax.experimental import pallas as pl
from jax.experimental.pallas import tpu as pltpu
from jax.sharding import PartitionSpec as P

WIN = 7
SHIFT = 3
STEP = 5


NORM_EPS = 1e-05
LEARN_RATE = 0.02
BETA_ONE = 0.9
BETA_TWO = 0.999
ADAM_EPS = 1e-08
WEIGHT_DECAY = 0.05
MASK_VALUE = -1000000000.0


BF = jnp.bfloat16
F32 = jnp.float32
MESH_ID = pl.DeviceIdType.MESH


def ring_position(index, count):
    column, row = index % 2, index // 2
    return (1 - column) * row + column * (count - 1 - row)


def ring_index(position, count):
    back = position // (count // 2)
    return (1 - back) * (2 * position) + back * (2 * (count - 1 - position) + 1)


def remote(src, dst, send, recv, **where):
    return pltpu.make_async_remote_copy(
        src_ref=src, dst_ref=dst, send_sem=send, recv_sem=recv, device_id=where, device_id_type=MESH_ID
    )


def greet(places):
    barrier = pltpu.get_barrier_semaphore()
    for where in places:
        pl.semaphore_signal(barrier, inc=1, device_id=where, device_id_type=MESH_ID)
    pl.semaphore_wait(barrier, len(places))


def gather_kernel(
    count, att, exp, red, vec, out_att, out_exp, out_red, out_vec,
    ring_send, ring_recv, pair_send, pair_recv, vec_send, vec_recv, own_sem,
):
    shard = lax.axis_index("shard")
    band = lax.axis_index("band")
    core = band % 2
    partner = band + 1 - 2 * core
    pos = ring_position(shard, count)
    to_right = ring_index((pos + 1) % count, count)
    to_left = ring_index((pos + count - 1) % count, count)
    peers = [(shard + j) % count for j in range(1, count)]
    greet([{"shard": peer} for peer in peers] + [{"band": partner}])

    def parts(block, quarter):
        lanes = pl.ds(pl.multiple_of(quarter * 512, 512), 512)
        return (
            out_att.at[block, :, lanes],
            out_exp.at[block, :, lanes],
            out_red.at[block, quarter],
        )

    def own_parts(quarter):
        lanes = pl.ds(pl.multiple_of(quarter * 512, 512), 512)
        return (att.at[:, lanes], exp.at[:, lanes], red.at[quarter])

    sends = []

    def send_ring(way, step):
        quarter = 2 * core + way
        block = ring_index((pos - step + count) % count if way == 0 else (pos + step) % count, count)
        target = to_right if way == 0 else to_left
        sources = own_parts(quarter) if step == 0 else parts(block, quarter)
        for k, (source, place) in enumerate(zip(sources, parts(block, quarter))):
            copy = remote(source, place, ring_send.at[way, step, k], ring_recv.at[way, step, k], shard=target)
            copy.start()
            sends.append(copy)

    for way in range(2):
        send_ring(way, 0)
    own = [
        pltpu.make_async_copy(source, place, own_sem.at[k])
        for k, (source, place) in enumerate(
            ((att, out_att.at[shard]), (exp, out_exp.at[shard]), (red, out_red.at[shard]), (vec, out_vec.at[shard]))
        )
    ]
    for copy in own:
        copy.start()
    for peer, j in zip(peers, range(count - 1)):
        copy = remote(vec, out_vec.at[shard], vec_send.at[j], vec_recv.at[j], shard=peer)
        copy.start()
        sends.append(copy)
    for step in range(count - 1):
        for way in range(2):
            quarter = 2 * core + way
            block = ring_index(
                (pos - step - 1 + count) % count if way == 0 else (pos + step + 1) % count, count
            )
            places = parts(block, quarter)
            for k, place in enumerate(places):
                remote(
                    place, place, ring_send.at[way, step, k], ring_recv.at[way, step, k], shard=to_right
                ).wait_recv()
            if step < count - 2:
                send_ring(way, step + 1)
            for k, place in enumerate(places):
                copy = remote(place, place, pair_send.at[way, step, k], pair_recv.at[way, step, k], band=partner)
                copy.start()
                sends.append(copy)
    for step in range(count - 1):
        for way in range(2):
            quarter = 2 * (1 - core) + way
            block = ring_index(
                (pos - step - 1 + count) % count if way == 0 else (pos + step + 1) % count, count
            )
            for k, place in enumerate(parts(block, quarter)):
                remote(
                    place, place, pair_send.at[way, step, k], pair_recv.at[way, step, k], band=partner
                ).wait_recv()
    for j in range(count - 1):
        source = (shard + count - 1 - j) % count
        remote(vec, out_vec.at[source], vec_send.at[j], vec_recv.at[j], shard=source).wait_recv()
    for copy in sends:
        copy.wait_send()
    for copy in own:
        copy.wait()


VM = pl.BlockSpec(memory_space=pltpu.VMEM)


def gather_shards(att, exp, red, vec):
    count = lax.axis_size("shard")
    rows = att.shape[0]
    dma = pltpu.SemaphoreType.DMA
    return pl.pallas_call(
        lambda *refs: gather_kernel(count, *refs),
        out_shape=(
            jax.ShapeDtypeStruct((count, rows, att.shape[1]), BF),
            jax.ShapeDtypeStruct((count, rows, exp.shape[1]), BF),
            jax.ShapeDtypeStruct((count,) + red.shape, BF),
            jax.ShapeDtypeStruct((count,) + vec.shape, BF),
        ),
        in_specs=[VM] * 4,
        out_specs=[VM] * 4,
        scratch_shapes=[
            dma((2, count - 1, 3)), dma((2, count - 1, 3)), dma((2, count - 1, 3)), dma((2, count - 1, 3)),
            dma((count - 1,)), dma((count - 1,)), dma((4,)),
        ],
        compiler_params=pltpu.CompilerParams(
            collective_id=0, has_side_effects=True, vmem_limit_bytes=48 * 1024 * 1024
        ),
        name="gather_shards",
    )(att, exp, red, vec)


def reduce_kernel(
    count, bands, att, exp, red, small, out_att, out_exp, out_red, out_small,
    paired, sent, got, done, others, mixed, small_band, small_shard,
    pair_send, pair_recv, ring_send, ring_recv, far_send, far_recv, mix_send, mix_recv,
    sb_send, sb_recv, ss_send, ss_recv,
):
    shard = lax.axis_index("shard")
    band = lax.axis_index("band")
    core = band % 2
    partner = band + 1 - 2 * core
    pos = ring_position(shard, count)
    to_right = ring_index((pos + 1) % count, count)
    to_left = ring_index((pos + count - 1) % count, count)
    shard_peers = [(shard + j) % count for j in range(1, count)]
    band_peers = [(band + j) % bands for j in range(1, bands)]
    rows = att.shape[1]
    greet([{"shard": peer} for peer in shard_peers] + [{"band": peer} for peer in band_peers])

    def block_of(way, step):
        if way == 0:
            return ring_index((pos - 1 - step + 2 * count) % count, count)
        return ring_index((pos + 1 + step) % count, count)

    def own_parts(block, quarter):
        lanes = pl.ds(pl.multiple_of(quarter * 512, 512), 512)
        return (att.at[block, :, lanes], exp.at[block, :, lanes], red.at[block, quarter])

    waits = []

    def pair_copy(way, step, k):
        block = block_of(way, step)
        source = own_parts(block, 2 * (1 - core) + way)[k]
        return remote(
            source, paired.at[way, step, k], pair_send.at[way, step, k], pair_recv.at[way, step, k], band=partner
        )

    for step in range(count):
        for way in range(2):
            for k in range(3):
                copy = pair_copy(way, step, k)
                copy.start()
                waits.append(copy)
        if step == 0:
            small_band[band] = small[...]
            for j, peer in enumerate(band_peers):
                copy = remote(small, small_band.at[band], sb_send.at[j], sb_recv.at[j], band=peer)
                copy.start()
                waits.append(copy)

    for step in range(count):
        for way in range(2):
            block = block_of(way, step)
            quarter = 2 * core + way
            if step > 0:
                remote(
                    sent.at[way, step - 1], got.at[way, step - 1],
                    ring_send.at[way, step - 1], ring_recv.at[way, step - 1], shard=to_right,
                ).wait_recv()
            lanes = pl.ds(pl.multiple_of(quarter * 512, 512), 512)
            for k in range(3):
                pair_copy(way, step, k).wait_recv()
                mine = (
                    att[block, :, lanes] if k == 0 else exp[block, :, lanes] if k == 1 else red[block, quarter]
                )
                total = mine.astype(F32) + paired[way, step, k].astype(F32)
                if step > 0:
                    total = total + got[way, step - 1, k].astype(F32)
                if step < count - 1:
                    sent[way, step, k] = total.astype(BF)
                else:
                    done[way, k] = total.astype(BF)
            if step < count - 1:
                copy = remote(
                    sent.at[way, step], got.at[way, step], ring_send.at[way, step], ring_recv.at[way, step],
                    shard=to_right if way == 0 else to_left,
                )
            else:
                for j in range(1, bands // 2):
                    copy = remote(
                        done.at[way], others.at[j - 1, way], far_send.at[j - 1, way], far_recv.at[j - 1, way],
                        band=(band + 2 * j) % bands,
                    )
                    copy.start()
                    waits.append(copy)
                continue
            copy.start()
            waits.append(copy)
        if step == 0:
            for j in range(bands - 1):
                source = (band + bands - 1 - j) % bands
                remote(small, small_band.at[source], sb_send.at[j], sb_recv.at[j], band=source).wait_recv()
            total = small_band[0]
            for j in range(1, bands):
                total = total + small_band[j]
            small_shard[shard] = total
            for j, peer in enumerate(shard_peers):
                copy = remote(
                    small_shard.at[shard], small_shard.at[shard], ss_send.at[j], ss_recv.at[j], shard=peer
                )
                copy.start()
                waits.append(copy)

    for way in range(2):
        for j in range(1, bands // 2):
            remote(
                done.at[way], others.at[j - 1, way], far_send.at[j - 1, way], far_recv.at[j - 1, way], band=partner
            ).wait_recv()
        total = done[way].astype(F32)
        for j in range(1, bands // 2):
            total = total + others[j - 1, way].astype(F32)
        mixed[core, way] = total.astype(BF)
        copy = remote(
            mixed.at[core, way], mixed.at[core, way], mix_send.at[way], mix_recv.at[way], band=partner
        )
        copy.start()
        waits.append(copy)
    for j in range(count - 1):
        source = (shard + count - 1 - j) % count
        remote(small, small_shard.at[source], ss_send.at[j], ss_recv.at[j], shard=source).wait_recv()
    total = small_shard[0]
    for j in range(1, count):
        total = total + small_shard[j]
    out_small[...] = total
    for way in range(2):
        remote(
            mixed.at[core, way], mixed.at[1 - core, way], mix_send.at[way], mix_recv.at[way], band=partner
        ).wait_recv()
    for quarter in range(4):
        out_att[:, quarter * 512 : quarter * 512 + 512] = mixed[quarter // 2, quarter % 2, 0].astype(F32)
        out_exp[:, quarter * 512 : quarter * 512 + 512] = mixed[quarter // 2, quarter % 2, 1].astype(F32)
        out_red[quarter] = mixed[quarter // 2, quarter % 2, 2].astype(F32)
    for copy in waits:
        copy.wait_send()


def reduce_to_owners(att, exp, red, small):
    count = lax.axis_size("shard")
    bands = lax.axis_size("band")
    rows = att.shape[1]
    dma = pltpu.SemaphoreType.DMA
    far = max(bands // 2 - 1, 1)
    return pl.pallas_call(
        lambda *refs: reduce_kernel(count, bands, *refs),
        out_shape=(
            jax.ShapeDtypeStruct(att.shape[1:], F32),
            jax.ShapeDtypeStruct(exp.shape[1:], F32),
            jax.ShapeDtypeStruct(red.shape[1:], F32),
            jax.ShapeDtypeStruct(small.shape, F32),
        ),
        in_specs=[VM] * 4,
        out_specs=[VM] * 4,
        scratch_shapes=[
            pltpu.VMEM((2, count, 3, rows, 512), BF),
            pltpu.VMEM((2, count - 1, 3, rows, 512), BF),
            pltpu.VMEM((2, count - 1, 3, rows, 512), BF),
            pltpu.VMEM((2, 3, rows, 512), BF),
            pltpu.VMEM((far, 2, 3, rows, 512), BF),
            pltpu.VMEM((2, 2, 3, rows, 512), BF),
            pltpu.VMEM((bands,) + small.shape, F32),
            pltpu.VMEM((count,) + small.shape, F32),
            dma((2, count, 3)), dma((2, count, 3)), dma((2, count - 1)), dma((2, count - 1)),
            dma((far, 2)), dma((far, 2)), dma((2,)), dma((2,)),
            dma((bands - 1,)), dma((bands - 1,)), dma((count - 1,)), dma((count - 1,)),
        ],
        compiler_params=pltpu.CompilerParams(
            collective_id=1, has_side_effects=True, vmem_limit_bytes=48 * 1024 * 1024
        ),
        name="reduce_to_owners",
    )(att, exp, red, small)


def passed_along(block, axis, distance):
    devices = range(lax.axis_size(axis))
    route = [((i - distance) % len(devices), i) for i in devices]
    return lax.ppermute(block, axis, route)


def to_windows(frame):
    image_count, rows_total, cols_total = (frame.shape[0], frame.shape[1], frame.shape[2])
    trailing = frame.shape[3:]
    blocks = frame.reshape((image_count, rows_total // WIN, WIN, cols_total // WIN, WIN) + trailing)
    blocks = jnp.moveaxis(blocks, 3, 2)
    return blocks.reshape(
        (image_count * (rows_total // WIN) * (cols_total // WIN), WIN * WIN) + trailing
    )


def from_windows(blocks, image_count, rows_total, cols_total):
    trailing = blocks.shape[2:]
    frame = blocks.reshape((image_count, rows_total // WIN, cols_total // WIN, WIN, WIN) + trailing)
    frame = jnp.moveaxis(frame, 3, 2)
    return frame.reshape((image_count, rows_total, cols_total) + trailing)


PW = 64
NT = (((1,), (1,)), ((), ()))
NN = (((1,), (0,)), ((), ()))
TN = (((0,), (0,)), ((), ()))

def dot(a, b, dims=NN):
    return lax.dot_general(a, b, dims, preferred_element_type=F32)

def norm(v):
    center = jnp.mean(v, axis=1, keepdims=True)
    v = v - center
    r = lax.rsqrt(jnp.mean(v * v, axis=1, keepdims=True) + NORM_EPS)
    return v * r, r

def norm_back(u, xhat, r):
    return r * (u - jnp.mean(u, axis=1, keepdims=True) - xhat * jnp.mean(u * xhat, axis=1, keepdims=True))

def colsum(v):
    return jnp.sum(v, axis=0, keepdims=True)

def gelu_and_slope(e):
    a = jnp.abs(e) * (1.0 / math.sqrt(2.0))
    g = jnp.exp(-0.5 * e * e)
    t = 1.0 / (1.0 + 0.3275911 * a)
    poly = t * (0.254829592 + t * (-0.284496736 + t * (1.421413741 + t * (-1.453152027 + t * 1.061405429))))
    half = 0.5 * poly * g
    cdf = jnp.where(e >= 0, 1.0 - half, half)
    return e * cdf, cdf + e * (g * (1.0 / math.sqrt(2.0 * math.pi)))

def head_mask(h):
    lane = lax.broadcasted_iota(jnp.int32, (PW, 128), 1)
    return (lane >= h * 32) & (lane < h * 32 + 32)

def stack_heads(v):
    zero = jnp.zeros_like(v)
    return jnp.concatenate([jnp.where(head_mask(h), v, zero) for h in range(4)], axis=0)

def pick_heads(r):
    out = jnp.where(head_mask(0), r[0:PW], 0.0)
    for h in range(1, 4):
        out = jnp.where(head_mask(h), r[h * PW:(h + 1) * PW], out)
    return out

def attention_forward(w, g, qkv, allowed, pos, prob, o):
    rows = pl.ds(w * PW, PW)
    q = qkv[rows, g * 128:(g + 1) * 128]
    k = qkv[rows, 512 + g * 128:512 + (g + 1) * 128]
    v = qkv[rows, 1024 + g * 128:1024 + (g + 1) * 128]
    s = dot(k, stack_heads(q), NT)
    s = jnp.where(allowed[w] > 0, s + pos[g], MASK_VALUE)
    e = jnp.exp(s - jnp.max(s, axis=0, keepdims=True))
    p = e * (1.0 / jnp.sum(e, axis=0, keepdims=True))
    prob[w, g] = p
    o[rows, g * 128:(g + 1) * 128] = pick_heads(dot(p.astype(BF), v, TN)).astype(BF)

def attention_backward(w, g, qkv, do, prob, gpos, dqkv, first):
    rows = pl.ds(w * PW, PW)
    q = qkv[rows, g * 128:(g + 1) * 128]
    k = qkv[rows, 512 + g * 128:512 + (g + 1) * 128]
    v = qkv[rows, 1024 + g * 128:1024 + (g + 1) * 128]
    dos = stack_heads(do[rows, g * 128:(g + 1) * 128])
    p = prob[w, g]
    dp = dot(v, dos, NT)
    ds = p * (dp - jnp.sum(p * dp, axis=0, keepdims=True))
    if first:
        gpos[g] = ds
    else:
        gpos[g] += ds
    dsb = ds.astype(BF)
    dq = pick_heads(dot(dsb, k, TN)) * (1.0 / math.sqrt(32.0))
    dk = dot(dsb, stack_heads(q), NN)
    dv = dot(p.astype(BF), dos, NN)
    dqkv[rows, g * 128:(g + 1) * 128] = dq.astype(BF)
    dqkv[rows, 512 + g * 128:512 + (g + 1) * 128] = dk.astype(BF)
    dqkv[rows, 1024 + g * 128:1024 + (g + 1) * 128] = dv.astype(BF)
    return colsum(dq), colsum(dv)

def compute_kernel(x_ref, d_ref, allowed, pos, att, exp, red, vec, y, dt, gatt, gexp, gred, gvec, gpos,
                   h1, qkv, prob, o, r1, xhat2, h2, z, slope, deb, do, dqkv, dr1, *, inv_root):
    x = x_ref[...].astype(F32)
    xhat1, rstd1 = norm(x)
    h1[...] = (xhat1 * (1.0 + vec[0:1]) + vec[1:2]).astype(BF)
    hb = h1[...]
    qkv[:, 0:512] = ((dot(hb, att[:, 0:512]) + vec[2:3]) * (1.0 / math.sqrt(32.0))).astype(BF)
    qkv[:, 512:1024] = dot(hb, att[:, 512:1024]).astype(BF)
    qkv[:, 1024:1536] = (dot(hb, att[:, 1024:1536]) + vec[3:4]).astype(BF)
    for w in range(4):
        for g in range(4):
            attention_forward(w, g, qkv, allowed, pos, prob, o)
    r1[...] = x + dot(o[...], att[:, 1536:2048]) + vec[4:5]
    xh2, rstd2 = norm(r1[...])
    xhat2[...] = xh2
    h2[...] = (xh2 * (1.0 + vec[5:6]) + vec[6:7]).astype(BF)
    d = d_ref[...]
    for c in range(4):
        cols = slice(c * 512, c * 512 + 512)
        e = dot(h2[...], exp[:, cols]) + vec[8 + c:9 + c]
        zz, sl = gelu_and_slope(e)
        z[:, cols] = zz.astype(BF)
        slope[:, cols] = sl
        gred[cols, :] = (dot(zz.astype(BF), d, TN) * inv_root).astype(BF)
    y[...] = r1[...] + dot(z[...], red[...]) + vec[7:8]
    h2t = h2[...].T
    for c in range(4):
        cols = slice(c * 512, c * 512 + 512)
        de = dot(d, red[cols, :], NT) * slope[:, cols]
        gvec[8 + c:9 + c] = colsum(de) * inv_root
        deb[:, cols] = de.astype(BF)
        gexp[:, cols] = (dot(h2t, de.astype(BF)) * inv_root).astype(BF)
    dh2 = dot(deb[...], exp[...], NT)
    df = d.astype(F32)
    gvec[7:8] = colsum(df) * inv_root
    gvec[5:6] = colsum(dh2 * xhat2[...]) * inv_root
    gvec[6:7] = colsum(dh2) * inv_root
    dr = df + norm_back(dh2 * (1.0 + vec[5:6]), xhat2[...], rstd2)
    dr1[...] = dr
    gvec[4:5] = colsum(dr) * inv_root
    drb = dr.astype(BF)
    gatt[:, 1536:2048] = (dot(o[...], drb, TN) * inv_root).astype(BF)
    do[...] = dot(drb, att[:, 1536:2048], NT).astype(BF)
    for g in range(4):
        sq = sv = None
        for w in range(4):
            a, b = attention_backward(w, g, qkv, do, prob, gpos, dqkv, w == 0)
            sq = a if sq is None else sq + a
            sv = b if sv is None else sv + b
        gvec[2:3, g * 128:(g + 1) * 128] = sq * inv_root
        gvec[3:4, g * 128:(g + 1) * 128] = sv * inv_root
    h1t = h1[...].T
    dh1 = jnp.zeros((4 * PW, 512), F32)
    for c in range(3):
        cols = slice(c * 512, c * 512 + 512)
        gatt[:, cols] = (dot(h1t, dqkv[:, cols]) * inv_root).astype(BF)
        dh1 = dh1 + dot(dqkv[:, cols], att[:, cols], NT)
    xhat1, rstd1 = norm(x_ref[...].astype(F32))
    gvec[0:1] = colsum(dh1 * xhat1) * inv_root
    gvec[1:2] = colsum(dh1) * inv_root
    dt[...] = dr1[...] + norm_back(dh1 * (1.0 + vec[0:1]), xhat1, rstd1)


def compute(xw, dw, allowed, pos, att, exp, red, vec, inv_root):
    T = 4 * PW
    sh = jax.ShapeDtypeStruct
    return pl.pallas_call(
        functools.partial(compute_kernel, inv_root=inv_root),
        out_shape=(sh((T, 512), F32), sh((T, 512), F32), sh((512, 2048), BF), sh((512, 2048), BF), sh((2048, 512), BF),
                   sh((16, 512), F32), sh((4, PW, 256), F32)),
        in_specs=[VM] * 8, out_specs=[VM] * 7,
        scratch_shapes=[pltpu.VMEM((T, 512), BF), pltpu.VMEM((T, 1536), BF), pltpu.VMEM((4, 4, PW, 256), F32),
                        pltpu.VMEM((T, 512), BF), pltpu.VMEM((T, 512), F32), pltpu.VMEM((T, 512), F32), pltpu.VMEM((T, 512), BF),
                        pltpu.VMEM((T, 2048), BF), pltpu.VMEM((T, 2048), F32), pltpu.VMEM((T, 2048), BF), pltpu.VMEM((T, 512), BF),
                        pltpu.VMEM((T, 1536), BF), pltpu.VMEM((T, 512), F32)],
        compiler_params=pltpu.CompilerParams(vmem_limit_bytes=56 * 1024 * 1024),
        name="compute",
    )(xw, dw, allowed, pos, att, exp, red, vec)


def adamw(weight, grad, first, second, decay):
    first_new = BETA_ONE * first + (1.0 - BETA_ONE) * grad
    second_new = BETA_TWO * second + (1.0 - BETA_TWO) * grad * grad
    corr_one = 1.0 - BETA_ONE**STEP
    corr_two = 1.0 - BETA_TWO**STEP
    step_dir = first_new / corr_one / (jnp.sqrt(second_new / corr_two) + ADAM_EPS)
    return (weight - LEARN_RATE * (step_dir + decay * weight), first_new, second_new)


def on_device(
    block_input,
    output_grad,
    region_ids,
    relative_index,
    attention_weight,
    expand_weight,
    reduce_weight,
    vectors,
    bias_table,
    attention_mean,
    attention_square,
    expand_mean,
    expand_square,
    reduce_mean,
    reduce_square,
    vectors_mean,
    vectors_square,
    table_mean,
    table_square,
):
    image_count, band_rows, columns, features = block_input.shape
    window_size = WIN * WIN
    shard_count = lax.axis_size("shard")
    band_count = lax.axis_size("band")
    edge_rows = jnp.stack([block_input[:, :SHIFT], output_grad[:, :SHIFT]])
    rows_below = passed_along(edge_rows, "band", -1)
    inner_rows = jnp.stack([block_input[:, SHIFT:], output_grad[:, SHIFT:]])
    shifted = jnp.roll(jnp.concatenate([inner_rows, rows_below], axis=2), -SHIFT, axis=3)
    pad = lambda a: jnp.pad(to_windows(a), ((0, 0), (0, PW - window_size), (0, 0))).reshape(4 * PW, features)
    windows_in = pad(shifted[0])
    grad_windows = pad(shifted[1])
    region_windows = jnp.pad(to_windows(region_ids[None]), ((0, 0), (0, PW - window_size)), constant_values=-1)
    allowed = jnp.tile((region_windows[:, :, None] == region_windows[:, None, :]).astype(F32), (1, 1, 4))
    table_rows = bias_table.shape[0]
    head_count = bias_table.shape[1]
    one_hot = (
        relative_index.reshape(-1)[:, None] == jnp.arange(table_rows, dtype=jnp.int32)[None, :]
    ).astype(jnp.float32)
    pos_bias = jnp.dot(one_hot, bias_table, precision=lax.Precision.HIGHEST).T.reshape(
        head_count, window_size, window_size
    )
    feature_rows = attention_weight.shape[0]
    gathered = gather_shards(
        attention_weight.astype(BF),
        expand_weight.astype(BF),
        reduce_weight.astype(BF).reshape(4, feature_rows, features),
        jnp.pad(vectors.astype(BF), ((0, 4), (0, 128 - vectors.shape[1]))),
    )
    matrices = (
        gathered[0].reshape(features, -1),
        gathered[1].reshape(features, -1),
        gathered[2].reshape(-1, features),
    )
    row_vectors_list = (
        jnp.moveaxis(gathered[3][:, :12, : vectors.shape[1]], 0, 1).reshape(12, features).astype(jnp.float32)
    )
    inv_root = 1.0 / math.sqrt(image_count * shard_count * band_rows * band_count * columns)
    padded_bias = jnp.pad(pos_bias, ((0, 0), (0, PW - window_size), (0, PW - window_size)))
    pos = jnp.transpose(padded_bias.reshape(4, 4, PW, PW), (0, 3, 1, 2)).reshape(4, PW, 4 * PW)
    output_rows, gradient_token_rows, grad_attention, grad_expand, grad_shrink, grad_vectors, grad_pos = compute(
        windows_in, grad_windows, allowed, pos, *matrices, jnp.pad(row_vectors_list, ((0, 4), (0, 0))), inv_root
    )
    unpad = lambda a: a.reshape(4, PW, features)[:, :window_size]
    grad_posbias = jnp.transpose(grad_pos.reshape(4, PW, 4, PW), (0, 2, 3, 1)).reshape(head_count, PW, PW)[
        :, :window_size, :window_size
    ]
    table_local = jnp.dot(
        grad_posbias.reshape(head_count, -1), one_hot, precision=lax.Precision.HIGHEST
    ).T
    vector_terms = 12 * features
    small = jnp.concatenate([grad_vectors[:12].reshape(-1), table_local.reshape(-1) * inv_root])
    small_rows = -(-small.size // 1024) * 8
    small = jnp.pad(small, (0, small_rows * 128 - small.size)).reshape(small_rows, 128)
    attention_grad, expand_grad, reduce_grad, small_sum = reduce_to_owners(
        grad_attention.reshape(shard_count, feature_rows, -1),
        grad_expand.reshape(shard_count, feature_rows, -1),
        grad_shrink.reshape(shard_count, 4, feature_rows, features),
        small,
    )
    reduce_grad = reduce_grad.reshape(reduce_weight.shape)
    small_sum = small_sum.reshape(-1)
    vectors_grad = lax.dynamic_slice_in_dim(
        small_sum[:vector_terms].reshape(12, features),
        lax.axis_index("shard") * vectors.shape[1],
        vectors.shape[1],
        axis=1,
    )
    table_grad = small_sum[vector_terms : vector_terms + bias_table.size].reshape(bias_table.shape)
    frames = jnp.stack(
        [
            from_windows(
                unpad(output_rows), image_count, band_rows, columns
            ),
            from_windows(
                unpad(gradient_token_rows),
                image_count,
                band_rows,
                columns,
            ),
        ]
    )
    frames = jnp.roll(frames, SHIFT, axis=3)
    rows_above = passed_along(
        frames[:, :, band_rows - SHIFT :].astype(jnp.bfloat16), "band", 1
    ).astype(jnp.float32)
    placed = jnp.concatenate([rows_above, frames[:, :, : band_rows - SHIFT]], axis=2)
    new_attention, new_attention_mean, new_attention_square = adamw(
        attention_weight, attention_grad, attention_mean, attention_square, WEIGHT_DECAY
    )
    new_expand, new_expand_mean, new_expand_square = adamw(
        expand_weight, expand_grad, expand_mean, expand_square, WEIGHT_DECAY
    )
    new_reduce, new_reduce_mean, new_reduce_square = adamw(
        reduce_weight, reduce_grad, reduce_mean, reduce_square, WEIGHT_DECAY
    )
    new_vectors, new_vectors_mean, new_vectors_square = adamw(
        vectors, vectors_grad, vectors_mean, vectors_square, 0.0
    )
    new_table, new_table_mean, new_table_square = adamw(
        bias_table, table_grad, table_mean, table_square, 0.0
    )
    return (
        placed[0],
        placed[1],
        attention_grad,
        expand_grad,
        reduce_grad,
        vectors_grad,
        table_grad,
        new_attention,
        new_expand,
        new_reduce,
        new_vectors,
        new_table,
        new_attention_mean,
        new_attention_square,
        new_expand_mean,
        new_expand_square,
        new_reduce_mean,
        new_reduce_square,
        new_vectors_mean,
        new_vectors_square,
        new_table_mean,
        new_table_square,
    )


def solution(mesh):
    return jax.shard_map(
        on_device,
        mesh=mesh,
        in_specs=(
            P("shard", "band", None, None),
            P("shard", "band", None, None),
            P("band", None),
            P(),
            P("shard", None),
            P("shard", None),
            P("shard", None),
            P(None, "shard"),
            P(),
            P("shard", None),
            P("shard", None),
            P("shard", None),
            P("shard", None),
            P("shard", None),
            P("shard", None),
            P(None, "shard"),
            P(None, "shard"),
            P(),
            P(),
        ),
        out_specs=(
            P("shard", "band", None, None),
            P("shard", "band", None, None),
            P("shard", None),
            P("shard", None),
            P("shard", None),
            P(None, "shard"),
            P(),
            P("shard", None),
            P("shard", None),
            P("shard", None),
            P(None, "shard"),
            P(),
            P("shard", None),
            P("shard", None),
            P("shard", None),
            P("shard", None),
            P("shard", None),
            P("shard", None),
            P(None, "shard"),
            P(None, "shard"),
            P(),
            P(),
        ),
        check_vma=False,
    )
```

```python
import functools
import math

import jax
import jax.numpy as jnp
from jax import lax
from jax.experimental import pallas as pl
from jax.experimental.pallas import tpu as pltpu
from jax.sharding import PartitionSpec as P

WIN = 7
SHIFT = 3
STEP = 5
NORM_EPS = 1e-05
LEARN_RATE = 0.02
BETA_ONE = 0.9
BETA_TWO = 0.999
ADAM_EPS = 1e-08
WEIGHT_DECAY = 0.05
MASK_VALUE = -1000000000.0

BF = jnp.bfloat16
F32 = jnp.float32
MESH_ID = pl.DeviceIdType.MESH
VM = pl.BlockSpec(memory_space=pltpu.VMEM)
NN = (((1,), (0,)), ((), ()))
NT = (((1,), (1,)), ((), ()))
TN = (((0,), (0,)), ((), ()))

PW = 64
TOK = 4 * PW
PAIRS = 52 * PW
ATT, EXP, RED = 0, 1, 2
GATHER_SHARE = (256, 384, 128)
REDUCE_SHARE = (0, 256, 128)


def iota(shape, axis):
    return lax.broadcasted_iota(jnp.int32, shape, axis)


def dot(a, b, dims=NN):
    return lax.dot_general(a, b, dims, preferred_element_type=F32)


def colsum(v):
    return jnp.sum(v, axis=0, keepdims=True)


def norm(v):
    v = v - jnp.mean(v, axis=1, keepdims=True)
    r = lax.rsqrt(jnp.mean(v * v, axis=1, keepdims=True) + NORM_EPS)
    return v * r, r


def norm_back(u, xhat, r):
    return r * (u - jnp.mean(u, axis=1, keepdims=True) - xhat * jnp.mean(u * xhat, axis=1, keepdims=True))


def gelu_and_slope(e):
    a = jnp.abs(e) * (1.0 / math.sqrt(2.0))
    g = jnp.exp(-0.5 * e * e)
    t = 1.0 / (1.0 + 0.3275911 * a)
    poly = t * (0.254829592 + t * (-0.284496736 + t * (1.421413741 + t * (-1.453152027 + t * 1.061405429))))
    half = 0.5 * poly * g
    cdf = jnp.where(e >= 0, 1.0 - half, half)
    return e * cdf, cdf + e * (g * (1.0 / math.sqrt(2.0 * math.pi)))


def head_mask(h):
    lane = iota((PW, 128), 1)
    return (lane >= h * 32) & (lane < h * 32 + 32)


def stack_heads(v):
    zero = jnp.zeros_like(v)
    return jnp.concatenate([jnp.where(head_mask(h), v, zero) for h in range(4)], axis=0)


def pick_heads(r):
    out = jnp.where(head_mask(0), r[0:PW], 0.0)
    for h in range(1, 4):
        out = jnp.where(head_mask(h), r[h * PW : (h + 1) * PW], out)
    return out


def attention_forward(w, g, qkv, allowed, pos, prob, o):
    rows = pl.ds(w * PW, PW)
    q = qkv[rows, g * 128 : (g + 1) * 128]
    k = qkv[rows, 512 + g * 128 : 512 + (g + 1) * 128]
    v = qkv[rows, 1024 + g * 128 : 1024 + (g + 1) * 128]
    s = jnp.where(allowed[w] > 0, dot(k, stack_heads(q), NT) + pos[g], MASK_VALUE)
    e = jnp.exp(s - jnp.max(s, axis=0, keepdims=True))
    p = e * (1.0 / jnp.sum(e, axis=0, keepdims=True))
    prob[w, g] = p
    o[rows, g * 128 : (g + 1) * 128] = pick_heads(dot(p.astype(BF), v, TN)).astype(BF)


def attention_backward(w, g, qkv, do, prob, gpos, dqkv, first):
    rows = pl.ds(w * PW, PW)
    q = qkv[rows, g * 128 : (g + 1) * 128]
    k = qkv[rows, 512 + g * 128 : 512 + (g + 1) * 128]
    v = qkv[rows, 1024 + g * 128 : 1024 + (g + 1) * 128]
    dos = stack_heads(do[rows, g * 128 : (g + 1) * 128])
    p = prob[w, g]
    dp = dot(v, dos, NT)
    ds = p * (dp - jnp.sum(p * dp, axis=0, keepdims=True))
    if first:
        gpos[g] = ds
    else:
        gpos[g] += ds
    dsb = ds.astype(BF)
    dq = pick_heads(dot(dsb, k, TN)) * (1.0 / math.sqrt(32.0))
    dk = dot(dsb, stack_heads(q), NN)
    dv = dot(p.astype(BF), dos, NN)
    dqkv[rows, g * 128 : (g + 1) * 128] = dq.astype(BF)
    dqkv[rows, 512 + g * 128 : 512 + (g + 1) * 128] = dk.astype(BF)
    dqkv[rows, 1024 + g * 128 : 1024 + (g + 1) * 128] = dv.astype(BF)
    return colsum(dq), colsum(dv)


def lanes(start, width):
    return pl.ds(pl.multiple_of(start, 128), width)


class Place:
    def __init__(self, count, send, recv):
        self.count, self.zc = count, count // 2
        self.send, self.recv = send, recv
        self.used, self.started = 0, []
        self.shard, self.band = lax.axis_index("shard"), lax.axis_index("band")
        self.x, self.z = self.shard % 2, self.shard // 2
        self.core, self.y = self.band % 2, self.band // 2
        self.to_x = {"shard": self.shard + 1 - 2 * self.x}
        self.to_core = {"band": self.band + 1 - 2 * self.core}
        self.to_y = {"band": (self.band + 2) % 4}

    def to_z(self, j):
        return {"shard": ((self.z + j) % self.zc) * 2 + self.x}

    def block(self, j, other):
        x = 1 - self.x if other else self.x
        return ((self.z + j) % self.zc) * 2 + x

    def greet(self):
        barrier = pltpu.get_barrier_semaphore()
        places = [self.to_z(j) for j in range(1, self.zc)] + [self.to_x]
        places += [{"band": (self.band + j) % 4} for j in range(1, 4)]
        for where in places:
            pl.semaphore_signal(barrier, inc=1, device_id=where, device_id_type=MESH_ID)
        pl.semaphore_wait(barrier, len(places))

    def slots(self, n):
        first = self.used
        self.used += n
        return first

    def copy(self, src, dst, slot, where):
        return pltpu.make_async_remote_copy(
            src_ref=src, dst_ref=dst, send_sem=self.send.at[slot], recv_sem=self.recv.at[slot],
            device_id=where, device_id_type=MESH_ID,
        )

    def put(self, src, dst, slot, where):
        copy = self.copy(src, dst, slot, where)
        copy.start()
        self.started.append(copy)

    def got(self, dst, slot):
        self.copy(dst, dst, slot, self.to_core).wait_recv()

    def done(self):
        for copy in self.started:
            copy.wait_send()


class Gather:
    def __init__(self, at, ref, rows, width, share):
        self.at, self.ref, self.rows, self.share = at, ref, rows, share
        self.half = width // 2
        self.window = self.half - share
        self.zs, self.xs = at.slots(at.zc - 1), at.slots(at.zc)
        self.ys, self.cs = at.slots(2 * at.zc), at.slots(2 * at.zc)

    def part(self, block, start, width):
        rows = pl.ds(pl.multiple_of(block * self.rows, self.rows), self.rows)
        return self.ref.at[rows, lanes(start, width)]

    def mine(self, block):
        at = self.at
        return self.part(block, at.core * self.half + at.y * self.share, self.window)

    def single(self, block, y):
        return self.part(block, self.at.core * self.half + y * self.window, self.share)

    def start(self):
        at = self.at
        own = self.mine(at.shard)
        for j in range(1, at.zc):
            at.put(own, own, self.zs + j - 1, at.to_z(j))
        at.put(own, own, self.xs, at.to_x)

    def over_y(self, j, other):
        if self.share:
            part = self.single(self.at.block(j, other), self.at.y)
            self.at.put(part, part, self.ys + 2 * j + other, self.at.to_y)

    def pass_z(self):
        at = self.at
        for j in range(at.zc - 1, 0, -1):
            part = self.mine(at.block(j, 0))
            at.got(part, self.zs + at.zc - j - 1)
            at.put(part, part, self.xs + j, at.to_x)
            self.over_y(j, 0)

    def pass_x(self):
        at = self.at
        for j in [0] + list(range(at.zc - 1, 0, -1)):
            at.got(self.mine(at.block(j, 1)), self.xs + j)
            self.over_y(j, 1)

    def pass_y(self):
        at = self.at
        for other in (0, 1):
            for j in [0] + list(range(at.zc - 1, 0, -1)):
                if j == 0 and not other:
                    continue
                block = at.block(j, other)
                if self.share:
                    at.got(self.single(block, 1 - at.y), self.ys + 2 * j + other)
                part = self.part(block, at.core * self.half, self.half)
                at.put(part, part, self.cs + 2 * j + other, at.to_core)

    def finish(self):
        at = self.at
        for other in (0, 1):
            for j in range(at.zc):
                if j or other:
                    part = self.part(at.block(j, other), (1 - at.core) * self.half, self.half)
                    at.got(part, self.cs + 2 * j + other)


class Reduce:
    def __init__(self, at, terms, rows, width, share, out, pair, acc, from_y, from_x, from_z, last, last_y):
        self.at, self.terms, self.rows, self.share, self.out = at, terms, rows, share, out
        self.pair, self.acc, self.from_y, self.from_x, self.from_z = pair, acc, from_y, from_x, from_z
        self.last, self.last_y = last, last_y
        self.half = width // 2
        self.window = self.half - share
        self.cs, self.ys, self.xs = at.slots(1), at.slots(1), at.slots(at.zc)
        self.zs, self.ls, self.es = at.slots(at.zc - 1), at.slots(1), at.slots(1)

    def of(self, block):
        return pl.ds(pl.multiple_of(block * self.rows, self.rows), self.rows)

    def start(self):
        at = self.at
        at.put(self.terms.at[:, lanes((1 - at.core) * self.half, self.half)], self.pair, self.cs, at.to_core)

    def sum_pair(self):
        at = self.at
        at.got(self.pair, self.cs)
        mine = lanes(at.core * self.half, self.half)

        def step(b, carry):
            rows = self.of(b)
            self.acc[rows, :] = (self.terms[rows, mine].astype(F32) + self.pair[rows, :].astype(F32)).astype(BF)
            return carry

        lax.fori_loop(0, at.count, step, 0)
        if self.share:
            at.put(self.acc.at[:, lanes((1 - at.y) * self.window, self.share)], self.from_y, self.ys, at.to_y)

    def send_x(self):
        at = self.at
        if self.share:
            at.got(self.from_y, self.ys)
            single = lanes(at.y * self.window, self.share)

            def step(b, carry):
                rows = self.of(b)
                self.acc[rows, single] = (
                    self.acc[rows, single].astype(F32) + self.from_y[rows, :].astype(F32)
                ).astype(BF)
                return carry

            lax.fori_loop(0, at.count, step, 0)
        window = lanes(at.y * self.share, self.window)
        for j in list(range(1, at.zc)) + [0]:
            at.put(self.acc.at[self.of(at.block(j, 1)), window], self.from_x.at[j], self.xs + j, at.to_x)

    def sum_x(self, first=True, rest=True):
        at = self.at
        window = lanes(at.y * self.share, self.window)
        for j in range(1, at.zc):
            at.got(self.from_x.at[j], self.xs + j)
            rows = self.of(at.block(j, 0))
            self.acc[rows, window] = (self.acc[rows, window].astype(F32) + self.from_x[j].astype(F32)).astype(BF)
            at.put(self.acc.at[rows, window], self.from_z.at[j - 1], self.zs + j - 1, at.to_z(j))

    def sum_z(self):
        at = self.at
        window = lanes(at.y * self.share, self.window)
        at.got(self.from_x.at[0], self.xs)
        total = self.acc[self.of(at.shard), window].astype(F32) + self.from_x[0].astype(F32)
        for j in range(1, at.zc):
            at.got(self.from_z.at[j - 1], self.zs + j - 1)
            total = total + self.from_z[j - 1].astype(F32)
        self.last[...] = total.astype(BF)
        at.put(self.last, self.last_y, self.ls, at.to_y)

    def sum_y(self):
        at, share, both = self.at, self.share, self.half - 2 * self.share
        at.got(self.last_y, self.ls)
        base = at.core * self.half
        if share:
            self.out[:, lanes(base + at.y * self.window, share)] = self.last[:, lanes(at.y * both, share)]
            self.out[:, lanes(base + (1 - at.y) * self.window, share)] = self.last_y[:, lanes((1 - at.y) * both, share)]
        if both:
            here, there = lanes((1 - at.y) * share, both), lanes(at.y * share, both)
            self.out[:, lanes(base + share, both)] = (
                self.last[:, here].astype(F32) + self.last_y[:, there].astype(F32)
            ).astype(BF)
        part = self.out.at[:, lanes(base, self.half)]
        at.put(part, part, self.es, at.to_core)

    def finish(self):
        at = self.at
        at.got(self.out.at[:, lanes((1 - at.core) * self.half, self.half)], self.es)


def divide(v, by, most):
    shift = 16
    factor = -(-(1 << shift) // by)
    return (v * factor) >> shift


def window_place(t):
    w, p = t >> 6, t & 63
    i = divide(p, WIN, 64)
    row = (w >> 1) * WIN + i
    col = (w & 1) * WIN + p - i * WIN
    return row, col, p < WIN * WIN


def prepare_masks(regions, padded, allowed):
    padded[...] = jnp.zeros_like(padded)
    padded[0:14, 0:14] = regions[...].astype(F32)
    region = padded[...].astype(BF)
    row, col, real = window_place(iota((TOK, 16), 0))
    pick = ((iota((TOK, 16), 1) == row) & real).astype(F32).astype(BF)
    row, col, real = window_place(iota((TOK, 128), 0))
    by_key = jnp.sum(jnp.where(iota((TOK, 128), 1) == col, dot(pick, region), 0.0), axis=1, keepdims=True)
    row, col, real = window_place(iota((TOK, 1), 0))
    by_key = jnp.where(real, by_key, -1.0)
    for w in range(4):
        row, col, real = window_place(w * PW + (iota((128, TOK), 1) & 63))
        pick = (iota((128, TOK), 0) == col).astype(F32).astype(BF)
        row, col, real = window_place(w * PW + (iota((16, TOK), 1) & 63))
        by_query = colsum(jnp.where(iota((16, TOK), 0) == row, dot(region, pick), 0.0))
        row, col, real = window_place(w * PW + (iota((1, TOK), 1) & 63))
        by_query = jnp.where(real, by_query, -2.0)
        allowed[w] = (by_key[w * PW : (w + 1) * PW] == by_query).astype(F32)


def prepare_bias(relative, table, padded, one_hot, by_head, pos):
    one_hot[...] = (iota((256, PAIRS), 0) == relative[...]).astype(F32).astype(BF)
    padded[...] = jnp.zeros_like(padded)
    padded[:, 0 : table.shape[1]] = table[...]
    left = padded[...]
    total = None
    for _ in range(3):
        part = left.astype(BF)
        left = left - part.astype(F32)
        term = dot(part, one_hot[...])
        total = term if total is None else total + term
    for j in range(WIN * WIN):
        by_head[:, j, :] = total[:, j * PW : (j + 1) * PW]
    for g in range(4):
        pos[g] = jnp.concatenate([by_head[4 * g + h] for h in range(4)], axis=1)


def table_terms(gpos, one_hot, by_head):
    for g in range(4):
        for h in range(4):
            by_head[4 * g + h] = gpos[g][:, h * PW : (h + 1) * PW]
    flat = jnp.concatenate([by_head[:, j, :] for j in range(52)], axis=1)
    high = flat.astype(BF)
    low = (flat - high.astype(F32)).astype(BF)
    return dot(high, one_hot[...], NT) + dot(low, one_hot[...], NT)


def to_windows(frame, own, edge, which, out):
    for r in range(14):
        row = own[r + SHIFT] if r + SHIFT < 14 else edge[which, r + SHIFT - 14]
        frame[r, 0:14, :] = row.astype(F32)
    row, col, real = window_place(iota((TOK, 224), 0))
    col = col + SHIFT
    col = jnp.where(col >= 14, col - 14, col)
    pick = ((iota((TOK, 224), 1) == row * 16 + col) & real).astype(F32).astype(BF)
    out[...] = dot(pick, frame[...].reshape(224, frame.shape[2]).astype(BF)).astype(BF)


def from_windows(values):
    t = iota((208, TOK), 0)
    t = jnp.where(t >= 160, t - 6, t)
    row = divide(t, 14, 256)
    col = t - row * 14 + 14 - SHIFT
    col = jnp.where(col >= 14, col - 14, col)
    right = (col >= WIN).astype(jnp.int32)
    below = (row >= WIN).astype(jnp.int32)
    place = (2 * below + right) * PW + (row - below * WIN) * WIN + col - right * WIN
    pick = (iota((208, TOK), 1) == place).astype(F32).astype(BF)
    high = values.astype(BF)
    low = (values - high.astype(F32)).astype(BF)
    return dot(pick, high) + dot(pick, low)


def block_kernel(
    count, inv_root, x_in, d_in, regions, relative, table, w_att, w_exp, w_red, vectors,
    g_att, g_exp, g_red, small_out, frames, edges_out,
    att, exp, red, t_att, t_exp, t_red,
    pair_a, pair_e, pair_r, acc_a, acc_e, acc_r, fy_e, fy_r, fx_a, fx_e, fx_r, fz_a, fz_e, fz_r,
    last_a, last_e, last_r, ly_a, ly_e, ly_r,
    edges_in, edges_go, vec_own, vec_all, vec,
    small, small_pair, small_sum, small_y, small_x, small_z,
    frame, xw, dw, region_pad, allowed, table_pad, one_hot, by_head, pos,
    h1, qkv, prob, o, r1, xhat2, h2, z, slope, deb, do, dqkv, dr1, gpos,
    send, recv,
):
    at = Place(count, send, recv)
    at.greet()
    rows, rows_red = w_att.shape[0], w_red.shape[0]
    es = at.slots(2)
    before, after = {"band": (at.band + 3) % 4}, {"band": (at.band + 1) % 4}
    for k, source in enumerate((x_in, d_in)):
        at.put(source.at[0:SHIFT], edges_in.at[k], es + k, before)
    gathers = [
        Gather(at, ref, n, ref.shape[1], share)
        for ref, n, share in zip((att, exp, red), (rows, rows, rows_red), GATHER_SHARE)
    ]
    for ref, shard, n, one in zip((att, exp, red), (w_att, w_exp, w_red), (rows, rows, rows_red), gathers):
        ref[pl.ds(pl.multiple_of(at.shard * n, n), n), :] = shard[...].astype(BF)
        if ref is not red:
            one.start()
    width = vectors.shape[1]
    vec_own[...] = jnp.zeros_like(vec_own)
    vec_own[0:12, 0:width] = vectors[...]
    vec_all[at.shard] = vec_own[...].astype(BF)
    vs = at.slots(count - 1)
    order = [(j, 0) for j in range(1, at.zc)] + [(j, 1) for j in range(at.zc)]
    for i, (j, other) in enumerate(order):
        if other:
            continue
        at.put(vec_all.at[at.shard], vec_all.at[at.shard], vs + i, at.to_z(j))
    at.put(vec_all.at[at.shard], vec_all.at[at.shard], vs + at.zc - 1, at.to_x)
    gather_att, gather_exp, gather_red = gathers
    prepare_masks(regions, region_pad, allowed)
    gather_att.pass_z()
    gather_red.start()
    for j in range(at.zc - 1, 0, -1):
        place = vec_all.at[at.block(j, 0)]
        at.got(place, vs + at.zc - j - 1)
        at.put(place, place, vs + at.zc - 1 + j, at.to_x)
    prepare_bias(relative, table, table_pad, one_hot, by_head, pos)
    gather_att.pass_x()
    gather_exp.pass_z()
    frame[...] = jnp.zeros_like(frame)
    for k, (source, windows) in enumerate(((x_in, xw), (d_in, dw))):
        at.got(edges_in.at[k], es + k)
        to_windows(frame, source, edges_in, k, windows)
    for j in range(at.zc):
        at.got(vec_all.at[at.block(j, 1)], vs + at.zc - 1 + j)
    total = None
    for b in range(count):
        place = (iota((128, 512), 1) == b * width + iota((128, 512), 0)) & (iota((128, 512), 0) < width)
        term = dot(vec_all[b], place.astype(F32).astype(BF))
        total = term if total is None else total + term
    vec[...] = total
    gather_att.pass_y()
    gather_att.finish()

    x = xw[...].astype(F32)
    xhat1, rstd1 = norm(x)
    h1[...] = (xhat1 * (1.0 + vec[0:1]) + vec[1:2]).astype(BF)
    hb = h1[...]
    qkv[:, 0:512] = ((dot(hb, att[:, 0:512]) + vec[2:3]) * (1.0 / math.sqrt(32.0))).astype(BF)
    qkv[:, 512:1024] = dot(hb, att[:, 512:1024]).astype(BF)
    qkv[:, 1024:1536] = (dot(hb, att[:, 1024:1536]) + vec[3:4]).astype(BF)
    gather_exp.pass_x()
    gather_red.pass_z()
    for w in range(4):
        for g in range(4):
            attention_forward(w, g, qkv, allowed, pos, prob, o)
        if w == 1:
            gather_exp.pass_y()
            gather_red.pass_x()
    r1[...] = x + dot(o[...], att[:, 1536:2048]) + vec[4:5]
    xh2, rstd2 = norm(r1[...])
    xhat2[...] = xh2
    h2[...] = (xh2 * (1.0 + vec[5:6]) + vec[6:7]).astype(BF)
    gather_exp.finish()
    reduce_red = Reduce(
        at, t_red, rows_red, 512, REDUCE_SHARE[RED], g_red, pair_r, acc_r, fy_r, fx_r, fz_r, last_r, ly_r
    )
    reduce_exp = Reduce(
        at, t_exp, rows, 2048, REDUCE_SHARE[EXP], g_exp, pair_e, acc_e, fy_e, fx_e, fz_e, last_e, ly_e
    )
    reduce_att = Reduce(at, t_att, rows, 2048, REDUCE_SHARE[ATT], g_att, pair_a, acc_a, None, fx_a, fz_a, last_a, ly_a)
    d = dw[...]
    for c in range(4):
        cols = slice(c * 512, c * 512 + 512)
        e = dot(h2[...], exp[:, cols]) + vec[8 + c : 9 + c]
        zz, sl = gelu_and_slope(e)
        z[:, cols] = zz.astype(BF)
        slope[:, cols] = sl
        t_red[cols, :] = (dot(zz.astype(BF), d, TN) * inv_root).astype(BF)
    reduce_red.start()
    gather_red.pass_y()
    gather_red.finish()

    ds_ = at.slots(2)
    h2t = h2[...].T
    for c in range(4):
        cols = slice(c * 512, c * 512 + 512)
        de = dot(d, red[cols, :], NT) * slope[:, cols]
        small[8 + c : 9 + c] = colsum(de) * inv_root
        deb[:, cols] = de.astype(BF)
        t_exp[:, cols] = (dot(h2t, de.astype(BF)) * inv_root).astype(BF)
        if c == 1:
            reduce_red.sum_pair()
    reduce_exp.start()
    out = from_windows(r1[...] + dot(z[...], red[...]) + vec[7:8])
    frames[0] = out[0:160]
    edges_go[0] = out[160:208].astype(BF)
    at.put(edges_go.at[0], edges_out.at[0], ds_, after)
    reduce_exp.sum_pair()
    reduce_red.send_x()
    dh2 = dot(deb[...], exp[...], NT)
    df = d.astype(F32)
    small[7:8] = colsum(df) * inv_root
    small[5:6] = colsum(dh2 * xhat2[...]) * inv_root
    small[6:7] = colsum(dh2) * inv_root
    dr = df + norm_back(dh2 * (1.0 + vec[5:6]), xhat2[...], rstd2)
    dr1[...] = dr
    small[4:5] = colsum(dr) * inv_root
    drb = dr.astype(BF)
    t_att[:, 1536:2048] = (dot(o[...], drb, TN) * inv_root).astype(BF)
    do[...] = dot(drb, att[:, 1536:2048], NT).astype(BF)
    reduce_red.sum_x()
    for g in range(4):
        sq = sv = None
        for w in range(4):
            a, b = attention_backward(w, g, qkv, do, prob, gpos, dqkv, w == 0)
            sq = a if sq is None else sq + a
            sv = b if sv is None else sv + b
        small[2:3, g * 128 : (g + 1) * 128] = sq * inv_root
        small[3:4, g * 128 : (g + 1) * 128] = sv * inv_root
        if g == 1:
            reduce_exp.send_x()
    h1t = h1[...].T
    for c in range(3):
        cols = slice(c * 512, c * 512 + 512)
        t_att[:, cols] = (dot(h1t, dqkv[:, cols]) * inv_root).astype(BF)
    reduce_att.start()
    reduce_red.sum_z()
    dh1 = None
    for c in range(3):
        cols = slice(c * 512, c * 512 + 512)
        term = dot(dqkv[:, cols], att[:, cols], NT)
        dh1 = term if dh1 is None else dh1 + term
    reduce_att.sum_pair()
    reduce_att.send_x()
    reduce_exp.sum_x()
    xhat1, rstd1 = norm(xw[...].astype(F32))
    small[0:1] = colsum(dh1 * xhat1) * inv_root
    small[1:2] = colsum(dh1) * inv_root
    out = from_windows(dr1[...] + norm_back(dh1 * (1.0 + vec[0:1]), xhat1, rstd1))
    frames[1] = out[0:160]
    edges_go[1] = out[160:208].astype(BF)
    at.put(edges_go.at[1], edges_out.at[1], ds_ + 1, after)
    terms = table_terms(gpos, one_hot, by_head) * inv_root
    small[16:24, 0:256] = terms[0:8]
    small[16:24, 256:512] = terms[8:16]
    small[12:16] = jnp.zeros((4, 512), F32)
    ss = at.slots(4 + at.zc)
    at.put(small.at[:, lanes((1 - at.core) * 256, 256)], small_pair, ss, at.to_core)
    reduce_red.sum_y()
    at.got(small_pair, ss)
    small_sum[0] = small[:, lanes(at.core * 256, 256)] + small_pair[...]
    at.put(small_sum.at[0], small_y, ss + 1, at.to_y)
    reduce_exp.sum_z()
    at.got(small_y, ss + 1)
    small_sum[1] = small_sum[0] + small_y[...]
    at.put(small_sum.at[1], small_x, ss + 2, at.to_x)
    reduce_exp.sum_y()
    at.got(small_x, ss + 2)
    small_z[at.z] = small_sum[1] + small_x[...]
    for j in range(1, at.zc):
        at.put(small_z.at[at.z], small_z.at[at.z], ss + 3 + j, at.to_z(j))
    reduce_att.sum_x()
    for j in range(1, at.zc):
        at.got(small_z.at[(at.z + at.zc - j) % at.zc], ss + 3 + j)
    total = small_z[0]
    for j in range(1, at.zc):
        total = total + small_z[j]
    small_out[:, lanes(at.core * 256, 256)] = total
    half = small_out.at[:, lanes(at.core * 256, 256)]
    at.put(half, half, ss + 3, at.to_core)
    reduce_att.sum_z()
    reduce_att.sum_y()
    for k in range(2):
        at.got(edges_out.at[k], ds_ + k)
    at.got(small_out.at[:, lanes((1 - at.core) * 256, 256)], ss + 3)
    for one in (reduce_red, reduce_exp, reduce_att):
        one.finish()
    at.done()
    assert at.used <= send.shape[0]


def block_step(x, d, regions, relative, table, w_att, w_exp, w_red, vectors, inv_root):
    count = lax.axis_size("shard")
    zc = count // 2
    rows, rows_red = w_att.shape[0], w_red.shape[0]
    sh = jax.ShapeDtypeStruct
    v = pltpu.VMEM
    slots = 3 * (7 * zc) + 3 * (2 * zc + 4) + count + zc + 16
    share_a, share_e, share_r = REDUCE_SHARE
    win_a, win_e, win_r = 1024 - share_a, 1024 - share_e, 256 - share_r
    return pl.pallas_call(
        functools.partial(block_kernel, count, inv_root),
        out_shape=(
            sh((rows, 2048), BF), sh((rows, 2048), BF), sh((rows_red, 512), BF), sh((24, 512), F32),
            sh((2, 160, 512), F32), sh((2, 48, 512), BF),
        ),
        in_specs=[VM] * 9,
        out_specs=[VM] * 6,
        scratch_shapes=[
            v((512, 2048), BF), v((512, 2048), BF), v((2048, 512), BF),
            v((512, 2048), BF), v((512, 2048), BF), v((2048, 512), BF),
            v((512, 1024), BF), v((512, 1024), BF), v((2048, 256), BF),
            v((512, 1024), BF), v((512, 1024), BF), v((2048, 256), BF),
            v((512, share_e), BF), v((2048, share_r), BF),
            v((zc, rows, win_a), BF), v((zc, rows, win_e), BF), v((zc, rows_red, win_r), BF),
            v((zc - 1, rows, win_a), BF), v((zc - 1, rows, win_e), BF), v((zc - 1, rows_red, win_r), BF),
            v((rows, win_a), BF), v((rows, win_e), BF), v((rows_red, win_r), BF),
            v((rows, win_a), BF), v((rows, win_e), BF), v((rows_red, win_r), BF),
            v((2, SHIFT, 14, 512), BF), v((2, 48, 512), BF),
            v((16, 128), F32), v((count, 16, 128), BF), v((16, 512), F32),
            v((24, 512), F32), v((24, 256), F32), v((2, 24, 256), F32), v((24, 256), F32), v((24, 256), F32),
            v((zc, 24, 256), F32),
            v((14, 16, 512), F32), v((TOK, 512), BF), v((TOK, 512), BF),
            v((16, 128), F32), v((4, PW, TOK), F32), v((16, 256), F32), v((256, PAIRS), BF), v((16, PW, PW), F32),
            v((4, PW, TOK), F32),
            v((TOK, 512), BF), v((TOK, 1536), BF), v((4, 4, PW, TOK), F32), v((TOK, 512), BF), v((TOK, 512), F32),
            v((TOK, 512), F32), v((TOK, 512), BF), v((TOK, 2048), BF), v((TOK, 2048), F32), v((TOK, 2048), BF),
            v((TOK, 512), BF), v((TOK, 1536), BF), v((TOK, 512), F32), v((4, PW, TOK), F32),
            pltpu.SemaphoreType.DMA((slots,)), pltpu.SemaphoreType.DMA((slots,)),
        ],
        compiler_params=pltpu.CompilerParams(
            collective_id=0, has_side_effects=True, vmem_limit_bytes=52 * 1024 * 1024
        ),
        name="block_step",
    )(x, d, regions, relative, table, w_att, w_exp, w_red, vectors)


def adamw(weight, grad, first, second, decay):
    first_new = BETA_ONE * first + (1.0 - BETA_ONE) * grad
    second_new = BETA_TWO * second + (1.0 - BETA_TWO) * grad * grad
    corr_one = 1.0 - BETA_ONE**STEP
    corr_two = 1.0 - BETA_TWO**STEP
    step_dir = first_new / corr_one / (jnp.sqrt(second_new / corr_two) + ADAM_EPS)
    return (weight - LEARN_RATE * (step_dir + decay * weight), first_new, second_new)


def finish_kernel(steps, frames, edges, small, *refs):
    grads, state, outs = refs[:3], refs[3:18], refs[18:]
    y, dt, o_grads, o_vec, o_table, new = outs[0], outs[1], outs[2:5], outs[5], outs[6], outs[7:]
    for m in range(3):
        grad = grads[m][...].astype(F32)
        o_grads[m][...] = grad
        new[3 * m][...], new[3 * m + 1][...], new[3 * m + 2][...] = adamw(
            state[3 * m][...], grad, state[3 * m + 1][...], state[3 * m + 2][...], WEIGHT_DECAY
        )

    @pl.when(pl.program_id(0) == 0)
    def _():
        width, table = state[9].shape[1], state[12].shape[1]
        turned = pltpu.roll(small[0:16, :], (512 - lax.axis_index("shard") * width) % 512, 1)
        grad = turned[0:12, 0:width]
        o_vec[...] = grad
        new[9][...], new[10][...], new[11][...] = adamw(state[9][...], grad, state[10][...], state[11][...], 0.0)
        grad = jnp.concatenate([small[16:24, 0:256], small[16:24, 256:512]], axis=0)[:, 0:table]
        o_table[...] = grad
        new[12][...], new[13][...], new[14][...] = adamw(state[12][...], grad, state[13][...], state[14][...], 0.0)
        for k, out in enumerate((y, dt)):
            above = edges[k].astype(F32)
            for b in range(4):
                cols = slice(b * 128, b * 128 + 128)
                out[pl.ds(b, 14 * SHIFT, stride=4), :] = above[0 : 14 * SHIFT, cols]
                out[pl.ds(14 * SHIFT * 4 + b, 14 * (14 - SHIFT), stride=4), :] = frames[
                    k, 0 : 14 * (14 - SHIFT), cols
                ]


def finish(grads, small, frames, edges, state):
    rows = state[0].shape[0]
    steps = 4 if rows % 64 == 0 else 1

    def part(a):
        return pl.BlockSpec((a.shape[0] // steps, a.shape[1]), lambda i: (i, 0))

    def whole(a):
        return pl.BlockSpec(a.shape, lambda i: (0,) * len(a.shape))

    sh = jax.ShapeDtypeStruct
    cut = [state[0], state[3], state[6]]
    outs = [sh((784, 128), F32)] * 2 + [sh(a.shape, F32) for a in cut] + [sh(state[9].shape, F32), sh(state[12].shape, F32)]
    outs += [sh(a.shape, F32) for a in state]
    specs = [whole(outs[0])] * 2 + [part(a) for a in cut] + [whole(state[9]), whole(state[12])]
    state_specs = [part(a) for a in state[:9]] + [whole(a) for a in state[9:]]
    return pl.pallas_call(
        functools.partial(finish_kernel, steps),
        grid=(steps,),
        out_shape=outs,
        in_specs=[whole(frames), whole(edges), whole(small)] + [part(a) for a in grads] + state_specs,
        out_specs=specs + state_specs,
        compiler_params=pltpu.CompilerParams(vmem_limit_bytes=40 * 1024 * 1024),
        name="finish",
    )(frames, edges, small, *grads, *state)


def on_device(
    block_input, output_grad, region_ids, relative_index, attention_weight, expand_weight, reduce_weight, vectors,
    bias_table, attention_mean, attention_square, expand_mean, expand_square, reduce_mean, reduce_square,
    vectors_mean, vectors_square, table_mean, table_square,
):
    images, band_rows, columns, features = block_input.shape
    tokens = images * lax.axis_size("shard") * band_rows * lax.axis_size("band") * columns
    relative = jnp.pad(relative_index.T, ((0, 3), (0, PW - WIN * WIN)), constant_values=-1).reshape(1, PAIRS)
    grads = block_step(
        block_input[0], output_grad[0], region_ids, relative, bias_table.T,
        attention_weight, expand_weight, reduce_weight, vectors, 1.0 / math.sqrt(tokens),
    )
    state = (
        attention_weight, attention_mean, attention_square, expand_weight, expand_mean, expand_square,
        reduce_weight, reduce_mean, reduce_square, vectors, vectors_mean, vectors_square,
        bias_table.T, table_mean.T, table_square.T,
    )
    outs = finish(grads[:3], grads[3], grads[4], grads[5], state)
    y, dt, grad_a, grad_e, grad_r, grad_v, grad_t = outs[:7]
    new = outs[7:]
    shape = block_input.shape
    return (
        y.reshape(shape), dt.reshape(shape), grad_a, grad_e, grad_r, grad_v, grad_t.T,
        new[0], new[3], new[6], new[9], new[12].T,
        new[1], new[2], new[4], new[5], new[7], new[8], new[10], new[11], new[13].T, new[14].T,
    )


def solution(mesh):
    return jax.shard_map(
        on_device,
        mesh=mesh,
        in_specs=(
            P("shard", "band", None, None),
            P("shard", "band", None, None),
            P("band", None),
            P(),
            P("shard", None),
            P("shard", None),
            P("shard", None),
            P(None, "shard"),
            P(),
            P("shard", None),
            P("shard", None),
            P("shard", None),
            P("shard", None),
            P("shard", None),
            P("shard", None),
            P(None, "shard"),
            P(None, "shard"),
            P(),
            P(),
        ),
        out_specs=(
            P("shard", "band", None, None),
            P("shard", "band", None, None),
            P("shard", None),
            P("shard", None),
            P("shard", None),
            P(None, "shard"),
            P(),
            P("shard", None),
            P("shard", None),
            P("shard", None),
            P(None, "shard"),
            P(),
            P("shard", None),
            P("shard", None),
            P("shard", None),
            P("shard", None),
            P("shard", None),
            P("shard", None),
            P(None, "shard"),
            P(None, "shard"),
            P(),
            P(),
        ),
        check_vma=False,
    )
```

```python
import functools
import math

import jax
import jax.numpy as jnp
from jax import lax
from jax.experimental import pallas as pl
from jax.experimental.pallas import tpu as pltpu
from jax.sharding import PartitionSpec as P

WIN = 7
SHIFT = 3
STEP = 5
NORM_EPS = 1e-05
LEARN_RATE = 0.02
BETA_ONE = 0.9
BETA_TWO = 0.999
ADAM_EPS = 1e-08
WEIGHT_DECAY = 0.05
MASK_VALUE = -1000000000.0

BF = jnp.bfloat16
F32 = jnp.float32
MESH_ID = pl.DeviceIdType.MESH
VM = pl.BlockSpec(memory_space=pltpu.VMEM)
HBM = pl.BlockSpec(memory_space=pltpu.HBM)
NN = (((1,), (0,)), ((), ()))
NT = (((1,), (1,)), ((), ()))
TN = (((0,), (0,)), ((), ()))

PW = 64
TOK = 4 * PW
PAIRS = 52 * PW
ATT, EXP, RED = 0, 1, 2
GATHER_SHARE = (512, 256, 128)
DEPTH, LAG = 2, (1, 8)
REDUCE_SHARE = (0, 512, 0)


def iota(shape, axis):
    return lax.broadcasted_iota(jnp.int32, shape, axis)


def dot(a, b, dims=NN):
    return lax.dot_general(a, b, dims, preferred_element_type=F32)


def colsum(v):
    return jnp.sum(v, axis=0, keepdims=True)


def norm(v):
    v = v - jnp.mean(v, axis=1, keepdims=True)
    r = lax.rsqrt(jnp.mean(v * v, axis=1, keepdims=True) + NORM_EPS)
    return v * r, r


def norm_back(u, xhat, r):
    return r * (u - jnp.mean(u, axis=1, keepdims=True) - xhat * jnp.mean(u * xhat, axis=1, keepdims=True))


def gelu_and_slope(e):
    a = jnp.abs(e) * (1.0 / math.sqrt(2.0))
    g = jnp.exp(-0.5 * e * e)
    t = 1.0 / (1.0 + 0.3275911 * a)
    poly = t * (0.254829592 + t * (-0.284496736 + t * (1.421413741 + t * (-1.453152027 + t * 1.061405429))))
    half = 0.5 * poly * g
    cdf = jnp.where(e >= 0, 1.0 - half, half)
    return e * cdf, cdf + e * (g * (1.0 / math.sqrt(2.0 * math.pi)))


def head_mask(h):
    lane = iota((PW, 128), 1)
    return (lane >= h * 32) & (lane < h * 32 + 32)


def stack_heads(v):
    zero = jnp.zeros_like(v)
    return jnp.concatenate([jnp.where(head_mask(h), v, zero) for h in range(4)], axis=0)


def pick_heads(r):
    out = jnp.where(head_mask(0), r[0:PW], 0.0)
    for h in range(1, 4):
        out = jnp.where(head_mask(h), r[h * PW : (h + 1) * PW], out)
    return out


def attention_forward(w, g, qkv, allowed, pos, prob, o):
    rows = pl.ds(w * PW, PW)
    q = qkv[rows, g * 128 : (g + 1) * 128]
    k = qkv[rows, 512 + g * 128 : 512 + (g + 1) * 128]
    v = qkv[rows, 1024 + g * 128 : 1024 + (g + 1) * 128]
    s = jnp.where(allowed[w] > 0, dot(k, stack_heads(q), NT) + pos[g], MASK_VALUE)
    e = jnp.exp(s - jnp.max(s, axis=0, keepdims=True))
    p = e * (1.0 / jnp.sum(e, axis=0, keepdims=True))
    prob[w, g] = p
    o[rows, g * 128 : (g + 1) * 128] = pick_heads(dot(p.astype(BF), v, TN)).astype(BF)


def attention_backward(w, g, qkv, do, prob, gpos, dqkv, first):
    rows = pl.ds(w * PW, PW)
    q = qkv[rows, g * 128 : (g + 1) * 128]
    k = qkv[rows, 512 + g * 128 : 512 + (g + 1) * 128]
    v = qkv[rows, 1024 + g * 128 : 1024 + (g + 1) * 128]
    dos = stack_heads(do[rows, g * 128 : (g + 1) * 128])
    p = prob[w, g]
    dp = dot(v, dos, NT)
    ds = p * (dp - jnp.sum(p * dp, axis=0, keepdims=True))
    if first:
        gpos[g] = ds
    else:
        gpos[g] += ds
    dsb = ds.astype(BF)
    dq = pick_heads(dot(dsb, k, TN)) * (1.0 / math.sqrt(32.0))
    dk = dot(dsb, stack_heads(q), NN)
    dv = dot(p.astype(BF), dos, NN)
    dqkv[rows, g * 128 : (g + 1) * 128] = dq.astype(BF)
    dqkv[rows, 512 + g * 128 : 512 + (g + 1) * 128] = dk.astype(BF)
    dqkv[rows, 1024 + g * 128 : 1024 + (g + 1) * 128] = dv.astype(BF)
    return colsum(dq), colsum(dv)


def lanes(start, width):
    return pl.ds(pl.multiple_of(start, 128), width)


class Place:
    def __init__(self, count, send, recv):
        self.count, self.zc = count, count // 2
        self.send, self.recv = send, recv
        self.used, self.started = 0, []
        self.shard, self.band = lax.axis_index("shard"), lax.axis_index("band")
        self.x, self.z = self.shard % 2, self.shard // 2
        self.core, self.y = self.band % 2, self.band // 2
        self.to_x = {"shard": self.shard + 1 - 2 * self.x}
        self.to_core = {"band": self.band + 1 - 2 * self.core}
        self.to_y = {"band": (self.band + 2) % 4}

    def to_z(self, j):
        return {"shard": ((self.z + j) % self.zc) * 2 + self.x}

    def block(self, j, other):
        x = 1 - self.x if other else self.x
        return ((self.z + j) % self.zc) * 2 + x

    def greet(self):
        barrier = pltpu.get_barrier_semaphore()
        places = [self.to_z(j) for j in range(1, self.zc)] + [self.to_x]
        places += [{"band": (self.band + j) % 4} for j in range(1, 4)]
        for where in places:
            pl.semaphore_signal(barrier, inc=1, device_id=where, device_id_type=MESH_ID)
        pl.semaphore_wait(barrier, len(places))

    def slots(self, n):
        first = self.used
        self.used += n
        return first

    def copy(self, src, dst, slot, where):
        return pltpu.make_async_remote_copy(
            src_ref=src, dst_ref=dst, send_sem=self.send.at[slot], recv_sem=self.recv.at[slot],
            device_id=where, device_id_type=MESH_ID,
        )

    def put(self, src, dst, slot, where):
        copy = self.copy(src, dst, slot, where)
        copy.start()
        self.started.append(copy)

    def got(self, dst, slot):
        self.copy(dst, dst, slot, self.to_core).wait_recv()

    def done(self):
        for copy in self.started:
            copy.wait_send()


class Gather:
    def __init__(self, at, ref, rows, width, share):
        self.at, self.ref, self.rows, self.share = at, ref, rows, share
        self.half = width // 2
        self.window = self.half - share
        self.zs, self.xs = at.slots(at.zc - 1), at.slots(at.zc)
        self.ys, self.cs = at.slots(2 * at.zc), at.slots(2 * at.zc)

    def part(self, block, start, width):
        rows = pl.ds(pl.multiple_of(block * self.rows, self.rows), self.rows)
        return self.ref.at[rows, lanes(start, width)]

    def mine(self, block):
        at = self.at
        return self.part(block, at.core * self.half + at.y * self.share, self.window)

    def single(self, block, y):
        return self.part(block, self.at.core * self.half + y * self.window, self.share)

    def send_z(self, j):
        own = self.mine(self.at.shard)
        self.at.put(own, own, self.zs + j - 1, self.at.to_z(j))

    def send_x(self, j):
        part = self.mine(self.at.block(j, 0))
        self.at.put(part, part, self.xs + j, self.at.to_x)

    def over_y(self, j, other):
        if self.share:
            part = self.single(self.at.block(j, other), self.at.y)
            self.at.put(part, part, self.ys + 2 * j + other, self.at.to_y)

    def pass_z(self, j):
        self.at.got(self.mine(self.at.block(j, 0)), self.zs + self.at.zc - j - 1)
        self.send_x(j)
        self.over_y(j, 0)

    def pass_x(self, j):
        self.at.got(self.mine(self.at.block(j, 1)), self.xs + j)
        self.over_y(j, 1)

    def pass_y(self, j, other):
        at = self.at
        block = at.block(j, other)
        if self.share:
            at.got(self.single(block, 1 - at.y), self.ys + 2 * j + other)
        part = self.part(block, at.core * self.half, self.half)
        at.put(part, part, self.cs + 2 * j + other, at.to_core)

    def finish(self):
        at = self.at
        for other in (0, 1):
            for j in range(at.zc):
                if j or other:
                    part = self.part(at.block(j, other), (1 - at.core) * self.half, self.half)
                    at.got(part, self.cs + 2 * j + other)


class Pump:
    def __init__(self, at, gathers):
        near = range(at.zc - 1, 0, -1)
        self.sends = [(one, j) for one in gathers for j in range(1, at.zc)]
        self.events, self.at, self.step, self.marks = [], at, 0, {}
        zs = [(one, j) for one in gathers for j in near]
        xs = [(one, j) for one in gathers for j in [0] + list(near)]
        ys = [(one, j, o) for one in gathers for j, o in [(0, 1)] + [(j, o) for j in near for o in (0, 1)]]
        lag_x, lag_y = LAG
        done_x = done_y = 0
        for k in range(len(zs) + lag_y + 1):
            if k < len(zs):
                self.events.append(("z",) + zs[k])
            want = len(xs) if k >= len(zs) + lag_x - 1 else max(0, (k - lag_x + 1) * at.zc // (at.zc - 1))
            while done_x < min(want, len(xs)):
                self.events.append(("x",) + xs[done_x])
                done_x += 1
            want = len(ys) if k >= len(zs) + lag_y - 1 else max(0, (k - lag_y + 1) * (2 * at.zc - 1) // (at.zc - 1))
            while done_y < min(want, len(ys)):
                self.events.append(("y",) + ys[done_y])
                done_y += 1
        self.next_send = 0
        self.last = {}
        for k, event in enumerate(self.events):
            self.last[event[1]] = k

    def issue(self, n):
        while self.next_send < min(n, len(self.sends)):
            one, j = self.sends[self.next_send]
            one.send_z(j)
            self.next_send += 1

    def begin(self, gathers):
        gathers[0].send_x(0)
        self.issue(DEPTH)
        for one in gathers[1:]:
            one.send_x(0)

    def run(self, upto=None):
        stop = len(self.events) if upto is None else self.last[upto] + 1
        while self.step < stop:
            kind, one, *where = self.events[self.step]
            if kind == "z":
                self.issue(sum(e[0] == "z" for e in self.events[: self.step]) + 1 + DEPTH)
                one.pass_z(*where)
            elif kind == "x":
                one.pass_x(*where)
            else:
                one.pass_y(*where)
            self.step += 1


class Reduce:
    def __init__(self, at, terms, rows, width, share, out, pair, acc, from_y, from_x, from_z, last, last_y):
        self.at, self.terms, self.rows, self.share, self.out = at, terms, rows, share, out
        self.pair, self.acc, self.from_y, self.from_x, self.from_z = pair, acc, from_y, from_x, from_z
        self.last, self.last_y = last, last_y
        self.half = width // 2
        self.window = self.half - share
        self.cs, self.ys, self.xs = at.slots(1), at.slots(1), at.slots(at.zc)
        self.zs, self.ls, self.es = at.slots(at.zc - 1), at.slots(1), at.slots(1)

    def of(self, block):
        return pl.ds(pl.multiple_of(block * self.rows, self.rows), self.rows)

    def start(self):
        at = self.at
        at.put(self.terms.at[:, lanes((1 - at.core) * self.half, self.half)], self.pair, self.cs, at.to_core)

    def sum_pair(self):
        at = self.at
        at.got(self.pair, self.cs)
        mine = lanes(at.core * self.half, self.half)

        def step(b, carry):
            rows = self.of(b)
            self.acc[rows, :] = (self.terms[rows, mine].astype(F32) + self.pair[rows, :].astype(F32)).astype(BF)
            return carry

        lax.fori_loop(0, at.count, step, 0)
        if self.share:
            at.put(self.acc.at[:, lanes((1 - at.y) * self.window, self.share)], self.from_y, self.ys, at.to_y)

    def send_x(self):
        at = self.at
        if self.share:
            at.got(self.from_y, self.ys)
            single = lanes(at.y * self.window, self.share)

            def step(b, carry):
                rows = self.of(b)
                self.acc[rows, single] = (
                    self.acc[rows, single].astype(F32) + self.from_y[rows, :].astype(F32)
                ).astype(BF)
                return carry

            lax.fori_loop(0, at.count, step, 0)
        window = lanes(at.y * self.share, self.window)
        for j in list(range(1, at.zc)) + [0]:
            at.put(self.acc.at[self.of(at.block(j, 1)), window], self.from_x.at[j], self.xs + j, at.to_x)

    def sum_x(self, some=None):
        at = self.at
        window = lanes(at.y * self.share, self.window)
        for j in range(1, at.zc) if some is None else some:
            at.got(self.from_x.at[j], self.xs + j)
            rows = self.of(at.block(j, 0))
            self.acc[rows, window] = (self.acc[rows, window].astype(F32) + self.from_x[j].astype(F32)).astype(BF)
            at.put(self.acc.at[rows, window], self.from_z.at[j - 1], self.zs + j - 1, at.to_z(j))

    def sum_z(self):
        at = self.at
        window = lanes(at.y * self.share, self.window)
        at.got(self.from_x.at[0], self.xs)
        total = self.acc[self.of(at.shard), window].astype(F32) + self.from_x[0].astype(F32)
        for j in range(1, at.zc):
            at.got(self.from_z.at[j - 1], self.zs + j - 1)
            total = total + self.from_z[j - 1].astype(F32)
        self.last[...] = total.astype(BF)
        at.put(self.last, self.last_y, self.ls, at.to_y)

    def sum_y(self):
        at, share, both = self.at, self.share, self.half - 2 * self.share
        at.got(self.last_y, self.ls)
        base = at.core * self.half
        if share:
            self.out[:, lanes(base + at.y * self.window, share)] = self.last[:, lanes(at.y * both, share)]
            self.out[:, lanes(base + (1 - at.y) * self.window, share)] = self.last_y[:, lanes((1 - at.y) * both, share)]
        if both:
            here, there = lanes((1 - at.y) * share, both), lanes(at.y * share, both)
            self.out[:, lanes(base + share, both)] = (
                self.last[:, here].astype(F32) + self.last_y[:, there].astype(F32)
            ).astype(BF)
        part = self.out.at[:, lanes(base, self.half)]
        at.put(part, part, self.es, at.to_core)

    def finish(self):
        at = self.at
        at.got(self.out.at[:, lanes((1 - at.core) * self.half, self.half)], self.es)


def divide(v, by, most):
    shift = 16
    factor = -(-(1 << shift) // by)
    return (v * factor) >> shift


def window_place(t):
    w, p = t >> 6, t & 63
    i = divide(p, WIN, 64)
    row = (w >> 1) * WIN + i
    col = (w & 1) * WIN + p - i * WIN
    return row, col, p < WIN * WIN


def prepare_masks(regions, padded, allowed):
    padded[...] = jnp.zeros_like(padded)
    padded[0:14, 0:14] = regions[...].astype(F32)
    region = padded[...].astype(BF)
    row, col, real = window_place(iota((TOK, 16), 0))
    pick = ((iota((TOK, 16), 1) == row) & real).astype(F32).astype(BF)
    row, col, real = window_place(iota((TOK, 128), 0))
    by_key = jnp.sum(jnp.where(iota((TOK, 128), 1) == col, dot(pick, region), 0.0), axis=1, keepdims=True)
    row, col, real = window_place(iota((TOK, 1), 0))
    by_key = jnp.where(real, by_key, -1.0)
    for w in range(4):
        row, col, real = window_place(w * PW + (iota((128, TOK), 1) & 63))
        pick = (iota((128, TOK), 0) == col).astype(F32).astype(BF)
        row, col, real = window_place(w * PW + (iota((16, TOK), 1) & 63))
        by_query = colsum(jnp.where(iota((16, TOK), 0) == row, dot(region, pick), 0.0))
        row, col, real = window_place(w * PW + (iota((1, TOK), 1) & 63))
        by_query = jnp.where(real, by_query, -2.0)
        allowed[w] = (by_key[w * PW : (w + 1) * PW] == by_query).astype(F32)


def prepare_bias(relative, table, padded, one_hot, by_head, pos):
    one_hot[...] = (iota((256, PAIRS), 0) == relative[...]).astype(F32).astype(BF)
    padded[...] = jnp.zeros_like(padded)
    padded[:, 0 : table.shape[1]] = table[...]
    left = padded[...]
    total = None
    for _ in range(3):
        part = left.astype(BF)
        left = left - part.astype(F32)
        term = dot(part, one_hot[...])
        total = term if total is None else total + term
    for j in range(WIN * WIN):
        by_head[:, j, :] = total[:, j * PW : (j + 1) * PW]
    for g in range(4):
        pos[g] = jnp.concatenate([by_head[4 * g + h] for h in range(4)], axis=1)


def table_terms(gpos, one_hot, by_head):
    for g in range(4):
        for h in range(4):
            by_head[4 * g + h] = gpos[g][:, h * PW : (h + 1) * PW]
    flat = jnp.concatenate([by_head[:, j, :] for j in range(52)], axis=1)
    high = flat.astype(BF)
    low = (flat - high.astype(F32)).astype(BF)
    return dot(high, one_hot[...], NT) + dot(low, one_hot[...], NT)


def to_windows(frame, own, edge, which, out):
    for r in range(14):
        row = own[r + SHIFT] if r + SHIFT < 14 else edge[which, r + SHIFT - 14]
        frame[r, 0:14, :] = row.astype(F32)
    row, col, real = window_place(iota((TOK, 224), 0))
    col = col + SHIFT
    col = jnp.where(col >= 14, col - 14, col)
    pick = ((iota((TOK, 224), 1) == row * 16 + col) & real).astype(F32).astype(BF)
    out[...] = dot(pick, frame[...].reshape(224, frame.shape[2]).astype(BF)).astype(BF)


def from_windows(values):
    t = iota((208, TOK), 0)
    t = jnp.where(t >= 160, t - 6, t)
    row = divide(t, 14, 256)
    col = t - row * 14 + 14 - SHIFT
    col = jnp.where(col >= 14, col - 14, col)
    right = (col >= WIN).astype(jnp.int32)
    below = (row >= WIN).astype(jnp.int32)
    place = (2 * below + right) * PW + (row - below * WIN) * WIN + col - right * WIN
    pick = (iota((208, TOK), 1) == place).astype(F32).astype(BF)
    high = values.astype(BF)
    low = (values - high.astype(F32)).astype(BF)
    return dot(pick, high) + dot(pick, low)


def block_kernel(
    count, inv_root, x_hbm, d_hbm, regions, relative, table, a_hbm, e_hbm, r_hbm, vectors,
    g_att, g_exp, g_red, small_out, frames, edges_out,
    att, exp, red, t_att, t_exp, t_red,
    pair_a, pair_e, pair_r, acc_a, acc_e, acc_r, fy_e, fx_a, fx_e, fx_r, fz_a, fz_e, fz_r,
    last_a, last_e, last_r, ly_a, ly_e, ly_r,
    edges_in, edges_go, vec_own, vec_all, vec,
    small, small_pair, small_sum, small_y, small_x, small_z,
    frame, xw, dw, region_pad, allowed, table_pad, one_hot, by_head, pos,
    h1, qkv, prob, o, r1, xhat2, h2, z, slope, deb, do, dqkv, dr1, gpos,
    x_in, d_in, w_att, w_exp, w_red, loads, send, recv,
):
    at = Place(count, send, recv)
    fetch = [
        pltpu.make_async_copy(source, place, loads.at[k])
        for k, (source, place) in enumerate(
            ((x_hbm, x_in), (d_hbm, d_in), (a_hbm, w_att), (e_hbm, w_exp), (r_hbm, w_red))
        )
    ]
    for copy in fetch:
        copy.start()
    at.greet()
    for copy in fetch:
        copy.wait()
    rows, rows_red = w_att.shape[0], w_red.shape[0]
    es = at.slots(2)
    before, after = {"band": (at.band + 3) % 4}, {"band": (at.band + 1) % 4}
    for k, source in enumerate((x_in, d_in)):
        at.put(source.at[0:SHIFT], edges_in.at[k], es + k, before)
    width = vectors.shape[1]
    vec_own[...] = jnp.zeros_like(vec_own)
    vec_own[0:12, 0:width] = vectors[...]
    vec_all[at.shard] = vec_own[...].astype(BF)
    vs = at.slots(count - 1)
    order = [(j, 0) for j in range(1, at.zc)] + [(j, 1) for j in range(at.zc)]
    for i, (j, other) in enumerate(order):
        if other:
            continue
        at.put(vec_all.at[at.shard], vec_all.at[at.shard], vs + i, at.to_z(j))
    at.put(vec_all.at[at.shard], vec_all.at[at.shard], vs + at.zc - 1, at.to_x)
    gathers = [
        Gather(at, ref, n, ref.shape[1], share)
        for ref, n, share in zip((att, exp, red), (rows, rows, rows_red), GATHER_SHARE)
    ]
    for ref, shard, n, one in zip((att, exp, red), (w_att, w_exp, w_red), (rows, rows, rows_red), gathers):
        ref[pl.ds(pl.multiple_of(at.shard * n, n), n), :] = shard[...].astype(BF)
    pump = Pump(at, gathers)
    pump.begin(gathers)
    for j in range(at.zc - 1, 0, -1):
        place = vec_all.at[at.block(j, 0)]
        at.got(place, vs + at.zc - j - 1)
        at.put(place, place, vs + at.zc - 1 + j, at.to_x)
    prepare_masks(regions, region_pad, allowed)
    prepare_bias(relative, table, table_pad, one_hot, by_head, pos)
    gather_att, gather_exp, gather_red = gathers
    pump.run(gather_att)
    frame[...] = jnp.zeros_like(frame)
    for k, (source, windows) in enumerate(((x_in, xw), (d_in, dw))):
        at.got(edges_in.at[k], es + k)
        to_windows(frame, source, edges_in, k, windows)
    for j in range(at.zc):
        at.got(vec_all.at[at.block(j, 1)], vs + at.zc - 1 + j)
    total = None
    for b in range(count):
        place = (iota((128, 512), 1) == b * width + iota((128, 512), 0)) & (iota((128, 512), 0) < width)
        term = dot(vec_all[b], place.astype(F32).astype(BF))
        total = term if total is None else total + term
    vec[...] = total
    gather_att.finish()

    x = xw[...].astype(F32)
    xhat1, rstd1 = norm(x)
    h1[...] = (xhat1 * (1.0 + vec[0:1]) + vec[1:2]).astype(BF)
    hb = h1[...]
    qkv[:, 0:512] = ((dot(hb, att[:, 0:512]) + vec[2:3]) * (1.0 / math.sqrt(32.0))).astype(BF)
    qkv[:, 512:1024] = dot(hb, att[:, 512:1024]).astype(BF)
    qkv[:, 1024:1536] = (dot(hb, att[:, 1024:1536]) + vec[3:4]).astype(BF)
    pump.run(gather_exp)
    for w in range(4):
        for g in range(4):
            attention_forward(w, g, qkv, allowed, pos, prob, o)
    r1[...] = x + dot(o[...], att[:, 1536:2048]) + vec[4:5]
    xh2, rstd2 = norm(r1[...])
    xhat2[...] = xh2
    h2[...] = (xh2 * (1.0 + vec[5:6]) + vec[6:7]).astype(BF)
    gather_exp.finish()
    reduce_red = Reduce(
        at, t_red, rows_red, 512, REDUCE_SHARE[RED], g_red, pair_r, acc_r, None, fx_r, fz_r, last_r, ly_r
    )
    reduce_exp = Reduce(
        at, t_exp, rows, 2048, REDUCE_SHARE[EXP], g_exp, pair_e, acc_e, fy_e, fx_e, fz_e, last_e, ly_e
    )
    reduce_att = Reduce(at, t_att, rows, 2048, REDUCE_SHARE[ATT], g_att, pair_a, acc_a, None, fx_a, fz_a, last_a, ly_a)
    d = dw[...]
    for c in range(4):
        cols = slice(c * 512, c * 512 + 512)
        e = dot(h2[...], exp[:, cols]) + vec[8 + c : 9 + c]
        zz, sl = gelu_and_slope(e)
        z[:, cols] = zz.astype(BF)
        slope[:, cols] = sl
        t_red[cols, :] = (dot(zz.astype(BF), d, TN) * inv_root).astype(BF)
    reduce_red.start()
    pump.run()
    reduce_red.sum_pair()
    reduce_red.send_x()
    gather_red.finish()

    ds_ = at.slots(2)
    h2t = h2[...].T
    for c in range(4):
        cols = slice(c * 512, c * 512 + 512)
        de = dot(d, red[cols, :], NT) * slope[:, cols]
        small[8 + c : 9 + c] = colsum(de) * inv_root
        deb[:, cols] = de.astype(BF)
        t_exp[:, cols] = (dot(h2t, de.astype(BF)) * inv_root).astype(BF)
    reduce_exp.start()
    out = from_windows(r1[...] + dot(z[...], red[...]) + vec[7:8])
    frames[0] = out[0:160]
    edges_go[0] = out[160:208].astype(BF)
    at.put(edges_go.at[0], edges_out.at[0], ds_, after)
    reduce_exp.sum_pair()
    dh2 = dot(deb[...], exp[...], NT)
    df = d.astype(F32)
    small[7:8] = colsum(df) * inv_root
    small[5:6] = colsum(dh2 * xhat2[...]) * inv_root
    small[6:7] = colsum(dh2) * inv_root
    dr = df + norm_back(dh2 * (1.0 + vec[5:6]), xhat2[...], rstd2)
    dr1[...] = dr
    small[4:5] = colsum(dr) * inv_root
    drb = dr.astype(BF)
    t_att[:, 1536:2048] = (dot(o[...], drb, TN) * inv_root).astype(BF)
    do[...] = dot(drb, att[:, 1536:2048], NT).astype(BF)
    cut, later = at.zc // 2, at.zc - at.zc // 4
    first, second, third = range(1, cut), range(cut, later), range(later, at.zc)
    for g in range(4):
        sq = sv = None
        for w in range(4):
            a, b = attention_backward(w, g, qkv, do, prob, gpos, dqkv, w == 0)
            sq = a if sq is None else sq + a
            sv = b if sv is None else sv + b
        small[2:3, g * 128 : (g + 1) * 128] = sq * inv_root
        small[3:4, g * 128 : (g + 1) * 128] = sv * inv_root
        if g == 1:
            reduce_red.sum_x(first)
    h1t = h1[...].T
    for c in range(3):
        cols = slice(c * 512, c * 512 + 512)
        t_att[:, cols] = (dot(h1t, dqkv[:, cols]) * inv_root).astype(BF)
    reduce_att.start()
    terms = table_terms(gpos, one_hot, by_head) * inv_root
    small[16:24, 0:256] = terms[0:8]
    small[16:24, 256:512] = terms[8:16]
    small[12:16] = jnp.zeros((4, 512), F32)
    dh1 = None
    for c in range(3):
        cols = slice(c * 512, c * 512 + 512)
        term = dot(dqkv[:, cols], att[:, cols], NT)
        dh1 = term if dh1 is None else dh1 + term
    xhat1, rstd1 = norm(xw[...].astype(F32))
    small[0:1] = colsum(dh1 * xhat1) * inv_root
    small[1:2] = colsum(dh1) * inv_root
    ss = at.slots(4 + at.zc)
    at.put(small.at[:, lanes((1 - at.core) * 256, 256)], small_pair, ss, at.to_core)
    reduce_red.sum_x(second)
    reduce_att.sum_pair()
    reduce_att.send_x()
    reduce_red.sum_x(third)
    at.got(small_pair, ss)
    small_sum[0] = small[:, lanes(at.core * 256, 256)] + small_pair[...]
    at.put(small_sum.at[0], small_y, ss + 1, at.to_y)
    out = from_windows(dr1[...] + norm_back(dh1 * (1.0 + vec[0:1]), xhat1, rstd1))
    frames[1] = out[0:160]
    edges_go[1] = out[160:208].astype(BF)
    at.put(edges_go.at[1], edges_out.at[1], ds_ + 1, after)
    reduce_att.sum_x(first)
    at.got(small_y, ss + 1)
    small_sum[1] = small_sum[0] + small_y[...]
    at.put(small_sum.at[1], small_x, ss + 2, at.to_x)
    reduce_exp.send_x()
    reduce_att.sum_x(second)
    reduce_red.sum_z()
    reduce_att.sum_x(third)
    at.got(small_x, ss + 2)
    small_z[at.z] = small_sum[1] + small_x[...]
    for j in range(1, at.zc):
        at.put(small_z.at[at.z], small_z.at[at.z], ss + 3 + j, at.to_z(j))
    reduce_exp.sum_x(first)
    reduce_red.sum_y()
    reduce_exp.sum_x(second)
    reduce_exp.sum_x(third)
    reduce_att.sum_z()
    for j in range(1, at.zc):
        at.got(small_z.at[(at.z + at.zc - j) % at.zc], ss + 3 + j)
    total = small_z[0]
    for j in range(1, at.zc):
        total = total + small_z[j]
    small_out[:, lanes(at.core * 256, 256)] = total
    half = small_out.at[:, lanes(at.core * 256, 256)]
    at.put(half, half, ss + 3, at.to_core)
    reduce_att.sum_y()
    reduce_exp.sum_z()
    reduce_exp.sum_y()
    for k in range(2):
        at.got(edges_out.at[k], ds_ + k)
    at.got(small_out.at[:, lanes((1 - at.core) * 256, 256)], ss + 3)
    for one in (reduce_red, reduce_exp, reduce_att):
        one.finish()
    at.done()
    assert at.used <= send.shape[0]


def block_step(x, d, regions, relative, table, w_att, w_exp, w_red, vectors, inv_root):
    count = lax.axis_size("shard")
    zc = count // 2
    rows, rows_red = w_att.shape[0], w_red.shape[0]
    sh = jax.ShapeDtypeStruct
    v = pltpu.VMEM
    slots = 3 * (7 * zc) + 3 * (2 * zc + 4) + count + zc + 16
    share_a, share_e, share_r = REDUCE_SHARE
    win_a, win_e, win_r = 1024 - share_a, 1024 - share_e, 256 - share_r
    return pl.pallas_call(
        functools.partial(block_kernel, count, inv_root),
        out_shape=(
            sh((rows, 2048), BF), sh((rows, 2048), BF), sh((rows_red, 512), BF), sh((24, 512), F32),
            sh((2, 160, 512), F32), sh((2, 48, 512), BF),
        ),
        in_specs=[HBM] * 2 + [VM] * 3 + [HBM] * 3 + [VM],
        out_specs=[VM] * 6,
        scratch_shapes=[
            v((512, 2048), BF), v((512, 2048), BF), v((2048, 512), BF),
            v((512, 2048), BF), v((512, 2048), BF), v((2048, 512), BF),
            v((512, 1024), BF), v((512, 1024), BF), v((2048, 256), BF),
            v((512, 1024), BF), v((512, 1024), BF), v((2048, 256), BF),
            v((512, share_e), BF),
            v((zc, rows, win_a), BF), v((zc, rows, win_e), BF), v((zc, rows_red, win_r), BF),
            v((zc - 1, rows, win_a), BF), v((zc - 1, rows, win_e), BF), v((zc - 1, rows_red, win_r), BF),
            v((rows, win_a), BF), v((rows, win_e), BF), v((rows_red, win_r), BF),
            v((rows, win_a), BF), v((rows, win_e), BF), v((rows_red, win_r), BF),
            v((2, SHIFT, 14, 512), BF), v((2, 48, 512), BF),
            v((16, 128), F32), v((count, 16, 128), BF), v((16, 512), F32),
            v((24, 512), F32), v((24, 256), F32), v((2, 24, 256), F32), v((24, 256), F32), v((24, 256), F32),
            v((zc, 24, 256), F32),
            v((14, 16, 512), F32), v((TOK, 512), BF), v((TOK, 512), BF),
            v((16, 128), F32), v((4, PW, TOK), F32), v((16, 256), F32), v((256, PAIRS), BF), v((16, PW, PW), F32),
            v((4, PW, TOK), F32),
            v((TOK, 512), BF), v((TOK, 1536), BF), v((4, 4, PW, TOK), F32), v((TOK, 512), BF), v((TOK, 512), F32),
            v((TOK, 512), F32), v((TOK, 512), BF), v((TOK, 2048), BF), v((TOK, 2048), F32), v((TOK, 2048), BF),
            v((TOK, 512), BF), v((TOK, 1536), BF), v((TOK, 512), F32), v((4, PW, TOK), F32),
            v(x.shape, BF), v(d.shape, BF), v(w_att.shape, F32), v(w_exp.shape, F32), v(w_red.shape, F32),
            pltpu.SemaphoreType.DMA((5,)), pltpu.SemaphoreType.DMA((slots,)), pltpu.SemaphoreType.DMA((slots,)),
        ],
        compiler_params=pltpu.CompilerParams(
            collective_id=0, has_side_effects=True, vmem_limit_bytes=60 * 1024 * 1024
        ),
        name="block_step",
    )(x, d, regions, relative, table, w_att, w_exp, w_red, vectors)


def adamw(weight, grad, first, second, decay):
    first_new = BETA_ONE * first + (1.0 - BETA_ONE) * grad
    second_new = BETA_TWO * second + (1.0 - BETA_TWO) * grad * grad
    corr_one = 1.0 - BETA_ONE**STEP
    corr_two = 1.0 - BETA_TWO**STEP
    step_dir = first_new / corr_one / (jnp.sqrt(second_new / corr_two) + ADAM_EPS)
    return (weight - LEARN_RATE * (step_dir + decay * weight), first_new, second_new)


def finish_kernel(steps, frames, edges, small, *refs):
    grads, state, outs = refs[:3], refs[3:18], refs[18:]
    y, dt, o_grads, o_vec, o_table, new = outs[0], outs[1], outs[2:5], outs[5], outs[6], outs[7:]
    for m in range(3):
        grad = grads[m][...].astype(F32)
        o_grads[m][...] = grad
        new[3 * m][...], new[3 * m + 1][...], new[3 * m + 2][...] = adamw(
            state[3 * m][...], grad, state[3 * m + 1][...], state[3 * m + 2][...], WEIGHT_DECAY
        )

    @pl.when(pl.program_id(0) == 0)
    def _():
        width, table = state[9].shape[1], state[12].shape[1]
        turned = pltpu.roll(small[0:16, :], (512 - lax.axis_index("shard") * width) % 512, 1)
        grad = turned[0:12, 0:width]
        o_vec[...] = grad
        new[9][...], new[10][...], new[11][...] = adamw(state[9][...], grad, state[10][...], state[11][...], 0.0)
        grad = jnp.concatenate([small[16:24, 0:256], small[16:24, 256:512]], axis=0)[:, 0:table]
        o_table[...] = grad
        new[12][...], new[13][...], new[14][...] = adamw(state[12][...], grad, state[13][...], state[14][...], 0.0)
        for k, out in enumerate((y, dt)):
            above = edges[k].astype(F32)
            for b in range(4):
                cols = slice(b * 128, b * 128 + 128)
                out[pl.ds(b, 14 * SHIFT, stride=4), :] = above[0 : 14 * SHIFT, cols]
                out[pl.ds(14 * SHIFT * 4 + b, 14 * (14 - SHIFT), stride=4), :] = frames[
                    k, 0 : 14 * (14 - SHIFT), cols
                ]


def finish(grads, small, frames, edges, state):
    steps = 2 if state[0].shape[0] % 32 == 0 else 1

    def part(a):
        return pl.BlockSpec((a.shape[0] // steps, a.shape[1]), lambda i: (i, 0))

    def whole(a):
        return pl.BlockSpec(a.shape, lambda i: (0,) * len(a.shape))

    sh = jax.ShapeDtypeStruct
    cut = [state[0], state[3], state[6]]
    outs = [sh((784, 128), F32)] * 2 + [sh(a.shape, F32) for a in cut] + [sh(state[9].shape, F32), sh(state[12].shape, F32)]
    outs += [sh(a.shape, F32) for a in state]
    specs = [whole(outs[0])] * 2 + [part(a) for a in cut] + [whole(state[9]), whole(state[12])]
    state_specs = [part(a) for a in state[:9]] + [whole(a) for a in state[9:]]
    return pl.pallas_call(
        functools.partial(finish_kernel, steps),
        grid=(steps,),
        out_shape=outs,
        in_specs=[whole(frames), whole(edges), whole(small)] + [part(a) for a in grads] + state_specs,
        out_specs=specs + state_specs,
        compiler_params=pltpu.CompilerParams(vmem_limit_bytes=60 * 1024 * 1024),
        name="finish",
    )(frames, edges, small, *grads, *state)


def on_device(
    block_input, output_grad, region_ids, relative_index, attention_weight, expand_weight, reduce_weight, vectors,
    bias_table, attention_mean, attention_square, expand_mean, expand_square, reduce_mean, reduce_square,
    vectors_mean, vectors_square, table_mean, table_square,
):
    images, band_rows, columns, features = block_input.shape
    tokens = images * lax.axis_size("shard") * band_rows * lax.axis_size("band") * columns
    relative = jnp.pad(relative_index.T, ((0, 3), (0, PW - WIN * WIN)), constant_values=-1).reshape(1, PAIRS)
    grads = block_step(
        block_input[0], output_grad[0], region_ids, relative, bias_table.T,
        attention_weight, expand_weight, reduce_weight, vectors, 1.0 / math.sqrt(tokens),
    )
    state = (
        attention_weight, attention_mean, attention_square, expand_weight, expand_mean, expand_square,
        reduce_weight, reduce_mean, reduce_square, vectors, vectors_mean, vectors_square,
        bias_table.T, table_mean.T, table_square.T,
    )
    outs = finish(grads[:3], grads[3], grads[4], grads[5], state)
    y, dt, grad_a, grad_e, grad_r, grad_v, grad_t = outs[:7]
    new = outs[7:]
    shape = block_input.shape
    return (
        y.reshape(shape), dt.reshape(shape), grad_a, grad_e, grad_r, grad_v, grad_t.T,
        new[0], new[3], new[6], new[9], new[12].T,
        new[1], new[2], new[4], new[5], new[7], new[8], new[10], new[11], new[13].T, new[14].T,
    )


def solution(mesh):
    return jax.shard_map(
        on_device,
        mesh=mesh,
        in_specs=(
            P("shard", "band", None, None),
            P("shard", "band", None, None),
            P("band", None),
            P(),
            P("shard", None),
            P("shard", None),
            P("shard", None),
            P(None, "shard"),
            P(),
            P("shard", None),
            P("shard", None),
            P("shard", None),
            P("shard", None),
            P("shard", None),
            P("shard", None),
            P(None, "shard"),
            P(None, "shard"),
            P(),
            P(),
        ),
        out_specs=(
            P("shard", "band", None, None),
            P("shard", "band", None, None),
            P("shard", None),
            P("shard", None),
            P("shard", None),
            P(None, "shard"),
            P(),
            P("shard", None),
            P("shard", None),
            P("shard", None),
            P(None, "shard"),
            P(),
            P("shard", None),
            P("shard", None),
            P("shard", None),
            P("shard", None),
            P("shard", None),
            P("shard", None),
            P(None, "shard"),
            P(None, "shard"),
            P(),
            P(),
        ),
        check_vma=False,
    )
```

```python
import functools
import math

import jax
import jax.numpy as jnp
from jax import lax
from jax.experimental import pallas as pl
from jax.experimental.pallas import tpu as pltpu
from jax.sharding import PartitionSpec as P

WIN = 7
SHIFT = 3
STEP = 5
NORM_EPS = 1e-05
LEARN_RATE = 0.02
BETA_ONE = 0.9
BETA_TWO = 0.999
ADAM_EPS = 1e-08
WEIGHT_DECAY = 0.05
MASK_VALUE = -1000000000.0

BF = jnp.bfloat16
F32 = jnp.float32
MESH_ID = pl.DeviceIdType.MESH
VM = pl.BlockSpec(memory_space=pltpu.VMEM)
HBM = pl.BlockSpec(memory_space=pltpu.HBM)
NN = (((1,), (0,)), ((), ()))
NT = (((1,), (1,)), ((), ()))
TN = (((0,), (0,)), ((), ()))

PW = 64
TOK = 4 * PW
PAIRS = 52 * PW
ATT, EXP, RED = 0, 1, 2
GATHER_SHARE = (512, 256, 128)
DEPTH, LAG = 3, (1, 5)
REDUCE_SHARE = (0, 512, 0)


def iota(shape, axis):
    return lax.broadcasted_iota(jnp.int32, shape, axis)


def dot(a, b, dims=NN):
    return lax.dot_general(a, b, dims, preferred_element_type=F32)


def colsum(v):
    return jnp.sum(v, axis=0, keepdims=True)


def norm(v):
    v = v - jnp.mean(v, axis=1, keepdims=True)
    r = lax.rsqrt(jnp.mean(v * v, axis=1, keepdims=True) + NORM_EPS)
    return v * r, r


def norm_back(u, xhat, r):
    return r * (u - jnp.mean(u, axis=1, keepdims=True) - xhat * jnp.mean(u * xhat, axis=1, keepdims=True))


def gelu_and_slope(e):
    a = jnp.abs(e) * (1.0 / math.sqrt(2.0))
    g = jnp.exp(-0.5 * e * e)
    t = 1.0 / (1.0 + 0.3275911 * a)
    poly = t * (0.254829592 + t * (-0.284496736 + t * (1.421413741 + t * (-1.453152027 + t * 1.061405429))))
    half = 0.5 * poly * g
    cdf = jnp.where(e >= 0, 1.0 - half, half)
    return e * cdf, cdf + e * (g * (1.0 / math.sqrt(2.0 * math.pi)))


def head_mask(h):
    lane = iota((PW, 128), 1)
    return (lane >= h * 32) & (lane < h * 32 + 32)


def stack_heads(v):
    zero = jnp.zeros_like(v)
    return jnp.concatenate([jnp.where(head_mask(h), v, zero) for h in range(4)], axis=0)


def pick_heads(r):
    out = jnp.where(head_mask(0), r[0:PW], 0.0)
    for h in range(1, 4):
        out = jnp.where(head_mask(h), r[h * PW : (h + 1) * PW], out)
    return out


def attention_forward(w, g, qkv, allowed, pos, prob, o):
    rows = pl.ds(w * PW, PW)
    q = qkv[rows, g * 128 : (g + 1) * 128]
    k = qkv[rows, 512 + g * 128 : 512 + (g + 1) * 128]
    v = qkv[rows, 1024 + g * 128 : 1024 + (g + 1) * 128]
    s = jnp.where(allowed[w] > 0, dot(k, stack_heads(q), NT) + pos[g], MASK_VALUE)
    e = jnp.exp(s - jnp.max(s, axis=0, keepdims=True))
    p = e * (1.0 / jnp.sum(e, axis=0, keepdims=True))
    prob[w, g] = p
    o[rows, g * 128 : (g + 1) * 128] = pick_heads(dot(p.astype(BF), v, TN)).astype(BF)


def attention_backward(w, g, qkv, do, prob, gpos, dqkv, first):
    rows = pl.ds(w * PW, PW)
    q = qkv[rows, g * 128 : (g + 1) * 128]
    k = qkv[rows, 512 + g * 128 : 512 + (g + 1) * 128]
    v = qkv[rows, 1024 + g * 128 : 1024 + (g + 1) * 128]
    dos = stack_heads(do[rows, g * 128 : (g + 1) * 128])
    p = prob[w, g]
    dp = dot(v, dos, NT)
    ds = p * (dp - jnp.sum(p * dp, axis=0, keepdims=True))
    if first:
        gpos[g] = ds
    else:
        gpos[g] += ds
    dsb = ds.astype(BF)
    dq = pick_heads(dot(dsb, k, TN)) * (1.0 / math.sqrt(32.0))
    dk = dot(dsb, stack_heads(q), NN)
    dv = dot(p.astype(BF), dos, NN)
    dqkv[rows, g * 128 : (g + 1) * 128] = dq.astype(BF)
    dqkv[rows, 512 + g * 128 : 512 + (g + 1) * 128] = dk.astype(BF)
    dqkv[rows, 1024 + g * 128 : 1024 + (g + 1) * 128] = dv.astype(BF)
    return colsum(dq), colsum(dv)


def lanes(start, width):
    return pl.ds(pl.multiple_of(start, 128), width)


class Place:
    def __init__(self, count, send, recv):
        self.count, self.zc = count, count // 2
        self.send, self.recv = send, recv
        self.used, self.started = 0, []
        self.shard, self.band = lax.axis_index("shard"), lax.axis_index("band")
        self.x, self.z = self.shard % 2, self.shard // 2
        self.core, self.y = self.band % 2, self.band // 2
        self.to_x = {"shard": self.shard + 1 - 2 * self.x}
        self.to_core = {"band": self.band + 1 - 2 * self.core}
        self.to_y = {"band": (self.band + 2) % 4}

    def to_z(self, j):
        return {"shard": ((self.z + j) % self.zc) * 2 + self.x}

    def block(self, j, other):
        x = 1 - self.x if other else self.x
        return ((self.z + j) % self.zc) * 2 + x

    def greet(self):
        barrier = pltpu.get_barrier_semaphore()
        places = [self.to_z(j) for j in range(1, self.zc)] + [self.to_x]
        places += [{"band": (self.band + j) % 4} for j in range(1, 4)]
        for where in places:
            pl.semaphore_signal(barrier, inc=1, device_id=where, device_id_type=MESH_ID)
        pl.semaphore_wait(barrier, len(places))

    def slots(self, n):
        first = self.used
        self.used += n
        return first

    def copy(self, src, dst, slot, where):
        return pltpu.make_async_remote_copy(
            src_ref=src, dst_ref=dst, send_sem=self.send.at[slot], recv_sem=self.recv.at[slot],
            device_id=where, device_id_type=MESH_ID,
        )

    def put(self, src, dst, slot, where):
        copy = self.copy(src, dst, slot, where)
        copy.start()
        self.started.append(copy)

    def got(self, dst, slot):
        self.copy(dst, dst, slot, self.to_core).wait_recv()

    def done(self):
        for copy in self.started:
            copy.wait_send()


class Gather:
    def __init__(self, at, ref, rows, width, share):
        self.at, self.ref, self.rows, self.share = at, ref, rows, share
        self.half = width // 2
        self.window = self.half - share
        self.zs, self.xs = at.slots(at.zc - 1), at.slots(at.zc)
        self.ys, self.cs = at.slots(2 * at.zc), at.slots(2 * at.zc)

    def part(self, block, start, width):
        rows = pl.ds(pl.multiple_of(block * self.rows, self.rows), self.rows)
        return self.ref.at[rows, lanes(start, width)]

    def mine(self, block):
        at = self.at
        return self.part(block, at.core * self.half + at.y * self.share, self.window)

    def single(self, block, y):
        return self.part(block, self.at.core * self.half + y * self.window, self.share)

    def send_z(self, j):
        own = self.mine(self.at.shard)
        self.at.put(own, own, self.zs + j - 1, self.at.to_z(j))

    def send_x(self, j):
        part = self.mine(self.at.block(j, 0))
        self.at.put(part, part, self.xs + j, self.at.to_x)

    def over_y(self, j, other):
        if self.share:
            part = self.single(self.at.block(j, other), self.at.y)
            self.at.put(part, part, self.ys + 2 * j + other, self.at.to_y)

    def pass_z(self, j):
        self.at.got(self.mine(self.at.block(j, 0)), self.zs + self.at.zc - j - 1)
        self.send_x(j)
        self.over_y(j, 0)

    def pass_x(self, j):
        self.at.got(self.mine(self.at.block(j, 1)), self.xs + j)
        self.over_y(j, 1)

    def pass_y(self, j, other):
        at = self.at
        block = at.block(j, other)
        if self.share:
            at.got(self.single(block, 1 - at.y), self.ys + 2 * j + other)
        part = self.part(block, at.core * self.half, self.half)
        at.put(part, part, self.cs + 2 * j + other, at.to_core)

    def finish(self):
        at = self.at
        for other in (0, 1):
            for j in range(at.zc):
                if j or other:
                    part = self.part(at.block(j, other), (1 - at.core) * self.half, self.half)
                    at.got(part, self.cs + 2 * j + other)


class Pump:
    def __init__(self, at, gathers):
        near = range(at.zc - 1, 0, -1)
        self.sends = [(one, j) for one in gathers for j in range(1, at.zc)]
        self.events, self.at, self.step, self.marks = [], at, 0, {}
        zs = [(one, j) for one in gathers for j in near]
        xs = [(one, j) for one in gathers for j in [0] + list(near)]
        ys = [(one, j, o) for one in gathers for j, o in [(0, 1)] + [(j, o) for j in near for o in (0, 1)]]
        lag_x, lag_y = LAG
        done_x = done_y = 0
        for k in range(len(zs) + lag_y + 1):
            if k < len(zs):
                self.events.append(("z",) + zs[k])
            want = len(xs) if k >= len(zs) + lag_x - 1 else max(0, (k - lag_x + 1) * at.zc // (at.zc - 1))
            while done_x < min(want, len(xs)):
                self.events.append(("x",) + xs[done_x])
                done_x += 1
            want = len(ys) if k >= len(zs) + lag_y - 1 else max(0, (k - lag_y + 1) * (2 * at.zc - 1) // (at.zc - 1))
            while done_y < min(want, len(ys)):
                self.events.append(("y",) + ys[done_y])
                done_y += 1
        self.next_send = 0
        self.last = {}
        for k, event in enumerate(self.events):
            self.last[event[1]] = k

    def issue(self, n):
        while self.next_send < min(n, len(self.sends)):
            one, j = self.sends[self.next_send]
            one.send_z(j)
            self.next_send += 1

    def begin(self, gathers):
        gathers[0].send_x(0)
        self.issue(DEPTH)
        for one in gathers[1:]:
            one.send_x(0)

    def run(self, upto=None):
        stop = len(self.events) if upto is None else self.last[upto] + 1
        while self.step < stop:
            kind, one, *where = self.events[self.step]
            if kind == "z":
                self.issue(sum(e[0] == "z" for e in self.events[: self.step]) + 1 + DEPTH)
                one.pass_z(*where)
            elif kind == "x":
                one.pass_x(*where)
            else:
                one.pass_y(*where)
            self.step += 1


class Reduce:
    def __init__(self, at, terms, rows, width, share, out, pair, acc, from_y, from_x, from_z, last, last_y):
        self.at, self.terms, self.rows, self.share, self.out = at, terms, rows, share, out
        self.pair, self.acc, self.from_y, self.from_x, self.from_z = pair, acc, from_y, from_x, from_z
        self.last, self.last_y = last, last_y
        self.half = width // 2
        self.window = self.half - share
        self.cs, self.ys, self.xs = at.slots(1), at.slots(1), at.slots(at.zc)
        self.zs, self.ls, self.es = at.slots(at.zc - 1), at.slots(1), at.slots(1)

    def of(self, block):
        return pl.ds(pl.multiple_of(block * self.rows, self.rows), self.rows)

    def start(self):
        at = self.at
        at.put(self.terms.at[:, lanes((1 - at.core) * self.half, self.half)], self.pair, self.cs, at.to_core)

    def sum_pair(self):
        at = self.at
        at.got(self.pair, self.cs)
        mine = lanes(at.core * self.half, self.half)

        def step(b, carry):
            rows = self.of(b)
            self.acc[rows, :] = (self.terms[rows, mine].astype(F32) + self.pair[rows, :].astype(F32)).astype(BF)
            return carry

        lax.fori_loop(0, at.count, step, 0)
        if self.share:
            at.put(self.acc.at[:, lanes((1 - at.y) * self.window, self.share)], self.from_y, self.ys, at.to_y)

    def send_x(self):
        at = self.at
        if self.share:
            at.got(self.from_y, self.ys)
            single = lanes(at.y * self.window, self.share)

            def step(b, carry):
                rows = self.of(b)
                self.acc[rows, single] = (
                    self.acc[rows, single].astype(F32) + self.from_y[rows, :].astype(F32)
                ).astype(BF)
                return carry

            lax.fori_loop(0, at.count, step, 0)
        window = lanes(at.y * self.share, self.window)
        for j in list(range(1, at.zc)) + [0]:
            at.put(self.acc.at[self.of(at.block(j, 1)), window], self.from_x.at[j], self.xs + j, at.to_x)

    def sum_x(self, some=None):
        at = self.at
        window = lanes(at.y * self.share, self.window)
        for j in range(1, at.zc) if some is None else some:
            at.got(self.from_x.at[j], self.xs + j)
            rows = self.of(at.block(j, 0))
            self.acc[rows, window] = (self.acc[rows, window].astype(F32) + self.from_x[j].astype(F32)).astype(BF)
            at.put(self.acc.at[rows, window], self.from_z.at[j - 1], self.zs + j - 1, at.to_z(j))

    def sum_z(self):
        at = self.at
        window = lanes(at.y * self.share, self.window)
        at.got(self.from_x.at[0], self.xs)
        total = self.acc[self.of(at.shard), window].astype(F32) + self.from_x[0].astype(F32)
        for j in range(1, at.zc):
            at.got(self.from_z.at[j - 1], self.zs + j - 1)
            total = total + self.from_z[j - 1].astype(F32)
        self.last[...] = total.astype(BF)
        at.put(self.last, self.last_y, self.ls, at.to_y)

    def sum_y(self):
        at, share, both = self.at, self.share, self.half - 2 * self.share
        at.got(self.last_y, self.ls)
        base = at.core * self.half
        if share:
            self.out[:, lanes(base + at.y * self.window, share)] = self.last[:, lanes(at.y * both, share)]
            self.out[:, lanes(base + (1 - at.y) * self.window, share)] = self.last_y[:, lanes((1 - at.y) * both, share)]
        if both:
            here, there = lanes((1 - at.y) * share, both), lanes(at.y * share, both)
            self.out[:, lanes(base + share, both)] = (
                self.last[:, here].astype(F32) + self.last_y[:, there].astype(F32)
            ).astype(BF)
        part = self.out.at[:, lanes(base, self.half)]
        at.put(part, part, self.es, at.to_core)

    def finish(self):
        at = self.at
        at.got(self.out.at[:, lanes((1 - at.core) * self.half, self.half)], self.es)


def divide(v, by, most):
    shift = 16
    factor = -(-(1 << shift) // by)
    return (v * factor) >> shift


def window_place(t):
    w, p = t >> 6, t & 63
    i = divide(p, WIN, 64)
    row = (w >> 1) * WIN + i
    col = (w & 1) * WIN + p - i * WIN
    return row, col, p < WIN * WIN


def prepare_masks(regions, padded, allowed):
    padded[...] = jnp.zeros_like(padded)
    padded[0:14, 0:14] = regions[...].astype(F32)
    region = padded[...].astype(BF)
    row, col, real = window_place(iota((TOK, 16), 0))
    pick = ((iota((TOK, 16), 1) == row) & real).astype(F32).astype(BF)
    row, col, real = window_place(iota((TOK, 128), 0))
    by_key = jnp.sum(jnp.where(iota((TOK, 128), 1) == col, dot(pick, region), 0.0), axis=1, keepdims=True)
    row, col, real = window_place(iota((TOK, 1), 0))
    by_key = jnp.where(real, by_key, -1.0)
    for w in range(4):
        row, col, real = window_place(w * PW + (iota((128, TOK), 1) & 63))
        pick = (iota((128, TOK), 0) == col).astype(F32).astype(BF)
        row, col, real = window_place(w * PW + (iota((16, TOK), 1) & 63))
        by_query = colsum(jnp.where(iota((16, TOK), 0) == row, dot(region, pick), 0.0))
        row, col, real = window_place(w * PW + (iota((1, TOK), 1) & 63))
        by_query = jnp.where(real, by_query, -2.0)
        allowed[w] = (by_key[w * PW : (w + 1) * PW] == by_query).astype(F32)


def prepare_bias(relative, square, flat, table, padded, one_hot, by_head, pos):
    square[...] = jnp.full(square.shape, -1.0, F32)
    square[0 : WIN * WIN, 0 : WIN * WIN] = relative[...].astype(F32)
    turned = square[...].T
    for j in range(PAIRS // PW):
        flat[0:1, j * PW : (j + 1) * PW] = turned[j : j + 1, 0:PW]
    one_hot[...] = (iota((256, PAIRS), 0) == flat[...].astype(jnp.int32)).astype(F32).astype(BF)
    padded[...] = jnp.zeros_like(padded)
    padded[:, 0 : table.shape[1]] = table[...]
    left = padded[...]
    total = None
    for _ in range(3):
        part = left.astype(BF)
        left = left - part.astype(F32)
        term = dot(part, one_hot[...])
        total = term if total is None else total + term
    for j in range(WIN * WIN):
        by_head[:, j, :] = total[:, j * PW : (j + 1) * PW]
    for g in range(4):
        pos[g] = jnp.concatenate([by_head[4 * g + h] for h in range(4)], axis=1)


def table_terms(gpos, one_hot, by_head):
    for g in range(4):
        for h in range(4):
            by_head[4 * g + h] = gpos[g][:, h * PW : (h + 1) * PW]
    flat = jnp.concatenate([by_head[:, j, :] for j in range(52)], axis=1)
    high = flat.astype(BF)
    low = (flat - high.astype(F32)).astype(BF)
    return dot(high, one_hot[...], NT) + dot(low, one_hot[...], NT)


def to_windows(frame, own, edge, which, out):
    for r in range(14):
        row = own[r + SHIFT] if r + SHIFT < 14 else edge[which, r + SHIFT - 14]
        frame[r, 0:14, :] = row.astype(F32)
    row, col, real = window_place(iota((TOK, 224), 0))
    col = col + SHIFT
    col = jnp.where(col >= 14, col - 14, col)
    pick = ((iota((TOK, 224), 1) == row * 16 + col) & real).astype(F32).astype(BF)
    out[...] = dot(pick, frame[...].reshape(224, frame.shape[2]).astype(BF)).astype(BF)


def from_windows(values):
    t = iota((208, TOK), 0)
    t = jnp.where(t >= 160, t - 6, t)
    row = divide(t, 14, 256)
    col = t - row * 14 + 14 - SHIFT
    col = jnp.where(col >= 14, col - 14, col)
    right = (col >= WIN).astype(jnp.int32)
    below = (row >= WIN).astype(jnp.int32)
    place = (2 * below + right) * PW + (row - below * WIN) * WIN + col - right * WIN
    pick = (iota((208, TOK), 1) == place).astype(F32).astype(BF)
    high = values.astype(BF)
    low = (values - high.astype(F32)).astype(BF)
    return dot(pick, high) + dot(pick, low)


def block_kernel(
    count, inv_root, x_hbm, d_hbm, regions, relative, table, a_hbm, e_hbm, r_hbm, vectors,
    g_att, g_exp, g_red, small_out, frames, edges_out,
    att, exp, red, t_att, t_exp, t_red,
    pair_a, pair_e, pair_r, acc_a, acc_e, acc_r, fy_e, fx_a, fx_e, fx_r, fz_a, fz_e, fz_r,
    last_a, last_e, last_r, ly_a, ly_e, ly_r,
    edges_in, edges_go, vec_own, vec_all, vec,
    small, small_pair, small_sum, small_y, small_x, small_z,
    frame, xw, dw, region_pad, allowed, square, flat, table_pad, one_hot, by_head, pos,
    h1, qkv, prob, o, r1, xhat2, h2, z, slope, deb, do, dqkv, dr1, gpos,
    x_in, d_in, w_att, w_exp, w_red, loads, send, recv,
):
    at = Place(count, send, recv)
    fetch = [
        pltpu.make_async_copy(source, place, loads.at[k])
        for k, (source, place) in enumerate(
            ((x_hbm, x_in), (d_hbm, d_in), (a_hbm, w_att), (e_hbm, w_exp), (r_hbm, w_red))
        )
    ]
    for copy in fetch:
        copy.start()
    at.greet()
    for copy in fetch:
        copy.wait()
    rows, rows_red = w_att.shape[0], w_red.shape[0]
    es = at.slots(2)
    before, after = {"band": (at.band + 3) % 4}, {"band": (at.band + 1) % 4}
    for k, source in enumerate((x_in, d_in)):
        at.put(source.at[0:SHIFT], edges_in.at[k], es + k, before)
    width = vectors.shape[1]
    vec_own[...] = jnp.zeros_like(vec_own)
    vec_own[0:12, 0:width] = vectors[...]
    vec_all[at.shard] = vec_own[...].astype(BF)
    vs = at.slots(count - 1)
    order = [(j, 0) for j in range(1, at.zc)] + [(j, 1) for j in range(at.zc)]
    for i, (j, other) in enumerate(order):
        if other:
            continue
        at.put(vec_all.at[at.shard], vec_all.at[at.shard], vs + i, at.to_z(j))
    at.put(vec_all.at[at.shard], vec_all.at[at.shard], vs + at.zc - 1, at.to_x)
    gathers = [
        Gather(at, ref, n, ref.shape[1], share)
        for ref, n, share in zip((att, exp, red), (rows, rows, rows_red), GATHER_SHARE)
    ]
    for ref, shard, n, one in zip((att, exp, red), (w_att, w_exp, w_red), (rows, rows, rows_red), gathers):
        ref[pl.ds(pl.multiple_of(at.shard * n, n), n), :] = shard[...].astype(BF)
    pump = Pump(at, gathers)
    pump.begin(gathers)
    for j in range(at.zc - 1, 0, -1):
        place = vec_all.at[at.block(j, 0)]
        at.got(place, vs + at.zc - j - 1)
        at.put(place, place, vs + at.zc - 1 + j, at.to_x)
    prepare_masks(regions, region_pad, allowed)
    prepare_bias(relative, square, flat, table, table_pad, one_hot, by_head, pos)
    gather_att, gather_exp, gather_red = gathers
    pump.run(gather_att)
    frame[...] = jnp.zeros_like(frame)
    for k, (source, windows) in enumerate(((x_in, xw), (d_in, dw))):
        at.got(edges_in.at[k], es + k)
        to_windows(frame, source, edges_in, k, windows)
    for j in range(at.zc):
        at.got(vec_all.at[at.block(j, 1)], vs + at.zc - 1 + j)
    total = None
    for b in range(count):
        place = (iota((128, 512), 1) == b * width + iota((128, 512), 0)) & (iota((128, 512), 0) < width)
        term = dot(vec_all[b], place.astype(F32).astype(BF))
        total = term if total is None else total + term
    vec[...] = total
    gather_att.finish()

    x = xw[...].astype(F32)
    xhat1, rstd1 = norm(x)
    h1[...] = (xhat1 * (1.0 + vec[0:1]) + vec[1:2]).astype(BF)
    hb = h1[...]
    qkv[:, 0:512] = ((dot(hb, att[:, 0:512]) + vec[2:3]) * (1.0 / math.sqrt(32.0))).astype(BF)
    qkv[:, 512:1024] = dot(hb, att[:, 512:1024]).astype(BF)
    qkv[:, 1024:1536] = (dot(hb, att[:, 1024:1536]) + vec[3:4]).astype(BF)
    pump.run(gather_exp)
    for w in range(4):
        for g in range(4):
            attention_forward(w, g, qkv, allowed, pos, prob, o)
    r1[...] = x + dot(o[...], att[:, 1536:2048]) + vec[4:5]
    xh2, rstd2 = norm(r1[...])
    xhat2[...] = xh2
    h2[...] = (xh2 * (1.0 + vec[5:6]) + vec[6:7]).astype(BF)
    gather_exp.finish()
    reduce_red = Reduce(
        at, t_red, rows_red, 512, REDUCE_SHARE[RED], g_red, pair_r, acc_r, None, fx_r, fz_r, last_r, ly_r
    )
    reduce_exp = Reduce(
        at, t_exp, rows, 2048, REDUCE_SHARE[EXP], g_exp, pair_e, acc_e, fy_e, fx_e, fz_e, last_e, ly_e
    )
    reduce_att = Reduce(at, t_att, rows, 2048, REDUCE_SHARE[ATT], g_att, pair_a, acc_a, None, fx_a, fz_a, last_a, ly_a)
    d = dw[...]
    for c in range(4):
        cols = slice(c * 512, c * 512 + 512)
        e = dot(h2[...], exp[:, cols]) + vec[8 + c : 9 + c]
        zz, sl = gelu_and_slope(e)
        z[:, cols] = zz.astype(BF)
        slope[:, cols] = sl
        t_red[cols, :] = (dot(zz.astype(BF), d, TN) * inv_root).astype(BF)
    reduce_red.start()
    pump.run()
    reduce_red.sum_pair()
    reduce_red.send_x()
    gather_red.finish()

    ds_ = at.slots(2)
    h2t = h2[...].T
    for c in range(4):
        cols = slice(c * 512, c * 512 + 512)
        de = dot(d, red[cols, :], NT) * slope[:, cols]
        small[8 + c : 9 + c] = colsum(de) * inv_root
        deb[:, cols] = de.astype(BF)
        t_exp[:, cols] = (dot(h2t, de.astype(BF)) * inv_root).astype(BF)
    reduce_exp.start()
    out = from_windows(r1[...] + dot(z[...], red[...]) + vec[7:8])
    frames[0] = out[0:160]
    edges_go[0] = out[160:208].astype(BF)
    at.put(edges_go.at[0], edges_out.at[0], ds_, after)
    reduce_exp.sum_pair()
    dh2 = dot(deb[...], exp[...], NT)
    df = d.astype(F32)
    small[7:8] = colsum(df) * inv_root
    small[5:6] = colsum(dh2 * xhat2[...]) * inv_root
    small[6:7] = colsum(dh2) * inv_root
    dr = df + norm_back(dh2 * (1.0 + vec[5:6]), xhat2[...], rstd2)
    dr1[...] = dr
    small[4:5] = colsum(dr) * inv_root
    drb = dr.astype(BF)
    t_att[:, 1536:2048] = (dot(o[...], drb, TN) * inv_root).astype(BF)
    do[...] = dot(drb, att[:, 1536:2048], NT).astype(BF)
    cut, later = at.zc // 2, at.zc - at.zc // 4
    first, second, third = range(1, cut), range(cut, later), range(later, at.zc)
    for g in range(4):
        sq = sv = None
        for w in range(4):
            a, b = attention_backward(w, g, qkv, do, prob, gpos, dqkv, w == 0)
            sq = a if sq is None else sq + a
            sv = b if sv is None else sv + b
        small[2:3, g * 128 : (g + 1) * 128] = sq * inv_root
        small[3:4, g * 128 : (g + 1) * 128] = sv * inv_root
        if g == 1:
            reduce_red.sum_x(first)
    h1t = h1[...].T
    for c in range(3):
        cols = slice(c * 512, c * 512 + 512)
        t_att[:, cols] = (dot(h1t, dqkv[:, cols]) * inv_root).astype(BF)
    reduce_att.start()
    terms = table_terms(gpos, one_hot, by_head) * inv_root
    small[16:24, 0:256] = terms[0:8]
    small[16:24, 256:512] = terms[8:16]
    small[12:16] = jnp.zeros((4, 512), F32)
    dh1 = None
    for c in range(3):
        cols = slice(c * 512, c * 512 + 512)
        term = dot(dqkv[:, cols], att[:, cols], NT)
        dh1 = term if dh1 is None else dh1 + term
    xhat1, rstd1 = norm(xw[...].astype(F32))
    small[0:1] = colsum(dh1 * xhat1) * inv_root
    small[1:2] = colsum(dh1) * inv_root
    ss = at.slots(4 + at.zc)
    at.put(small.at[:, lanes((1 - at.core) * 256, 256)], small_pair, ss, at.to_core)
    reduce_red.sum_x(second)
    reduce_att.sum_pair()
    reduce_att.send_x()
    reduce_red.sum_x(third)
    at.got(small_pair, ss)
    small_sum[0] = small[:, lanes(at.core * 256, 256)] + small_pair[...]
    at.put(small_sum.at[0], small_y, ss + 1, at.to_y)
    out = from_windows(dr1[...] + norm_back(dh1 * (1.0 + vec[0:1]), xhat1, rstd1))
    frames[1] = out[0:160]
    edges_go[1] = out[160:208].astype(BF)
    at.put(edges_go.at[1], edges_out.at[1], ds_ + 1, after)
    reduce_att.sum_x(first)
    at.got(small_y, ss + 1)
    small_sum[1] = small_sum[0] + small_y[...]
    at.put(small_sum.at[1], small_x, ss + 2, at.to_x)
    reduce_exp.send_x()
    reduce_att.sum_x(second)
    reduce_red.sum_z()
    reduce_att.sum_x(third)
    at.got(small_x, ss + 2)
    small_z[at.z] = small_sum[1] + small_x[...]
    for j in range(1, at.zc):
        at.put(small_z.at[at.z], small_z.at[at.z], ss + 3 + j, at.to_z(j))
    reduce_exp.sum_x(first)
    reduce_red.sum_y()
    reduce_exp.sum_x(second)
    reduce_exp.sum_x(third)
    reduce_att.sum_z()
    reduce_exp.sum_z()
    for j in range(1, at.zc):
        at.got(small_z.at[(at.z + at.zc - j) % at.zc], ss + 3 + j)
    total = small_z[0]
    for j in range(1, at.zc):
        total = total + small_z[j]
    small_out[:, lanes(at.core * 256, 256)] = total
    half = small_out.at[:, lanes(at.core * 256, 256)]
    at.put(half, half, ss + 3, at.to_core)
    reduce_att.sum_y()
    reduce_exp.sum_y()
    for k in range(2):
        at.got(edges_out.at[k], ds_ + k)
    at.got(small_out.at[:, lanes((1 - at.core) * 256, 256)], ss + 3)
    for one in (reduce_red, reduce_exp, reduce_att):
        one.finish()
    at.done()
    assert at.used <= send.shape[0]


def block_step(x, d, regions, relative, table, w_att, w_exp, w_red, vectors, inv_root):
    count = lax.axis_size("shard")
    zc = count // 2
    rows, rows_red = w_att.shape[0], w_red.shape[0]
    sh = jax.ShapeDtypeStruct
    v = pltpu.VMEM
    slots = 3 * (7 * zc) + 3 * (2 * zc + 4) + count + zc + 16
    share_a, share_e, share_r = REDUCE_SHARE
    win_a, win_e, win_r = 1024 - share_a, 1024 - share_e, 256 - share_r
    return pl.pallas_call(
        functools.partial(block_kernel, count, inv_root),
        out_shape=(
            sh((rows, 2048), BF), sh((rows, 2048), BF), sh((rows_red, 512), BF), sh((24, 512), F32),
            sh((2, 160, 512), F32), sh((2, 48, 512), BF),
        ),
        in_specs=[HBM] * 2 + [VM] * 3 + [HBM] * 3 + [VM],
        out_specs=[VM] * 6,
        scratch_shapes=[
            v((512, 2048), BF), v((512, 2048), BF), v((2048, 512), BF),
            v((512, 2048), BF), v((512, 2048), BF), v((2048, 512), BF),
            v((512, 1024), BF), v((512, 1024), BF), v((2048, 256), BF),
            v((512, 1024), BF), v((512, 1024), BF), v((2048, 256), BF),
            v((512, share_e), BF),
            v((zc, rows, win_a), BF), v((zc, rows, win_e), BF), v((zc, rows_red, win_r), BF),
            v((zc - 1, rows, win_a), BF), v((zc - 1, rows, win_e), BF), v((zc - 1, rows_red, win_r), BF),
            v((rows, win_a), BF), v((rows, win_e), BF), v((rows_red, win_r), BF),
            v((rows, win_a), BF), v((rows, win_e), BF), v((rows_red, win_r), BF),
            v((2, SHIFT, 14, 512), BF), v((2, 48, 512), BF),
            v((16, 128), F32), v((count, 16, 128), BF), v((16, 512), F32),
            v((24, 512), F32), v((24, 256), F32), v((2, 24, 256), F32), v((24, 256), F32), v((24, 256), F32),
            v((zc, 24, 256), F32),
            v((14, 16, 512), F32), v((TOK, 512), BF), v((TOK, 512), BF),
            v((16, 128), F32), v((4, PW, TOK), F32), v((128, 128), F32), v((1, PAIRS), F32), v((16, 256), F32), v((256, PAIRS), BF), v((16, PW, PW), F32),
            v((4, PW, TOK), F32),
            v((TOK, 512), BF), v((TOK, 1536), BF), v((4, 4, PW, TOK), F32), v((TOK, 512), BF), v((TOK, 512), F32),
            v((TOK, 512), F32), v((TOK, 512), BF), v((TOK, 2048), BF), v((TOK, 2048), F32), v((TOK, 2048), BF),
            v((TOK, 512), BF), v((TOK, 1536), BF), v((TOK, 512), F32), v((4, PW, TOK), F32),
            v(x.shape, BF), v(d.shape, BF), v(w_att.shape, F32), v(w_exp.shape, F32), v(w_red.shape, F32),
            pltpu.SemaphoreType.DMA((5,)), pltpu.SemaphoreType.DMA((slots,)), pltpu.SemaphoreType.DMA((slots,)),
        ],
        compiler_params=pltpu.CompilerParams(
            collective_id=0, has_side_effects=True, vmem_limit_bytes=60 * 1024 * 1024
        ),
        name="block_step",
    )(x, d, regions, relative, table, w_att, w_exp, w_red, vectors)


def adamw(weight, grad, first, second, decay):
    first_new = BETA_ONE * first + (1.0 - BETA_ONE) * grad
    second_new = BETA_TWO * second + (1.0 - BETA_TWO) * grad * grad
    corr_one = 1.0 - BETA_ONE**STEP
    corr_two = 1.0 - BETA_TWO**STEP
    step_dir = first_new / corr_one / (jnp.sqrt(second_new / corr_two) + ADAM_EPS)
    return (weight - LEARN_RATE * (step_dir + decay * weight), first_new, second_new)


def finish_kernel(steps, frames, edges, small, *refs):
    grads, state, outs = refs[:3], refs[3:18], refs[18:]
    y, dt, o_grads, o_vec, o_table, new = outs[0], outs[1], outs[2:5], outs[5], outs[6], outs[7:]
    for m in range(3):
        grad = grads[m][...].astype(F32)
        o_grads[m][...] = grad
        new[3 * m][...], new[3 * m + 1][...], new[3 * m + 2][...] = adamw(
            state[3 * m][...], grad, state[3 * m + 1][...], state[3 * m + 2][...], WEIGHT_DECAY
        )

    @pl.when(pl.program_id(0) == 0)
    def _():
        width, table = state[9].shape[1], state[12].shape[1]
        turned = pltpu.roll(small[0:16, :], (512 - lax.axis_index("shard") * width) % 512, 1)
        grad = turned[0:12, 0:width]
        o_vec[...] = grad
        new[9][...], new[10][...], new[11][...] = adamw(state[9][...], grad, state[10][...], state[11][...], 0.0)
        grad = jnp.concatenate([small[16:24, 0:256], small[16:24, 256:512]], axis=0)[:, 0:table]
        o_table[...] = grad
        new[12][...], new[13][...], new[14][...] = adamw(state[12][...], grad, state[13][...], state[14][...], 0.0)
        for k, out in enumerate((y, dt)):
            above = edges[k].astype(F32)
            for b in range(4):
                cols = slice(b * 128, b * 128 + 128)
                out[pl.ds(b, 14 * SHIFT, stride=4), :] = above[0 : 14 * SHIFT, cols]
                out[pl.ds(14 * SHIFT * 4 + b, 14 * (14 - SHIFT), stride=4), :] = frames[
                    k, 0 : 14 * (14 - SHIFT), cols
                ]


def finish(grads, small, frames, edges, state):
    steps = 2 if state[0].shape[0] % 32 == 0 else 1

    def part(a):
        return pl.BlockSpec((a.shape[0] // steps, a.shape[1]), lambda i: (i, 0))

    def whole(a):
        return pl.BlockSpec(a.shape, lambda i: (0,) * len(a.shape))

    sh = jax.ShapeDtypeStruct
    cut = [state[0], state[3], state[6]]
    outs = [sh((784, 128), F32)] * 2 + [sh(a.shape, F32) for a in cut] + [sh(state[9].shape, F32), sh(state[12].shape, F32)]
    outs += [sh(a.shape, F32) for a in state]
    specs = [whole(outs[0])] * 2 + [part(a) for a in cut] + [whole(state[9]), whole(state[12])]
    state_specs = [part(a) for a in state[:9]] + [whole(a) for a in state[9:]]
    return pl.pallas_call(
        functools.partial(finish_kernel, steps),
        grid=(steps,),
        out_shape=outs,
        in_specs=[whole(frames), whole(edges), whole(small)] + [part(a) for a in grads] + state_specs,
        out_specs=specs + state_specs,
        compiler_params=pltpu.CompilerParams(vmem_limit_bytes=60 * 1024 * 1024),
        name="finish",
    )(frames, edges, small, *grads, *state)


def on_device(
    block_input, output_grad, region_ids, relative_index, attention_weight, expand_weight, reduce_weight, vectors,
    bias_table, attention_mean, attention_square, expand_mean, expand_square, reduce_mean, reduce_square,
    vectors_mean, vectors_square, table_mean, table_square,
):
    images, band_rows, columns, features = block_input.shape
    tokens = images * lax.axis_size("shard") * band_rows * lax.axis_size("band") * columns
    grads = block_step(
        block_input[0], output_grad[0], region_ids, relative_index, bias_table.T,
        attention_weight, expand_weight, reduce_weight, vectors, 1.0 / math.sqrt(tokens),
    )
    state = (
        attention_weight, attention_mean, attention_square, expand_weight, expand_mean, expand_square,
        reduce_weight, reduce_mean, reduce_square, vectors, vectors_mean, vectors_square,
        bias_table.T, table_mean.T, table_square.T,
    )
    outs = finish(grads[:3], grads[3], grads[4], grads[5], state)
    y, dt, grad_a, grad_e, grad_r, grad_v, grad_t = outs[:7]
    new = outs[7:]
    shape = block_input.shape
    return (
        y.reshape(shape), dt.reshape(shape), grad_a, grad_e, grad_r, grad_v, grad_t.T,
        new[0], new[3], new[6], new[9], new[12].T,
        new[1], new[2], new[4], new[5], new[7], new[8], new[10], new[11], new[13].T, new[14].T,
    )


def solution(mesh):
    return jax.shard_map(
        on_device,
        mesh=mesh,
        in_specs=(
            P("shard", "band", None, None),
            P("shard", "band", None, None),
            P("band", None),
            P(),
            P("shard", None),
            P("shard", None),
            P("shard", None),
            P(None, "shard"),
            P(),
            P("shard", None),
            P("shard", None),
            P("shard", None),
            P("shard", None),
            P("shard", None),
            P("shard", None),
            P(None, "shard"),
            P(None, "shard"),
            P(),
            P(),
        ),
        out_specs=(
            P("shard", "band", None, None),
            P("shard", "band", None, None),
            P("shard", None),
            P("shard", None),
            P("shard", None),
            P(None, "shard"),
            P(),
            P("shard", None),
            P("shard", None),
            P("shard", None),
            P(None, "shard"),
            P(),
            P("shard", None),
            P("shard", None),
            P("shard", None),
            P("shard", None),
            P("shard", None),
            P("shard", None),
            P(None, "shard"),
            P(None, "shard"),
            P(),
            P(),
        ),
        check_vma=False,
    )
```

```python
import functools
import math

import jax
import jax.numpy as jnp
from jax import lax
from jax.experimental import pallas as pl
from jax.experimental.pallas import tpu as pltpu
from jax.sharding import PartitionSpec as P

WIN = 7
SHIFT = 3
STEP = 5
NORM_EPS = 1e-05
LEARN_RATE = 0.02
BETA_ONE = 0.9
BETA_TWO = 0.999
ADAM_EPS = 1e-08
WEIGHT_DECAY = 0.05
MASK_VALUE = -1000000000.0

BF = jnp.bfloat16
F32 = jnp.float32
MESH_ID = pl.DeviceIdType.MESH
VM = pl.BlockSpec(memory_space=pltpu.VMEM)
HBM = pl.BlockSpec(memory_space=pltpu.HBM)
NN = (((1,), (0,)), ((), ()))
NT = (((1,), (1,)), ((), ()))
TN = (((0,), (0,)), ((), ()))

PW = 64
TOK = 4 * PW
PAIRS = 52 * PW
ATT, EXP, RED = 0, 1, 2
GATHER_SHARE = (512, 256, 128)
DEPTH, LAG = 3, (1, 5)
REDUCE_SHARE = (0, 512, 0)


def iota(shape, axis):
    return lax.broadcasted_iota(jnp.int32, shape, axis)


def dot(a, b, dims=NN):
    return lax.dot_general(a, b, dims, preferred_element_type=F32)


def colsum(v):
    return jnp.sum(v, axis=0, keepdims=True)


def norm(v):
    v = v - jnp.mean(v, axis=1, keepdims=True)
    r = lax.rsqrt(jnp.mean(v * v, axis=1, keepdims=True) + NORM_EPS)
    return v * r, r


def norm_back(u, xhat, r):
    return r * (u - jnp.mean(u, axis=1, keepdims=True) - xhat * jnp.mean(u * xhat, axis=1, keepdims=True))


def gelu_and_slope(e):
    a = jnp.abs(e) * (1.0 / math.sqrt(2.0))
    g = jnp.exp(-0.5 * e * e)
    t = 1.0 / (1.0 + 0.3275911 * a)
    poly = t * (0.254829592 + t * (-0.284496736 + t * (1.421413741 + t * (-1.453152027 + t * 1.061405429))))
    half = 0.5 * poly * g
    cdf = jnp.where(e >= 0, 1.0 - half, half)
    return e * cdf, cdf + e * (g * (1.0 / math.sqrt(2.0 * math.pi)))


def head_mask(h):
    lane = iota((PW, 128), 1)
    return (lane >= h * 32) & (lane < h * 32 + 32)


def stack_heads(v):
    zero = jnp.zeros_like(v)
    return jnp.concatenate([jnp.where(head_mask(h), v, zero) for h in range(4)], axis=0)


def pick_heads(r):
    out = jnp.where(head_mask(0), r[0:PW], 0.0)
    for h in range(1, 4):
        out = jnp.where(head_mask(h), r[h * PW : (h + 1) * PW], out)
    return out


def attention_forward(w, g, qkv, allowed, pos, prob, o):
    rows = pl.ds(w * PW, PW)
    q = qkv[rows, g * 128 : (g + 1) * 128]
    k = qkv[rows, 512 + g * 128 : 512 + (g + 1) * 128]
    v = qkv[rows, 1024 + g * 128 : 1024 + (g + 1) * 128]
    s = jnp.where(allowed[w] > 0, dot(k, stack_heads(q), NT) + pos[g], MASK_VALUE)
    e = jnp.exp(s - jnp.max(s, axis=0, keepdims=True))
    p = e * (1.0 / jnp.sum(e, axis=0, keepdims=True))
    prob[w, g] = p
    o[rows, g * 128 : (g + 1) * 128] = pick_heads(dot(p.astype(BF), v, TN)).astype(BF)


def attention_backward(w, g, qkv, do, prob, gpos, dqkv, first):
    rows = pl.ds(w * PW, PW)
    q = qkv[rows, g * 128 : (g + 1) * 128]
    k = qkv[rows, 512 + g * 128 : 512 + (g + 1) * 128]
    v = qkv[rows, 1024 + g * 128 : 1024 + (g + 1) * 128]
    dos = stack_heads(do[rows, g * 128 : (g + 1) * 128])
    p = prob[w, g]
    dp = dot(v, dos, NT)
    ds = p * (dp - jnp.sum(p * dp, axis=0, keepdims=True))
    if first:
        gpos[g] = ds
    else:
        gpos[g] += ds
    dsb = ds.astype(BF)
    dq = pick_heads(dot(dsb, k, TN)) * (1.0 / math.sqrt(32.0))
    dk = dot(dsb, stack_heads(q), NN)
    dv = dot(p.astype(BF), dos, NN)
    dqkv[rows, g * 128 : (g + 1) * 128] = dq.astype(BF)
    dqkv[rows, 512 + g * 128 : 512 + (g + 1) * 128] = dk.astype(BF)
    dqkv[rows, 1024 + g * 128 : 1024 + (g + 1) * 128] = dv.astype(BF)
    return colsum(dq), colsum(dv)


def lanes(start, width):
    return pl.ds(pl.multiple_of(start, 128), width)


class Place:
    def __init__(self, count, send, recv):
        self.count, self.zc = count, count // 2
        self.send, self.recv = send, recv
        self.used, self.started = 0, []
        self.shard, self.band = lax.axis_index("shard"), lax.axis_index("band")
        self.x, self.z = self.shard % 2, self.shard // 2
        self.core, self.y = self.band % 2, self.band // 2
        self.to_x = {"shard": self.shard + 1 - 2 * self.x}
        self.to_core = {"band": self.band + 1 - 2 * self.core}
        self.to_y = {"band": (self.band + 2) % 4}

    def to_z(self, j):
        return {"shard": ((self.z + j) % self.zc) * 2 + self.x}

    def block(self, j, other):
        x = 1 - self.x if other else self.x
        return ((self.z + j) % self.zc) * 2 + x

    def greet(self):
        barrier = pltpu.get_barrier_semaphore()
        places = [self.to_z(j) for j in range(1, self.zc)] + [self.to_x]
        places += [{"band": (self.band + j) % 4} for j in range(1, 4)]
        for where in places:
            pl.semaphore_signal(barrier, inc=1, device_id=where, device_id_type=MESH_ID)
        pl.semaphore_wait(barrier, len(places))

    def slots(self, n):
        first = self.used
        self.used += n
        return first

    def copy(self, src, dst, slot, where):
        return pltpu.make_async_remote_copy(
            src_ref=src, dst_ref=dst, send_sem=self.send.at[slot], recv_sem=self.recv.at[slot],
            device_id=where, device_id_type=MESH_ID,
        )

    def put(self, src, dst, slot, where):
        copy = self.copy(src, dst, slot, where)
        copy.start()
        self.started.append(copy)

    def got(self, dst, slot):
        self.copy(dst, dst, slot, self.to_core).wait_recv()

    def done(self):
        for copy in self.started:
            copy.wait_send()


class Gather:
    def __init__(self, at, ref, rows, width, share):
        self.at, self.ref, self.rows, self.share = at, ref, rows, share
        self.half = width // 2
        self.window = self.half - share
        self.zs, self.xs = at.slots(at.zc - 1), at.slots(at.zc)
        self.ys, self.cs = at.slots(2 * at.zc), at.slots(2 * at.zc)

    def part(self, block, start, width):
        rows = pl.ds(pl.multiple_of(block * self.rows, self.rows), self.rows)
        return self.ref.at[rows, lanes(start, width)]

    def mine(self, block):
        at = self.at
        return self.part(block, at.core * self.half + at.y * self.share, self.window)

    def single(self, block, y):
        return self.part(block, self.at.core * self.half + y * self.window, self.share)

    def send_z(self, j):
        own = self.mine(self.at.shard)
        self.at.put(own, own, self.zs + j - 1, self.at.to_z(j))

    def send_x(self, j):
        part = self.mine(self.at.block(j, 0))
        self.at.put(part, part, self.xs + j, self.at.to_x)

    def over_y(self, j, other):
        if self.share:
            part = self.single(self.at.block(j, other), self.at.y)
            self.at.put(part, part, self.ys + 2 * j + other, self.at.to_y)

    def pass_z(self, j):
        self.at.got(self.mine(self.at.block(j, 0)), self.zs + self.at.zc - j - 1)
        self.send_x(j)
        self.over_y(j, 0)

    def pass_x(self, j):
        self.at.got(self.mine(self.at.block(j, 1)), self.xs + j)
        self.over_y(j, 1)

    def pass_y(self, j, other):
        at = self.at
        block = at.block(j, other)
        if self.share:
            at.got(self.single(block, 1 - at.y), self.ys + 2 * j + other)
        part = self.part(block, at.core * self.half, self.half)
        at.put(part, part, self.cs + 2 * j + other, at.to_core)

    def finish(self):
        at = self.at
        for other in (0, 1):
            for j in range(at.zc):
                if j or other:
                    part = self.part(at.block(j, other), (1 - at.core) * self.half, self.half)
                    at.got(part, self.cs + 2 * j + other)


class Pump:
    def __init__(self, at, gathers):
        near = range(at.zc - 1, 0, -1)
        self.sends = [(one, j) for one in gathers for j in range(1, at.zc)]
        self.events, self.at, self.step, self.marks = [], at, 0, {}
        zs = [(one, j) for one in gathers for j in near]
        xs = [(one, j) for one in gathers for j in [0] + list(near)]
        ys = [(one, j, o) for one in gathers for j, o in [(0, 1)] + [(j, o) for j in near for o in (0, 1)]]
        lag_x, lag_y = LAG
        done_x = done_y = 0
        for k in range(len(zs) + lag_y + 1):
            if k < len(zs):
                self.events.append(("z",) + zs[k])
            want = len(xs) if k >= len(zs) + lag_x - 1 else max(0, (k - lag_x + 1) * at.zc // (at.zc - 1))
            while done_x < min(want, len(xs)):
                self.events.append(("x",) + xs[done_x])
                done_x += 1
            want = len(ys) if k >= len(zs) + lag_y - 1 else max(0, (k - lag_y + 1) * (2 * at.zc - 1) // (at.zc - 1))
            while done_y < min(want, len(ys)):
                self.events.append(("y",) + ys[done_y])
                done_y += 1
        self.next_send = 0
        self.last = {}
        for k, event in enumerate(self.events):
            self.last[event[1]] = k

    def issue(self, n):
        while self.next_send < min(n, len(self.sends)):
            one, j = self.sends[self.next_send]
            one.send_z(j)
            self.next_send += 1

    def begin(self, gathers):
        gathers[0].send_x(0)
        self.issue(DEPTH)
        for one in gathers[1:]:
            one.send_x(0)

    def run(self, upto=None):
        stop = len(self.events) if upto is None else self.last[upto] + 1
        while self.step < stop:
            kind, one, *where = self.events[self.step]
            if kind == "z":
                self.issue(sum(e[0] == "z" for e in self.events[: self.step]) + 1 + DEPTH)
                one.pass_z(*where)
            elif kind == "x":
                one.pass_x(*where)
            else:
                one.pass_y(*where)
            self.step += 1


class Reduce:
    def __init__(self, at, terms, rows, width, share, out, pair, acc, from_y, from_x, from_z, last, last_y):
        self.at, self.terms, self.rows, self.share, self.out = at, terms, rows, share, out
        self.pair, self.acc, self.from_y, self.from_x, self.from_z = pair, acc, from_y, from_x, from_z
        self.last, self.last_y = last, last_y
        self.half = width // 2
        self.window = self.half - share
        self.cs, self.ys, self.xs = at.slots(1), at.slots(1), at.slots(at.zc)
        self.zs, self.ls, self.es = at.slots(at.zc - 1), at.slots(1), at.slots(1)

    def of(self, block):
        return pl.ds(pl.multiple_of(block * self.rows, self.rows), self.rows)

    def start(self):
        at = self.at
        at.put(self.terms.at[:, lanes((1 - at.core) * self.half, self.half)], self.pair, self.cs, at.to_core)

    def sum_pair(self):
        at = self.at
        at.got(self.pair, self.cs)
        mine = lanes(at.core * self.half, self.half)

        def step(b, carry):
            rows = self.of(b)
            self.acc[rows, :] = (self.terms[rows, mine].astype(F32) + self.pair[rows, :].astype(F32)).astype(BF)
            return carry

        lax.fori_loop(0, at.count, step, 0)
        if self.share:
            at.put(self.acc.at[:, lanes((1 - at.y) * self.window, self.share)], self.from_y, self.ys, at.to_y)

    def send_x(self):
        at = self.at
        if self.share:
            at.got(self.from_y, self.ys)
            single = lanes(at.y * self.window, self.share)

            def step(b, carry):
                rows = self.of(b)
                self.acc[rows, single] = (
                    self.acc[rows, single].astype(F32) + self.from_y[rows, :].astype(F32)
                ).astype(BF)
                return carry

            lax.fori_loop(0, at.count, step, 0)
        window = lanes(at.y * self.share, self.window)
        for j in list(range(1, at.zc)) + [0]:
            at.put(self.acc.at[self.of(at.block(j, 1)), window], self.from_x.at[j], self.xs + j, at.to_x)

    def sum_x(self, some=None):
        at = self.at
        window = lanes(at.y * self.share, self.window)
        for j in range(1, at.zc) if some is None else some:
            at.got(self.from_x.at[j], self.xs + j)
            rows = self.of(at.block(j, 0))
            self.acc[rows, window] = (self.acc[rows, window].astype(F32) + self.from_x[j].astype(F32)).astype(BF)
            at.put(self.acc.at[rows, window], self.from_z.at[j - 1], self.zs + j - 1, at.to_z(j))

    def sum_z(self):
        at = self.at
        window = lanes(at.y * self.share, self.window)
        at.got(self.from_x.at[0], self.xs)
        total = self.acc[self.of(at.shard), window].astype(F32) + self.from_x[0].astype(F32)
        for j in range(1, at.zc):
            at.got(self.from_z.at[j - 1], self.zs + j - 1)
            total = total + self.from_z[j - 1].astype(F32)
        self.last[...] = total.astype(BF)
        at.put(self.last, self.last_y, self.ls, at.to_y)

    def sum_y(self):
        at, share, both = self.at, self.share, self.half - 2 * self.share
        at.got(self.last_y, self.ls)
        base = at.core * self.half
        if share:
            self.out[:, lanes(base + at.y * self.window, share)] = self.last[:, lanes(at.y * both, share)]
            self.out[:, lanes(base + (1 - at.y) * self.window, share)] = self.last_y[:, lanes((1 - at.y) * both, share)]
        if both:
            here, there = lanes((1 - at.y) * share, both), lanes(at.y * share, both)
            self.out[:, lanes(base + share, both)] = (
                self.last[:, here].astype(F32) + self.last_y[:, there].astype(F32)
            ).astype(BF)
        part = self.out.at[:, lanes(base, self.half)]
        at.put(part, part, self.es, at.to_core)

    def finish(self):
        at = self.at
        at.got(self.out.at[:, lanes((1 - at.core) * self.half, self.half)], self.es)


def divide(v, by, most):
    shift = 16
    factor = -(-(1 << shift) // by)
    return (v * factor) >> shift


def window_place(t):
    w, p = t >> 6, t & 63
    i = divide(p, WIN, 64)
    row = (w >> 1) * WIN + i
    col = (w & 1) * WIN + p - i * WIN
    return row, col, p < WIN * WIN


def prepare_masks(regions, padded, allowed):
    padded[...] = jnp.zeros_like(padded)
    padded[0:14, 0:14] = regions[...].astype(F32)
    region = padded[...].astype(BF)
    row, col, real = window_place(iota((TOK, 16), 0))
    pick = ((iota((TOK, 16), 1) == row) & real).astype(F32).astype(BF)
    row, col, real = window_place(iota((TOK, 128), 0))
    by_key = jnp.sum(jnp.where(iota((TOK, 128), 1) == col, dot(pick, region), 0.0), axis=1, keepdims=True)
    row, col, real = window_place(iota((TOK, 1), 0))
    by_key = jnp.where(real, by_key, -1.0)
    for w in range(4):
        row, col, real = window_place(w * PW + (iota((128, TOK), 1) & 63))
        pick = (iota((128, TOK), 0) == col).astype(F32).astype(BF)
        row, col, real = window_place(w * PW + (iota((16, TOK), 1) & 63))
        by_query = colsum(jnp.where(iota((16, TOK), 0) == row, dot(region, pick), 0.0))
        row, col, real = window_place(w * PW + (iota((1, TOK), 1) & 63))
        by_query = jnp.where(real, by_query, -2.0)
        allowed[w] = (by_key[w * PW : (w + 1) * PW] == by_query).astype(F32)


def prepare_bias(relative, square, flat, table, padded, one_hot, by_head, pos):
    square[...] = jnp.full(square.shape, -1.0, F32)
    square[0 : WIN * WIN, 0 : WIN * WIN] = relative[...].astype(F32)
    turned = square[...].T
    for j in range(PAIRS // PW):
        flat[0:1, j * PW : (j + 1) * PW] = turned[j : j + 1, 0:PW]
    one_hot[...] = (iota((256, PAIRS), 0) == flat[...].astype(jnp.int32)).astype(F32).astype(BF)
    padded[...] = jnp.zeros_like(padded)
    padded[:, 0 : table.shape[1]] = table[...]
    left = padded[...]
    total = None
    for _ in range(3):
        part = left.astype(BF)
        left = left - part.astype(F32)
        term = dot(part, one_hot[...])
        total = term if total is None else total + term
    for j in range(WIN * WIN):
        by_head[:, j, :] = total[:, j * PW : (j + 1) * PW]
    for g in range(4):
        pos[g] = jnp.concatenate([by_head[4 * g + h] for h in range(4)], axis=1)


def table_terms(gpos, one_hot, by_head):
    for g in range(4):
        for h in range(4):
            by_head[4 * g + h] = gpos[g][:, h * PW : (h + 1) * PW]
    flat = jnp.concatenate([by_head[:, j, :] for j in range(52)], axis=1)
    high = flat.astype(BF)
    low = (flat - high.astype(F32)).astype(BF)
    return dot(high, one_hot[...], NT) + dot(low, one_hot[...], NT)


def to_windows(frame, own, edge, which, out):
    for r in range(14):
        row = own[r + SHIFT] if r + SHIFT < 14 else edge[which, r + SHIFT - 14]
        frame[r, 0:14, :] = row.astype(F32)
    row, col, real = window_place(iota((TOK, 224), 0))
    col = col + SHIFT
    col = jnp.where(col >= 14, col - 14, col)
    pick = ((iota((TOK, 224), 1) == row * 16 + col) & real).astype(F32).astype(BF)
    out[...] = dot(pick, frame[...].reshape(224, frame.shape[2]).astype(BF)).astype(BF)


def from_windows(values):
    t = iota((208, TOK), 0)
    t = jnp.where(t >= 160, t - 6, t)
    row = divide(t, 14, 256)
    col = t - row * 14 + 14 - SHIFT
    col = jnp.where(col >= 14, col - 14, col)
    right = (col >= WIN).astype(jnp.int32)
    below = (row >= WIN).astype(jnp.int32)
    place = (2 * below + right) * PW + (row - below * WIN) * WIN + col - right * WIN
    pick = (iota((208, TOK), 1) == place).astype(F32).astype(BF)
    high = values.astype(BF)
    low = (values - high.astype(F32)).astype(BF)
    return dot(pick, high) + dot(pick, low)


def block_kernel(
    count, inv_root, x_hbm, d_hbm, regions, relative, table, a_hbm, e_hbm, r_hbm, vectors,
    g_att, g_exp, g_red, small_out, frames, edges_out,
    att, exp, red, t_att, t_exp, t_red,
    pair_a, pair_e, pair_r, acc_a, acc_e, acc_r, fy_e, fx_a, fx_e, fx_r, fz_a, fz_e, fz_r,
    last_a, last_e, last_r, ly_a, ly_e, ly_r,
    edges_in, edges_go, vec_own, vec_all, vec,
    small, small_pair, small_sum, small_y, small_x, small_z,
    frame, xw, dw, region_pad, allowed, square, flat, table_pad, one_hot, by_head, pos,
    h1, qkv, prob, o, r1, xhat2, h2, z, slope, deb, do, dqkv, dr1, gpos,
    x_in, d_in, w_att, w_exp, w_red, loads, send, recv,
):
    at = Place(count, send, recv)
    fetch = [
        pltpu.make_async_copy(source, place, loads.at[k])
        for k, (source, place) in enumerate(
            ((x_hbm, x_in), (d_hbm, d_in), (a_hbm, w_att), (e_hbm, w_exp), (r_hbm, w_red))
        )
    ]
    for copy in fetch:
        copy.start()
    at.greet()
    for copy in fetch:
        copy.wait()
    rows, rows_red = w_att.shape[0], w_red.shape[0]
    es = at.slots(2)
    before, after = {"band": (at.band + 3) % 4}, {"band": (at.band + 1) % 4}
    for k, source in enumerate((x_in, d_in)):
        at.put(source.at[0:SHIFT], edges_in.at[k], es + k, before)
    width = vectors.shape[1]
    vec_own[...] = jnp.zeros_like(vec_own)
    vec_own[0:12, 0:width] = vectors[...]
    vec_all[at.shard] = vec_own[...].astype(BF)
    vs = at.slots(count - 1)
    order = [(j, 0) for j in range(1, at.zc)] + [(j, 1) for j in range(at.zc)]
    for i, (j, other) in enumerate(order):
        if other:
            continue
        at.put(vec_all.at[at.shard], vec_all.at[at.shard], vs + i, at.to_z(j))
    at.put(vec_all.at[at.shard], vec_all.at[at.shard], vs + at.zc - 1, at.to_x)
    gathers = [
        Gather(at, ref, n, ref.shape[1], share)
        for ref, n, share in zip((att, exp, red), (rows, rows, rows_red), GATHER_SHARE)
    ]
    for ref, shard, n, one in zip((att, exp, red), (w_att, w_exp, w_red), (rows, rows, rows_red), gathers):
        ref[pl.ds(pl.multiple_of(at.shard * n, n), n), :] = shard[...].astype(BF)
    pump = Pump(at, gathers)
    pump.begin(gathers)
    for j in range(at.zc - 1, 0, -1):
        place = vec_all.at[at.block(j, 0)]
        at.got(place, vs + at.zc - j - 1)
        at.put(place, place, vs + at.zc - 1 + j, at.to_x)
    prepare_masks(regions, region_pad, allowed)
    prepare_bias(relative, square, flat, table, table_pad, one_hot, by_head, pos)
    gather_att, gather_exp, gather_red = gathers
    pump.run(gather_att)
    frame[...] = jnp.zeros_like(frame)
    for k, (source, windows) in enumerate(((x_in, xw), (d_in, dw))):
        at.got(edges_in.at[k], es + k)
        to_windows(frame, source, edges_in, k, windows)
    for j in range(at.zc):
        at.got(vec_all.at[at.block(j, 1)], vs + at.zc - 1 + j)
    total = None
    for b in range(count):
        place = (iota((128, 512), 1) == b * width + iota((128, 512), 0)) & (iota((128, 512), 0) < width)
        term = dot(vec_all[b], place.astype(F32).astype(BF))
        total = term if total is None else total + term
    vec[...] = total
    gather_att.finish()

    x = xw[...].astype(F32)
    xhat1, rstd1 = norm(x)
    h1[...] = (xhat1 * (1.0 + vec[0:1]) + vec[1:2]).astype(BF)
    hb = h1[...]
    qkv[:, 0:512] = ((dot(hb, att[:, 0:512]) + vec[2:3]) * (1.0 / math.sqrt(32.0))).astype(BF)
    qkv[:, 512:1024] = dot(hb, att[:, 512:1024]).astype(BF)
    qkv[:, 1024:1536] = (dot(hb, att[:, 1024:1536]) + vec[3:4]).astype(BF)
    pump.run(gather_exp)
    for w in range(4):
        for g in range(4):
            attention_forward(w, g, qkv, allowed, pos, prob, o)
    r1[...] = x + dot(o[...], att[:, 1536:2048]) + vec[4:5]
    xh2, rstd2 = norm(r1[...])
    xhat2[...] = xh2
    h2[...] = (xh2 * (1.0 + vec[5:6]) + vec[6:7]).astype(BF)
    gather_exp.finish()
    reduce_red = Reduce(
        at, t_red, rows_red, 512, REDUCE_SHARE[RED], g_red, pair_r, acc_r, None, fx_r, fz_r, last_r, ly_r
    )
    reduce_exp = Reduce(
        at, t_exp, rows, 2048, REDUCE_SHARE[EXP], g_exp, pair_e, acc_e, fy_e, fx_e, fz_e, last_e, ly_e
    )
    reduce_att = Reduce(at, t_att, rows, 2048, REDUCE_SHARE[ATT], g_att, pair_a, acc_a, None, fx_a, fz_a, last_a, ly_a)
    d = dw[...]
    for c in range(4):
        cols = slice(c * 512, c * 512 + 512)
        e = dot(h2[...], exp[:, cols]) + vec[8 + c : 9 + c]
        zz, sl = gelu_and_slope(e)
        z[:, cols] = zz.astype(BF)
        slope[:, cols] = sl
        t_red[cols, :] = (dot(zz.astype(BF), d, TN) * inv_root).astype(BF)
    reduce_red.start()
    pump.run()
    reduce_red.sum_pair()
    reduce_red.send_x()
    gather_red.finish()

    ds_ = at.slots(2)
    h2t = h2[...].T
    for c in range(4):
        cols = slice(c * 512, c * 512 + 512)
        de = dot(d, red[cols, :], NT) * slope[:, cols]
        small[8 + c : 9 + c] = colsum(de) * inv_root
        deb[:, cols] = de.astype(BF)
        t_exp[:, cols] = (dot(h2t, de.astype(BF)) * inv_root).astype(BF)
    reduce_exp.start()
    out = from_windows(r1[...] + dot(z[...], red[...]) + vec[7:8])
    frames[0] = out[0:160]
    edges_go[0] = out[160:208].astype(BF)
    at.put(edges_go.at[0], edges_out.at[0], ds_, after)
    reduce_exp.sum_pair()
    dh2 = dot(deb[...], exp[...], NT)
    df = d.astype(F32)
    small[7:8] = colsum(df) * inv_root
    small[5:6] = colsum(dh2 * xhat2[...]) * inv_root
    small[6:7] = colsum(dh2) * inv_root
    dr = df + norm_back(dh2 * (1.0 + vec[5:6]), xhat2[...], rstd2)
    dr1[...] = dr
    small[4:5] = colsum(dr) * inv_root
    drb = dr.astype(BF)
    t_att[:, 1536:2048] = (dot(o[...], drb, TN) * inv_root).astype(BF)
    do[...] = dot(drb, att[:, 1536:2048], NT).astype(BF)
    cut, later = at.zc // 2, at.zc - at.zc // 4
    first, second, third = range(1, cut), range(cut, later), range(later, at.zc)
    for g in range(4):
        sq = sv = None
        for w in range(4):
            a, b = attention_backward(w, g, qkv, do, prob, gpos, dqkv, w == 0)
            sq = a if sq is None else sq + a
            sv = b if sv is None else sv + b
        small[2:3, g * 128 : (g + 1) * 128] = sq * inv_root
        small[3:4, g * 128 : (g + 1) * 128] = sv * inv_root
        if g == 0:
            reduce_red.sum_x(first)
    reduce_red.sum_x(second)
    h1t = h1[...].T
    for c in range(3):
        cols = slice(c * 512, c * 512 + 512)
        t_att[:, cols] = (dot(h1t, dqkv[:, cols]) * inv_root).astype(BF)
    reduce_att.start()
    terms = table_terms(gpos, one_hot, by_head) * inv_root
    small[16:24, 0:256] = terms[0:8]
    small[16:24, 256:512] = terms[8:16]
    small[12:16] = jnp.zeros((4, 512), F32)
    dh1 = None
    for c in range(3):
        cols = slice(c * 512, c * 512 + 512)
        term = dot(dqkv[:, cols], att[:, cols], NT)
        dh1 = term if dh1 is None else dh1 + term
    xhat1, rstd1 = norm(xw[...].astype(F32))
    small[0:1] = colsum(dh1 * xhat1) * inv_root
    small[1:2] = colsum(dh1) * inv_root
    ss = at.slots(4 + at.zc)
    at.put(small.at[:, lanes((1 - at.core) * 256, 256)], small_pair, ss, at.to_core)
    reduce_att.sum_pair()
    reduce_att.send_x()
    reduce_red.sum_x(third)
    at.got(small_pair, ss)
    small_sum[0] = small[:, lanes(at.core * 256, 256)] + small_pair[...]
    at.put(small_sum.at[0], small_y, ss + 1, at.to_y)
    out = from_windows(dr1[...] + norm_back(dh1 * (1.0 + vec[0:1]), xhat1, rstd1))
    frames[1] = out[0:160]
    edges_go[1] = out[160:208].astype(BF)
    at.put(edges_go.at[1], edges_out.at[1], ds_ + 1, after)
    reduce_att.sum_x(first)
    at.got(small_y, ss + 1)
    small_sum[1] = small_sum[0] + small_y[...]
    at.put(small_sum.at[1], small_x, ss + 2, at.to_x)
    reduce_exp.send_x()
    reduce_att.sum_x(second)
    reduce_red.sum_z()
    reduce_att.sum_x(third)
    at.got(small_x, ss + 2)
    small_z[at.z] = small_sum[1] + small_x[...]
    for j in range(1, at.zc):
        at.put(small_z.at[at.z], small_z.at[at.z], ss + 3 + j, at.to_z(j))
    reduce_exp.sum_x(first)
    reduce_red.sum_y()
    reduce_exp.sum_x(second)
    reduce_exp.sum_x(third)
    reduce_att.sum_z()
    reduce_exp.sum_z()
    for j in range(1, at.zc):
        at.got(small_z.at[(at.z + at.zc - j) % at.zc], ss + 3 + j)
    total = small_z[0]
    for j in range(1, at.zc):
        total = total + small_z[j]
    small_out[:, lanes(at.core * 256, 256)] = total
    half = small_out.at[:, lanes(at.core * 256, 256)]
    at.put(half, half, ss + 3, at.to_core)
    reduce_att.sum_y()
    reduce_exp.sum_y()
    for k in range(2):
        at.got(edges_out.at[k], ds_ + k)
    at.got(small_out.at[:, lanes((1 - at.core) * 256, 256)], ss + 3)
    for one in (reduce_red, reduce_exp, reduce_att):
        one.finish()
    at.done()
    assert at.used <= send.shape[0]


def block_step(x, d, regions, relative, table, w_att, w_exp, w_red, vectors, inv_root):
    count = lax.axis_size("shard")
    zc = count // 2
    rows, rows_red = w_att.shape[0], w_red.shape[0]
    sh = jax.ShapeDtypeStruct
    v = pltpu.VMEM
    slots = 3 * (7 * zc) + 3 * (2 * zc + 4) + count + zc + 16
    share_a, share_e, share_r = REDUCE_SHARE
    win_a, win_e, win_r = 1024 - share_a, 1024 - share_e, 256 - share_r
    return pl.pallas_call(
        functools.partial(block_kernel, count, inv_root),
        out_shape=(
            sh((rows, 2048), BF), sh((rows, 2048), BF), sh((rows_red, 512), BF), sh((24, 512), F32),
            sh((2, 160, 512), F32), sh((2, 48, 512), BF),
        ),
        in_specs=[HBM] * 2 + [VM] * 3 + [HBM] * 3 + [VM],
        out_specs=[VM] * 6,
        scratch_shapes=[
            v((512, 2048), BF), v((512, 2048), BF), v((2048, 512), BF),
            v((512, 2048), BF), v((512, 2048), BF), v((2048, 512), BF),
            v((512, 1024), BF), v((512, 1024), BF), v((2048, 256), BF),
            v((512, 1024), BF), v((512, 1024), BF), v((2048, 256), BF),
            v((512, share_e), BF),
            v((zc, rows, win_a), BF), v((zc, rows, win_e), BF), v((zc, rows_red, win_r), BF),
            v((zc - 1, rows, win_a), BF), v((zc - 1, rows, win_e), BF), v((zc - 1, rows_red, win_r), BF),
            v((rows, win_a), BF), v((rows, win_e), BF), v((rows_red, win_r), BF),
            v((rows, win_a), BF), v((rows, win_e), BF), v((rows_red, win_r), BF),
            v((2, SHIFT, 14, 512), BF), v((2, 48, 512), BF),
            v((16, 128), F32), v((count, 16, 128), BF), v((16, 512), F32),
            v((24, 512), F32), v((24, 256), F32), v((2, 24, 256), F32), v((24, 256), F32), v((24, 256), F32),
            v((zc, 24, 256), F32),
            v((14, 16, 512), F32), v((TOK, 512), BF), v((TOK, 512), BF),
            v((16, 128), F32), v((4, PW, TOK), F32), v((128, 128), F32), v((1, PAIRS), F32), v((16, 256), F32), v((256, PAIRS), BF), v((16, PW, PW), F32),
            v((4, PW, TOK), F32),
            v((TOK, 512), BF), v((TOK, 1536), BF), v((4, 4, PW, TOK), F32), v((TOK, 512), BF), v((TOK, 512), F32),
            v((TOK, 512), F32), v((TOK, 512), BF), v((TOK, 2048), BF), v((TOK, 2048), F32), v((TOK, 2048), BF),
            v((TOK, 512), BF), v((TOK, 1536), BF), v((TOK, 512), F32), v((4, PW, TOK), F32),
            v(x.shape, BF), v(d.shape, BF), v(w_att.shape, F32), v(w_exp.shape, F32), v(w_red.shape, F32),
            pltpu.SemaphoreType.DMA((5,)), pltpu.SemaphoreType.DMA((slots,)), pltpu.SemaphoreType.DMA((slots,)),
        ],
        compiler_params=pltpu.CompilerParams(
            collective_id=0, has_side_effects=True, vmem_limit_bytes=60 * 1024 * 1024
        ),
        name="block_step",
    )(x, d, regions, relative, table, w_att, w_exp, w_red, vectors)


def adamw(weight, grad, first, second, decay):
    first_new = BETA_ONE * first + (1.0 - BETA_ONE) * grad
    second_new = BETA_TWO * second + (1.0 - BETA_TWO) * grad * grad
    corr_one = 1.0 - BETA_ONE**STEP
    corr_two = 1.0 - BETA_TWO**STEP
    step_dir = first_new / corr_one / (jnp.sqrt(second_new / corr_two) + ADAM_EPS)
    return (weight - LEARN_RATE * (step_dir + decay * weight), first_new, second_new)


def finish_kernel(steps, frames, edges, small, *refs):
    grads, state, outs = refs[:3], refs[3:18], refs[18:]
    y, dt, o_grads, o_vec, o_table, new = outs[0], outs[1], outs[2:5], outs[5], outs[6], outs[7:]
    for m in range(3):
        grad = grads[m][...].astype(F32)
        o_grads[m][...] = grad
        new[3 * m][...], new[3 * m + 1][...], new[3 * m + 2][...] = adamw(
            state[3 * m][...], grad, state[3 * m + 1][...], state[3 * m + 2][...], WEIGHT_DECAY
        )

    @pl.when(pl.program_id(0) == 0)
    def _():
        width, table = state[9].shape[1], state[12].shape[1]
        turned = pltpu.roll(small[0:16, :], (512 - lax.axis_index("shard") * width) % 512, 1)
        grad = turned[0:12, 0:width]
        o_vec[...] = grad
        new[9][...], new[10][...], new[11][...] = adamw(state[9][...], grad, state[10][...], state[11][...], 0.0)
        grad = jnp.concatenate([small[16:24, 0:256], small[16:24, 256:512]], axis=0)[:, 0:table]
        o_table[...] = grad
        new[12][...], new[13][...], new[14][...] = adamw(state[12][...], grad, state[13][...], state[14][...], 0.0)
        for k, out in enumerate((y, dt)):
            above = edges[k].astype(F32)
            for b in range(4):
                cols = slice(b * 128, b * 128 + 128)
                out[pl.ds(b, 14 * SHIFT, stride=4), :] = above[0 : 14 * SHIFT, cols]
                out[pl.ds(14 * SHIFT * 4 + b, 14 * (14 - SHIFT), stride=4), :] = frames[
                    k, 0 : 14 * (14 - SHIFT), cols
                ]


def finish(grads, small, frames, edges, state):
    steps = 2 if state[0].shape[0] % 32 == 0 else 1

    def part(a):
        return pl.BlockSpec((a.shape[0] // steps, a.shape[1]), lambda i: (i, 0))

    def whole(a):
        return pl.BlockSpec(a.shape, lambda i: (0,) * len(a.shape))

    sh = jax.ShapeDtypeStruct
    cut = [state[0], state[3], state[6]]
    outs = [sh((784, 128), F32)] * 2 + [sh(a.shape, F32) for a in cut] + [sh(state[9].shape, F32), sh(state[12].shape, F32)]
    outs += [sh(a.shape, F32) for a in state]
    specs = [whole(outs[0])] * 2 + [part(a) for a in cut] + [whole(state[9]), whole(state[12])]
    state_specs = [part(a) for a in state[:9]] + [whole(a) for a in state[9:]]
    return pl.pallas_call(
        functools.partial(finish_kernel, steps),
        grid=(steps,),
        out_shape=outs,
        in_specs=[whole(frames), whole(edges), whole(small)] + [part(a) for a in grads] + state_specs,
        out_specs=specs + state_specs,
        compiler_params=pltpu.CompilerParams(vmem_limit_bytes=60 * 1024 * 1024),
        name="finish",
    )(frames, edges, small, *grads, *state)


def on_device(
    block_input, output_grad, region_ids, relative_index, attention_weight, expand_weight, reduce_weight, vectors,
    bias_table, attention_mean, attention_square, expand_mean, expand_square, reduce_mean, reduce_square,
    vectors_mean, vectors_square, table_mean, table_square,
):
    images, band_rows, columns, features = block_input.shape
    tokens = images * lax.axis_size("shard") * band_rows * lax.axis_size("band") * columns
    grads = block_step(
        block_input[0], output_grad[0], region_ids, relative_index, bias_table.T,
        attention_weight, expand_weight, reduce_weight, vectors, 1.0 / math.sqrt(tokens),
    )
    state = (
        attention_weight, attention_mean, attention_square, expand_weight, expand_mean, expand_square,
        reduce_weight, reduce_mean, reduce_square, vectors, vectors_mean, vectors_square,
        bias_table.T, table_mean.T, table_square.T,
    )
    outs = finish(grads[:3], grads[3], grads[4], grads[5], state)
    y, dt, grad_a, grad_e, grad_r, grad_v, grad_t = outs[:7]
    new = outs[7:]
    shape = block_input.shape
    return (
        y.reshape(shape), dt.reshape(shape), grad_a, grad_e, grad_r, grad_v, grad_t.T,
        new[0], new[3], new[6], new[9], new[12].T,
        new[1], new[2], new[4], new[5], new[7], new[8], new[10], new[11], new[13].T, new[14].T,
    )


def solution(mesh):
    return jax.shard_map(
        on_device,
        mesh=mesh,
        in_specs=(
            P("shard", "band", None, None),
            P("shard", "band", None, None),
            P("band", None),
            P(),
            P("shard", None),
            P("shard", None),
            P("shard", None),
            P(None, "shard"),
            P(),
            P("shard", None),
            P("shard", None),
            P("shard", None),
            P("shard", None),
            P("shard", None),
            P("shard", None),
            P(None, "shard"),
            P(None, "shard"),
            P(),
            P(),
        ),
        out_specs=(
            P("shard", "band", None, None),
            P("shard", "band", None, None),
            P("shard", None),
            P("shard", None),
            P("shard", None),
            P(None, "shard"),
            P(),
            P("shard", None),
            P("shard", None),
            P("shard", None),
            P(None, "shard"),
            P(),
            P("shard", None),
            P("shard", None),
            P("shard", None),
            P("shard", None),
            P("shard", None),
            P("shard", None),
            P(None, "shard"),
            P(None, "shard"),
            P(),
            P(),
        ),
        check_vma=False,
    )
```
